32 devices in a mesh: seq: 8 (over y, x, core), tensor: 4 (over z).
Axes of the slice: x: 2, y: 2, z: 4, core: 2. Of those that a mesh axis runs over, the one named last changes fastest.
Arguments:
- queries: bfloat16 [8192, 8, 128], P('seq', 'tensor'), may hold values from -16 to 16
- keys: bfloat16 [8192, 128], P('seq'), may hold values from -6 to 6
- values: bfloat16 [8192, 128], P('seq'), may hold values from -6 to 6
- doc_ids: int32 [8192], P('seq'), may hold values from 0 to 7, never falling along the last dimension, each value on 1 to 4096 neighbouring positions
- w_query: bfloat16 [8, 128, 64], P('tensor'), may hold values from -0.5 to 0.5
- w_key: bfloat16 [128, 64], replicated, may hold values from -0.5 to 0.5
Outputs:
- student: bfloat16 [8192, 8, 128], P('seq', 'tensor')
- grad_wq: float32 [8, 128, 64], P('tensor')
- grad_key_weight: float32 [128, 64], replicated
- key_feature_grads: float32 [8192, 128], P('seq', 'tensor')
The draws below stay inside these ranges and needn't reach their ends.
Inputs may be any that keep to these rules, and one draw needn't show every extreme that they name: `doc_ids`: document numbers never fall along the sequence and each number is used; each document has 1 to 4096 positions, and one has exactly 4096.
All inputs are finite; a program needn't handle non-finite values.
Results may differ from the reference program's by a relative error of at most 0.017.
Values may be sent and summed in bfloat16 or wider, within the bound.
No kernel may reach another device: no remote copies, remote signals or barrier semaphores. Data moves between devices by JAX's collectives and lax.ppermute only.
A program may use at most 64 MiB of HBM per device.

```python
import math
import jax
import jax.numpy as jnp
import numpy as np
from jax import lax

HEAD_SIZE = 128
HEADS = 8
FEAT = 128
REACH = 4
TOK_DEV = 1024
HALF = 64
SEQ = 8192
MOST = 4096
N_SEQ = 8


def paired_draw(key):
    folded = jax.random.fold_in(key, 4099)
    first_key, second_key = jax.random.split(folded, 2)
    key_draw = jnp.clip(jax.random.normal(first_key, (SEQ, HEAD_SIZE), jnp.float32), -6.0, 6.0)
    query_draw = jnp.clip(jax.random.normal(second_key, (SEQ, HEADS, HEAD_SIZE), jnp.float32), -6.0, 6.0)
    return (query_draw, key_draw)


def draw_queries(key, part):
    return paired_draw(key)[0].astype(jnp.bfloat16)


def draw_keys(key, part):
    return paired_draw(key)[1].astype(jnp.bfloat16)


def shard_levels(rng, dims, shards, low, high):
    def one(axis_at, blocks):
        heights = jax.random.uniform(jax.random.fold_in(jax.random.fold_in(rng, 6), axis_at), (blocks,), jnp.float32, low / len(shards), high / len(shards))
        return jnp.repeat(jnp.exp(heights), dims[axis_at] // blocks).reshape((-1,) + (1,) * (len(dims) - axis_at - 1))

    loudness = one(*shards[0])
    for cut in shards[1:]:
        loudness = loudness * one(*cut)
    return loudness


def profile(count, total, most, skew):
    portions = [(1 << 20) // math.isqrt(grade ** skew) + 1 for grade in range(2, count + 1)]
    spare, holding = total - most - (count - 1), [1] * (count - 1)
    while spare > 0:
        candidates = [i for i in range(count - 1) if holding[i] < most]
        whole, remaining = sum([portions[i] for i in candidates]), spare
        for i in candidates:
            addition = min(most - holding[i], max(1, remaining * portions[i] // whole), spare)
            holding[i] = holding[i] + addition
            spare = spare - addition
    return np.array([most] + holding)


def uneven_parts(rng, count, total, bound, slope):
    if count == 2:
        one = jax.random.randint(rng, (), max(1, total - bound), min(bound, total - 1) + 1)
        return jnp.stack([one, total - one])
    sizes = jnp.asarray(profile(count, total, bound, slope), jnp.int32)
    twos = (count - 1) // 2
    source_of, taker = sizes[1:1 + 2 * twos:2], sizes[2:2 + 2 * twos:2]
    slack = jnp.minimum(source_of - 1, bound - taker)
    moved = jax.random.randint(jax.random.fold_in(rng, 1), (twos,), 0, 1 << 20) % (slack + 1)
    sizes = sizes.at[1:1 + 2 * twos:2].set(source_of - moved).at[2:2 + 2 * twos:2].set(taker + moved)
    return sizes[jax.random.permutation(jax.random.fold_in(rng, 2), count)]


def bell_draw(own_key, extent, spread, reach, cuts=(), held_as=jnp.bfloat16):
    array = jax.random.normal(own_key, extent, jnp.float32) * spread
    if len(cuts) > 0:
        array = shard_levels(own_key, extent, cuts, -0.22, 0.18) * array
    return jnp.clip(array, min=-reach, max=reach).astype(held_as)


def setup_inputs(seed: int = 0) -> dict:
    arg_keys = jax.random.split(jax.random.key(seed), 7)
    queries = draw_queries(jax.random.fold_in(arg_keys[6], 71), 0)
    keys = draw_keys(jax.random.fold_in(arg_keys[6], 71), 0)
    values = bell_draw(arg_keys[2], (SEQ, HEAD_SIZE), 1.0, 6.0, ((0, 8),))
    doc_ids = jnp.searchsorted(jnp.cumsum(uneven_parts(arg_keys[3], N_SEQ, SEQ, MOST, 2)), jnp.arange(SEQ), side="right").astype(jnp.int32)
    w_query = bell_draw(arg_keys[4], (HEADS, HEAD_SIZE, HALF), HEAD_SIZE ** -0.5, 0.5, ((0, 4),))
    w_key = bell_draw(arg_keys[5], (HEAD_SIZE, HALF), HEAD_SIZE ** -0.5, 0.5)
    return dict(queries=queries, keys=keys, values=values, doc_ids=doc_ids, w_query=w_query, w_key=w_key)


NEGATIVE = -1e30
exact_setting = lax.Precision.HIGHEST


def feature(logits):
    return jnp.concatenate([jax.nn.softmax(logits, axis=-1), jax.nn.softmax(-logits, axis=-1)], axis=-1)


def feature_back(features, incoming_grad):
    middle = features.shape[-1] // 2
    upper_half = features[..., :middle]
    lower_half = features[..., middle:]
    grad_upper = incoming_grad[..., :middle]
    grad_lower = incoming_grad[..., middle:]
    upper_term = upper_half * (grad_upper - jnp.sum(grad_upper * upper_half, axis=-1, keepdims=True))
    lower_term = lower_half * (grad_lower - jnp.sum(grad_lower * lower_half, axis=-1, keepdims=True))
    return upper_term - lower_term


def join_states(earlier, later):
    earlier_state, earlier_sum, earlier_code = earlier
    later_state, later_sum, later_code = later
    vacant = later_code == 0.0
    matching = (later_code == earlier_code).astype(jnp.float32)
    joined_state = jnp.where(vacant, earlier_state, later_state + matching * earlier_state)
    joined_sum = jnp.where(vacant, earlier_sum, later_sum + matching * earlier_sum)
    return joined_state, joined_sum, jnp.where(vacant, earlier_code, later_code)


def to_bfloat(array_in):
    return lax.optimization_barrier(array_in.astype(jnp.bfloat16)).astype(jnp.float32)


def chain_step(carry, element):
    return join_states(carry, element), carry


def reference(queries, keys, values, doc_ids, w_query, w_key):
    count_of_rows = TOK_DEV
    pad_rows = REACH * count_of_rows
    score_scale = HEAD_SIZE ** -0.5
    doc_codes = (doc_ids + 1).astype(jnp.int32)
    key_features = feature(jnp.dot(keys, w_key, preferred_element_type=jnp.float32))
    key_feat_b = to_bfloat(key_features)
    keys_wide = jnp.concatenate([jnp.zeros((pad_rows, HEAD_SIZE), jnp.float32), keys.astype(jnp.float32)], axis=0)
    values_wide = jnp.concatenate([jnp.zeros((pad_rows, HEAD_SIZE), jnp.float32), values.astype(jnp.float32)], axis=0)
    codes_wide = jnp.concatenate([jnp.zeros((pad_rows,), jnp.int32), doc_codes], axis=0)
    key_blocks = key_feat_b.reshape(N_SEQ, count_of_rows, FEAT)
    blocked_values = values.astype(jnp.float32).reshape(N_SEQ, count_of_rows, HEAD_SIZE)
    code_blocks = doc_codes.reshape(N_SEQ, count_of_rows)
    query_blocks = queries.astype(jnp.float32).reshape(N_SEQ, count_of_rows, HEADS, HEAD_SIZE)
    w_query_f = w_query.astype(jnp.float32)

    def local_state(feature_rows, value_rows, code_rows):
        chosen = (code_rows == code_rows[-1]).astype(jnp.float32)[:, None] * feature_rows
        return (jnp.einsum('kf,kd->fd', chosen, value_rows, precision=exact_setting), jnp.sum(chosen, axis=0), code_rows[-1].astype(jnp.float32))

    identity = (jnp.zeros((FEAT, HEAD_SIZE), jnp.float32), jnp.zeros((FEAT,), jnp.float32), jnp.zeros((), jnp.float32))
    local_states = jax.vmap(local_state)(key_blocks, blocked_values, code_blocks)
    _, incoming = lax.scan(chain_step, identity, local_states)
    query_pos = jnp.arange(count_of_rows, dtype=jnp.int32)
    key_pos = jnp.arange(pad_rows + count_of_rows, dtype=jnp.int32) - pad_rows

    def block_terms(inputs):
        block_index, query_rows, carried_state, carried_sum, carried_code = inputs
        first_row = (block_index * count_of_rows).astype(jnp.int32)
        code_rows = lax.dynamic_slice_in_dim(doc_codes, first_row, count_of_rows)
        window_keys = lax.dynamic_slice_in_dim(keys_wide, first_row, pad_rows + count_of_rows)
        window_values = lax.dynamic_slice_in_dim(values_wide, first_row, pad_rows + count_of_rows)
        window_codes = lax.dynamic_slice_in_dim(codes_wide, first_row, pad_rows + count_of_rows)
        scores = jnp.einsum('qhd,kd->qhk', query_rows, window_keys, precision=exact_setting) * score_scale
        allowed = (code_rows[:, None] == window_codes[None, :]) & (key_pos[None, :] <= query_pos[:, None])
        row_top = jnp.max(jnp.where(allowed[:, None, :], scores, NEGATIVE), axis=-1, keepdims=True)
        weights = jnp.where(allowed[:, None, :], jnp.exp(scores - row_top), 0.0)
        teacher = jnp.einsum('qhk,kd->qhd', to_bfloat(weights), window_values, precision=exact_setting) / jnp.sum(weights, axis=-1)[..., None]
        feature_rows = lax.dynamic_index_in_dim(key_blocks, block_index, 0, keepdims=False)
        value_rows = lax.dynamic_index_in_dim(blocked_values, block_index, 0, keepdims=False)
        query_features = feature(jnp.einsum('qhd,hdf->qhf', query_rows, w_query_f, precision=exact_setting))
        query_feat_b = to_bfloat(query_features)
        local_mask = (code_rows[:, None] == code_rows[None, :]) & (query_pos[None, :] <= query_pos[:, None])
        products = jnp.where(local_mask[:, None, :], jnp.einsum('qhf,kf->qhk', query_feat_b, feature_rows, precision=exact_setting), 0.0)
        receive = (code_rows.astype(jnp.float32) == carried_code).astype(jnp.float32)
        numerator = jnp.einsum('qhk,kd->qhd', to_bfloat(products), value_rows, precision=exact_setting) + receive[:, None, None] * jnp.einsum('qhf,fd->qhd', query_feat_b, carried_state, precision=exact_setting)
        denominator = jnp.sum(products, axis=-1) + receive[:, None] * jnp.einsum('qhf,f->qh', query_feat_b, carried_sum, precision=exact_setting)
        estimate = numerator / denominator[..., None]
        grad_out = (2.0 / SEQ) * (estimate - teacher)
        grad_num = grad_out / denominator[..., None]
        grad_den = -jnp.sum(grad_out * estimate, axis=-1) / denominator
        grad_prod = to_bfloat(jnp.where(local_mask[:, None, :], jnp.einsum('qhd,kd->qhk', to_bfloat(grad_num), value_rows, precision=exact_setting) + grad_den[..., None], 0.0))
        grad_qf = jnp.einsum('qhk,kf->qhf', grad_prod, feature_rows, precision=exact_setting) + receive[:, None, None] * (jnp.einsum('qhd,fd->qhf', grad_num, carried_state, precision=exact_setting) + grad_den[..., None] * carried_sum)
        grad_kf_local = jnp.einsum('qhk,qhf->kf', grad_prod, query_feat_b, precision=exact_setting)
        leading = (code_rows == code_rows[0]).astype(jnp.float32)[:, None, None] * query_feat_b
        adjoint_state = jnp.einsum('qhf,qhd->fd', leading, grad_num, precision=exact_setting)
        adjoint_sum = jnp.einsum('qhf,qh->f', leading, grad_den, precision=exact_setting)
        grad_aq = to_bfloat(feature_back(query_features, grad_qf))
        grad_wq_block = jnp.einsum('qhd,qhf->hdf', query_rows, grad_aq, precision=exact_setting)
        return estimate.astype(jnp.bfloat16), grad_kf_local, adjoint_state, adjoint_sum, code_rows[0].astype(jnp.float32), grad_wq_block

    block_ids = jnp.arange(N_SEQ, dtype=jnp.int32)
    students, grad_kf_local, adjoint_states, adjoint_sums, leading_codes, grad_wq_blocks = lax.map(block_terms, (block_ids, query_blocks, incoming[0], incoming[1], incoming[2]))
    _, adjoint_entering = lax.scan(chain_step, identity, (adjoint_states, adjoint_sums, leading_codes), reverse=True)
    receive_back = (code_blocks.astype(jnp.float32) == adjoint_entering[2][:, None]).astype(jnp.float32)
    additional_terms = jnp.einsum('woa,wxa->wox', blocked_values, adjoint_entering[0], precision=exact_setting) + adjoint_entering[1][:, None, :]
    grad_kf = grad_kf_local + receive_back[:, :, None] * additional_terms
    grad_attention_key = to_bfloat(feature_back(key_features.reshape(N_SEQ, count_of_rows, FEAT), grad_kf))
    grad_key_weight = jnp.einsum('srg,srv->gv', keys.astype(jnp.float32).reshape(N_SEQ, count_of_rows, HEAD_SIZE), grad_attention_key, precision=exact_setting)
    grad_wq = jnp.sum(grad_wq_blocks, axis=0)
    key_feature_grads = grad_kf.reshape(SEQ, FEAT) * float(SEQ)
    return students.reshape(SEQ, HEADS, HEAD_SIZE), grad_wq, grad_key_weight, key_feature_grads
```

```python
import functools

import jax
import jax.numpy as jnp
from jax import lax
from jax.experimental import pallas as pl
from jax.experimental.pallas import tpu as pltpu
from jax.sharding import PartitionSpec as P

REACH = 4
NEG = -1e30
LOG2E = 1.4426950408889634
TQ = 256
TK = 512
BF = jnp.bfloat16
F32 = jnp.float32

NT = (((1,), (1,)), ((), ()))
NN = (((1,), (0,)), ((), ()))


def mm(a, b, dims=NN):
    return lax.dot_general(a, b, dims, preferred_element_type=F32)


def feature_t(logits):
    top = jnp.max(logits, axis=0, keepdims=True)
    low = jnp.min(logits, axis=0, keepdims=True)
    up = jnp.exp(logits - top)
    down = jnp.exp(low - logits)
    up = up * (1.0 / jnp.sum(up, axis=0, keepdims=True))
    down = down * (1.0 / jnp.sum(down, axis=0, keepdims=True))
    return jnp.concatenate([up, down], axis=0)


def feature_back_t(feat, grad):
    half = feat.shape[0] // 2
    p, m = feat[:half], feat[half:]
    a, b = grad[:half], grad[half:]
    return p * (a - jnp.sum(a * p, axis=0, keepdims=True)) - m * (
        b - jnp.sum(b * m, axis=0, keepdims=True)
    )


def allowed_t(limit, first, start):
    j = lax.broadcasted_iota(jnp.int32, (limit, TQ), 0)
    i = lax.broadcasted_iota(jnp.int32, (1, TQ), 1) + first
    return (j <= i) & (j >= start)


def transposed(x):
    return x.astype(F32).T


def local_kernel(
    scale, q_ref, k_ref, v_ref, start_ref, wq_ref, wk_ref,
    qf_ref, kf_ref, vt_ref, acc_ref, num_ref, stat_ref, kfb_ref,
):
    n, width = k_ref.shape
    heads = q_ref.shape[1] // width
    kf = feature_t(mm(wk_ref[...], k_ref[...], NT))
    kf_ref[...] = kf
    kfb_ref[...] = kf.T.astype(BF)
    vt_ref[...] = transposed(v_ref[...]).astype(BF)

    def head(h, carry):
        lane = pl.multiple_of(h * width, width)
        for qt in range(n // TQ):
            first = qt * TQ
            limit = first + TQ
            col = pl.ds(pl.multiple_of(h * n + first, TQ), TQ)
            q = q_ref[first:limit, pl.ds(lane, width)]
            ok = allowed_t(limit, first, start_ref[:, first:limit])
            s = jnp.where(ok, mm(k_ref[:limit], q, NT), NEG)
            top = jnp.max(s, axis=0, keepdims=True)
            w = jnp.exp2((s - top) * (scale * LOG2E))
            stat_ref[0:1, col] = top
            stat_ref[1:2, col] = jnp.sum(w, axis=0, keepdims=True)
            acc_ref[:, col] = mm(vt_ref[:, :limit], w.astype(BF))
            qf = feature_t(mm(wq_ref[h], q, NT))
            qf_ref[:, col] = qf
            pr = jnp.where(ok, mm(kfb_ref[:limit], qf.astype(BF)), 0.0)
            stat_ref[2:3, col] = jnp.sum(pr, axis=0, keepdims=True)
            num_ref[:, col] = mm(vt_ref[:, :limit], pr.astype(BF))
        return carry

    lax.fori_loop(0, heads, head, 0)


def main_kernel(
    scale, grad_scale,
    doc_ref, q_ref, k_ref, v_ref, start_ref, wk_ref,
    qf_ref, kf_ref, vt_ref, acc_in, num_ref, stat_ref,
    two_ref, four_ref, own_ref, swap_two_ref, swap_four_ref,
    stu_ref, gkf_ref, out_ref,
    wink, winv, wcode, wkf, wvt, gwq_ref, gwk_ref, adj_ref, adjs_ref,
    state_ref, statet_ref, csum_ref, acc_ref, st2_ref, sem,
):
    n, width = k_ref.shape
    heads = q_ref.shape[1] // width
    half = wk_ref.shape[0]
    total = REACH * n
    odd = lax.rem(lax.axis_index("seq"), 2)

    def copies(src, slot):
        return (
            pltpu.make_async_copy(src.at[0:n], wink.at[pl.ds(slot * n, n)], sem.at[slot, 0]),
            pltpu.make_async_copy(src.at[n : 2 * n], winv.at[pl.ds(slot * n, n)], sem.at[slot, 1]),
            pltpu.make_async_copy(src.at[2 * n : 2 * n + 16], wcode.at[slot], sem.at[slot, 2]),
        )

    def begin(src, slot):
        for c in copies(src, slot):
            c.start()

    begin(four_ref, 0)
    begin(two_ref, 2)

    @pl.when(odd == 0)
    def _():
        begin(swap_four_ref, 1)
        begin(swap_two_ref, 3)

    @pl.when(odd == 1)
    def _():
        begin(swap_two_ref, 1)
        begin(own_ref, 3)

    gkf_ref[...] = jnp.zeros_like(gkf_ref)
    gwq_ref[...] = jnp.zeros_like(gwq_ref)
    gwk_ref[...] = jnp.zeros_like(gwk_ref)
    adj_ref[...] = jnp.zeros_like(adj_ref)
    adjs_ref[...] = jnp.zeros_like(adjs_ref)
    state_ref[...] = jnp.zeros_like(state_ref)
    statet_ref[...] = jnp.zeros_like(statet_ref)
    csum_ref[...] = jnp.zeros_like(csum_ref)
    acc_ref[...] = acc_in[...]
    st2_ref[...] = stat_ref[...]
    lead_code = (doc_ref[0] + 1).astype(F32)
    lead_rows = jnp.sum((start_ref[...] == 0).astype(jnp.int32))
    for slot in range(REACH):
        for c in copies(two_ref, slot):
            c.wait()
    length = jnp.sum((wcode[...].astype(F32) == lead_code).astype(jnp.int32))
    begin_key = total - length
    tile0 = begin_key // TK
    tiles = total // TK
    linked = length > 0

    @pl.when(linked)
    def _():
        def prepare(kt, carry):
            row = pl.ds(pl.multiple_of(kt * TK, TK), TK)
            kf = feature_t(mm(wk_ref[...], wink[row], NT))
            wkf[:, row] = kf
            j = lax.broadcasted_iota(jnp.int32, (1, TK), 1) + kt * TK
            kfm = jnp.where(j >= begin_key, kf, 0.0).astype(BF)
            vt = transposed(winv[row]).astype(BF)
            wvt[:, row] = vt
            statet_ref[...] += mm(vt, kfm, NT)
            part = kfm.astype(F32)
            for c in range(TK // 128):
                csum_ref[...] += part[:, c * 128 : (c + 1) * 128]
            return carry

        lax.fori_loop(tile0, tiles, prepare, 0)
        state_ref[...] = statet_ref[...].T
        csum_ref[...] = jnp.broadcast_to(
            jnp.sum(csum_ref[...], axis=1, keepdims=True), csum_ref.shape
        )

        def head(h, carry):
            lane = pl.multiple_of(h * width, width)

            def qtile(qt, carry):
                first = pl.multiple_of(qt * TQ, TQ)
                col = pl.ds(pl.multiple_of(h * n + first, TQ), TQ)
                q = q_ref[pl.ds(first, TQ), pl.ds(lane, width)]

                def update(state, kt, masked):
                    top, wsum, acc = state
                    row = pl.ds(pl.multiple_of(kt * TK, TK), TK)
                    s = mm(wink[row], q, NT)
                    if masked:
                        j = lax.broadcasted_iota(jnp.int32, (TK, 1), 0) + kt * TK
                        s = jnp.where(j >= begin_key, s, NEG)
                    new = jnp.maximum(top, jnp.max(s, axis=0, keepdims=True))
                    w = jnp.exp2((s - new) * (scale * LOG2E))
                    f = jnp.exp2((top - new) * (scale * LOG2E))
                    return (
                        new,
                        wsum * f + jnp.sum(w, axis=0, keepdims=True),
                        acc * f + mm(wvt[:, row], w.astype(BF)),
                    )

                old = (st2_ref[0:1, col], st2_ref[1:2, col], acc_ref[:, col])
                new = update(old, tile0, True)
                new = lax.fori_loop(tile0 + 1, tiles, lambda kt, s: update(s, kt, False), new)
                i = lax.broadcasted_iota(jnp.int32, (1, TQ), 1) + first
                live = i < lead_rows
                st2_ref[1:2, col] = jnp.where(live, new[1], old[1])
                acc_ref[:, col] = jnp.where(live, new[2], old[2])
                return carry

            return lax.fori_loop(0, (lead_rows + TQ - 1) // TQ, qtile, carry)

        lax.fori_loop(0, heads, head, 0)

    state_b = state_ref[...].astype(BF)
    statet_b = statet_ref[...].astype(BF)
    kft_b = kf_ref[...].astype(BF)
    link = linked.astype(F32)

    def head(h, carry):
        lane = pl.multiple_of(h * width, width)
        csum = jnp.concatenate([csum_ref[...]] * (TQ // 128), axis=1)
        for qt in range(n // TQ):
            first = qt * TQ
            limit = first + TQ
            col = pl.ds(pl.multiple_of(h * n + first, TQ), TQ)
            q = q_ref[first:limit, pl.ds(lane, width)]
            start = start_ref[:, first:limit]
            lead = (start == 0).astype(F32)
            r = lead * link
            qf = qf_ref[:, col]
            qf_b = qf.astype(BF)
            qf_f = qf_b.astype(F32)
            teacher = acc_ref[:, col] * (1.0 / st2_ref[1:2, col])
            num = num_ref[:, col] + r * mm(statet_b, qf_b)
            den = st2_ref[2:3, col] + r * jnp.sum(qf_f * csum, axis=0, keepdims=True)
            inv = 1.0 / den
            est = num * inv
            stu_ref[first:limit, pl.ds(lane, width)] = est.T.astype(BF)
            g = grad_scale * (est - teacher)
            gd = -jnp.sum(g * est, axis=0, keepdims=True) * inv
            gn_b = (g * inv).astype(BF)
            ok = allowed_t(limit, first, start)
            gp = jnp.where(ok, mm(v_ref[:limit], gn_b) + gd, 0.0).astype(BF)
            gq = mm(kft_b[:, :limit], gp) + r * (mm(state_b, gn_b) + csum * gd)
            gkf_ref[:, :limit] += mm(qf_b, gp, NT)
            adj_ref[...] += mm((qf_f * lead).astype(BF), gn_b, NT)
            weighted = qf_f * (lead * gd)
            for c in range(TQ // 128):
                adjs_ref[...] += weighted[:, c * 128 : (c + 1) * 128]
            ga = feature_back_t(qf, gq).astype(BF)
            gwq_ref[h] += mm(ga, q)
        return carry

    lax.fori_loop(0, heads, head, 0)

    gl = feature_back_t(kf_ref[...], gkf_ref[...]).astype(BF)
    gwk_ref[...] += mm(gl, k_ref[...])
    adj_b = adj_ref[...].astype(BF)
    adjs_col = jnp.sum(adjs_ref[...], axis=1, keepdims=True)

    @pl.when(linked)
    def _():
        def back(kt, carry):
            row = pl.ds(pl.multiple_of(kt * TK, TK), TK)
            more = mm(adj_b, winv[row], NT) + adjs_col
            j = lax.broadcasted_iota(jnp.int32, (1, TK), 1) + kt * TK
            gl = feature_back_t(wkf[:, row], more)
            gl = jnp.where(j >= begin_key, gl, 0.0).astype(BF)
            gwk_ref[...] += mm(gl, wink[row])
            return carry

        lax.fori_loop(tile0, tiles, back, 0)

    for h in range(heads):
        out_ref[h * half : (h + 1) * half] = gwq_ref[h].astype(BF)
    at = heads * half
    gwk = gwk_ref[...]
    hi = gwk.astype(BF)
    out_ref[at : at + half] = hi
    out_ref[at + half : at + 2 * half] = (gwk - hi.astype(F32)).astype(BF)
    at += 2 * half
    out_ref[at : at + width] = adj_b
    at += width
    row = jnp.sum(adjs_ref[...].T, axis=0, keepdims=True)
    row_hi = row.astype(BF).astype(F32)
    index = lax.broadcasted_iota(jnp.int32, (16, width), 0)
    tail = jnp.where(index == 0, row_hi, jnp.where(index == 1, row - row_hi, lead_code))
    out_ref[at : at + 16] = tail.astype(BF)


def join_kernel(
    seq, tensor, heads, back_scale,
    doc_ref, edge_ref, gath_ref, gkf_ref, v_ref,
    gwq_ref, *rest,
):
    outs, (tot_ref, adj_ref, adjs_ref, gwk_ref) = rest[:tensor], rest[tensor:]
    n, width = v_ref.shape
    half = width // 2
    me = lax.axis_index("seq")
    mine = lax.axis_index("tensor")
    last_code = (doc_ref[n - 1] + 1).astype(F32)
    edge = edge_ref[n - 1]
    at = heads * half
    for h in range(heads):
        s = gath_ref[0, h * half : (h + 1) * half].astype(F32)
        for d in range(1, seq):
            s = s + gath_ref[d, h * half : (h + 1) * half].astype(F32)
        gwq_ref[h] = s.T
    w = gath_ref[0, at : at + 2 * half].astype(F32)
    for d in range(1, seq):
        w = w + gath_ref[d, at : at + 2 * half].astype(F32)
    w = w[:half] + w[half:]
    w_hi = w.astype(BF).astype(F32)
    gwk_ref[...] = jnp.concatenate([w_hi, w - w_hi], axis=0).astype(BF)
    at += 2 * half
    adj_ref[...] = jnp.zeros_like(adj_ref)
    adjs_ref[...] = jnp.zeros_like(adjs_ref)

    def later(s, carry):
        a = gath_ref[s, at : at + width].astype(F32)
        t = gath_ref[s, at + width : at + width + 16].astype(F32)
        same = t[2:3] == last_code
        adj_ref[...] += jnp.where(same, a, 0.0)
        adjs_ref[...] += jnp.where(same, t[0:1] + t[1:2], 0.0)
        return carry

    lax.fori_loop(me + 1, jnp.minimum(me + REACH + 1, seq), later, 0)
    adj = adj_ref[...]
    a_hi = adj.astype(BF)
    a_lo = (adj - a_hi.astype(F32)).astype(BF)
    col = jnp.broadcast_to(adjs_ref[...], (width, width)).T[:, 0:1]
    j = lax.broadcasted_iota(jnp.int32, (1, n), 1)
    more = mm(a_hi, v_ref[...], NT) + mm(a_lo, v_ref[...], NT) + col
    tot_ref[...] = (gkf_ref[...] + jnp.where(j >= edge, more, 0.0)) * back_scale
    rows = width // tensor
    for k in range(tensor):
        piece = lax.rem(mine + k, tensor)
        outs[k][0:rows] = tot_ref[pl.ds(pl.multiple_of(piece * rows, rows), rows)].astype(BF)
        for c in range(n // width):
            outs[k][rows:, c * width : (c + 1) * width] = gwk_ref[c * 16 : (c + 1) * 16]


def last_kernel(tensor, *refs):
    ins, (kfg_ref, gwk_ref) = refs[:tensor], refs[tensor:]
    total = ins[0][...].astype(F32)
    for k in range(1, tensor):
        total = total + ins[k][...].astype(F32)
    rows = kfg_ref.shape[1]
    width = gwk_ref.shape[0]
    kfg_ref[...] = total[:rows].T
    w = total[rows:]
    w = jnp.concatenate(
        [w[:, c * width : (c + 1) * width] for c in range(w.shape[1] // width)], axis=0
    )
    half = w.shape[0] // 2
    gwk_ref[...] = (w[:half] + w[half:]).T


VM = pl.BlockSpec(memory_space=pltpu.VMEM)
SM = pl.BlockSpec(memory_space=pltpu.SMEM)
ANY = pl.BlockSpec(memory_space=pl.ANY)


def cost(flops, size):
    return pl.CostEstimate(flops=flops, bytes_accessed=size, transcendentals=0)


def shards(queries, keys, values, doc_ids, w_query, w_key):
    n, heads, width = queries.shape
    half = w_key.shape[1]
    seq = lax.axis_size("seq")
    tensor = lax.axis_size("tensor")
    scale = width ** (-0.5)
    everyone = range(seq)
    assert n // width <= 16 and n // width * 16 == width

    codes = (doc_ids + 1).astype(BF).reshape(n // width, width)
    codes = jnp.pad(codes, ((0, 16 - n // width), (0, 0)))
    pack = jnp.concatenate([keys, values, codes], axis=0)

    def hop(x, distance):
        return lax.ppermute(x, "seq", [(i, i + distance) for i in everyone if i + distance < seq])

    own = lax.ppermute(pack, "seq", [(i, i + 1) for i in everyone if i % 2 == 0])
    four = hop(pack, 4)
    two = hop(pack, 2)

    qs = queries.reshape(n, heads * width)
    starts = jnp.sum((doc_ids[None, :] < doc_ids[:, None]).astype(jnp.int32), axis=1)
    start_row = starts.reshape(1, n)
    wq_t = jnp.transpose(w_query, (0, 2, 1))
    wk_t = w_key.T
    sds = jax.ShapeDtypeStruct
    cols = heads * n
    qf, kf, vt, acc, num, stat = pl.pallas_call(
        functools.partial(local_kernel, scale),
        out_shape=(
            sds((width, cols), F32), sds((width, n), F32), sds((width, n), BF),
            sds((width, cols), F32), sds((width, cols), F32), sds((8, cols), F32),
        ),
        in_specs=[VM] * 6,
        out_specs=[VM] * 6,
        scratch_shapes=[pltpu.VMEM((n, width), BF)],
        cost_estimate=cost(8 * n * n * width * heads, 8 << 20),
    )(qs, keys, values, start_row, wq_t, wk_t)

    swap_two = lax.ppermute(two, "seq", [(i, i ^ 1) for i in everyone])
    swap_four = lax.ppermute(four, "seq", [(i, i - 1) for i in everyone if i % 2 == 1])

    packed = heads * half + 2 * half + width + 16
    total = REACH * n
    student, gkf, out = pl.pallas_call(
        functools.partial(main_kernel, scale, 2.0 / (n * seq)),
        out_shape=(sds((n, heads * width), BF), sds((width, n), F32), sds((packed, width), BF)),
        in_specs=[SM] + [VM] * 11 + [ANY] * 5,
        out_specs=[VM] * 3,
        scratch_shapes=[
            pltpu.VMEM((total, width), BF),
            pltpu.VMEM((total, width), BF),
            pltpu.VMEM((REACH, 16, width), BF),
            pltpu.VMEM((width, total), F32),
            pltpu.VMEM((width, total), BF),
            pltpu.VMEM((heads, half, width), F32),
            pltpu.VMEM((half, width), F32),
            pltpu.VMEM((width, width), F32),
            pltpu.VMEM((width, 128), F32),
            pltpu.VMEM((width, width), F32),
            pltpu.VMEM((width, width), F32),
            pltpu.VMEM((width, 128), F32),
            pltpu.VMEM((width, cols), F32),
            pltpu.VMEM((8, cols), F32),
            pltpu.SemaphoreType.DMA((REACH, 3)),
        ],
        cost_estimate=cost(16 * n * n * width * heads, 8 << 20),
    )(
        doc_ids, qs, keys, values, start_row, wk_t, qf, kf, vt, acc, num, stat,
        two, four, own, swap_two, swap_four,
    )

    gathered = lax.all_gather(out, "seq")
    rows = width // tensor
    gwq, *pieces = pl.pallas_call(
        functools.partial(join_kernel, seq, tensor, heads, float(n * seq)),
        out_shape=[sds((heads, width, half), F32)] + [sds((rows + 16, n), BF)] * tensor,
        in_specs=[SM, SM, VM, VM, VM],
        out_specs=[VM] * (tensor + 1),
        scratch_shapes=[
            pltpu.VMEM((width, n), F32),
            pltpu.VMEM((width, width), F32),
            pltpu.VMEM((1, width), F32),
            pltpu.VMEM((width, width), BF),
        ],
        cost_estimate=cost(4 * n * width * width, 2 << 20),
    )(doc_ids, starts, gathered, gkf, values)

    arrived = [pieces[0]]
    for k in range(1, tensor):
        arrived.append(
            lax.ppermute(pieces[k], "tensor", [(i, (i + k) % tensor) for i in range(tensor)])
        )
    key_grads, gwk = pl.pallas_call(
        functools.partial(last_kernel, tensor),
        out_shape=(sds((n, rows), F32), sds((width, half), F32)),
        in_specs=[VM] * tensor,
        out_specs=[VM] * 2,
        cost_estimate=cost(n * width, 1 << 20),
    )(*arrived)
    return student.reshape(n, heads, width), gwq, gwk, key_grads


def solution(mesh):
    placed = (
        P("seq", "tensor", None),
        P("seq", None),
        P("seq", None),
        P("seq"),
        P("tensor", None, None),
        P(),
    )
    return jax.shard_map(
        shards,
        mesh=mesh,
        in_specs=placed,
        out_specs=(P("seq", "tensor", None), P("tensor", None, None), P(), P("seq", "tensor")),
        check_vma=False,
    )
```

```python
import functools

import jax
import jax.numpy as jnp
from jax import lax
from jax.experimental import pallas as pl
from jax.experimental.pallas import tpu as pltpu
from jax.sharding import PartitionSpec as P

REACH = 4
NEG = -1e30
LOG2E = 1.4426950408889634
TQ = 256
TK = 1024
TC = 256
CH = 256
BF = jnp.bfloat16
F32 = jnp.float32

NT = (((1,), (1,)), ((), ()))
NN = (((1,), (0,)), ((), ()))


def mm(a, b, dims=NN):
    return lax.dot_general(a, b, dims, preferred_element_type=F32)


def feature_t(logits):
    top = jnp.max(logits, axis=0, keepdims=True)
    low = jnp.min(logits, axis=0, keepdims=True)
    up = jnp.exp(logits - top)
    down = jnp.exp(low - logits)
    up = up * (1.0 / jnp.sum(up, axis=0, keepdims=True))
    down = down * (1.0 / jnp.sum(down, axis=0, keepdims=True))
    return jnp.concatenate([up, down], axis=0)


def feature_back_t(feat, grad):
    half = feat.shape[0] // 2
    p, m = feat[:half], feat[half:]
    a, b = grad[:half], grad[half:]
    return p * (a - jnp.sum(a * p, axis=0, keepdims=True)) - m * (
        b - jnp.sum(b * m, axis=0, keepdims=True)
    )


def allowed_t(limit, first, start):
    j = lax.broadcasted_iota(jnp.int32, (limit, TQ), 0)
    i = lax.broadcasted_iota(jnp.int32, (1, TQ), 1) + first
    return (j <= i) & (j >= start)


def transposed(x):
    return x.astype(F32).T


def local_kernel(
    scale, q_ref, k_ref, v_ref, start_ref, wq_ref, wk_ref,
    qf_ref, kf_ref, vt_ref, acc_ref, num_ref, stat_ref, kfb_ref,
):
    n, width = k_ref.shape
    heads = q_ref.shape[1] // width
    kf = feature_t(mm(wk_ref[...], k_ref[...], NT))
    kf_ref[...] = kf
    kfb_ref[...] = kf.T.astype(BF)
    vt_ref[...] = transposed(v_ref[...]).astype(BF)

    def head(h, carry):
        lane = pl.multiple_of(h * width, width)
        for qt in range(n // TQ):
            first = qt * TQ
            limit = first + TQ
            col = pl.ds(pl.multiple_of(h * n + first, TQ), TQ)
            q = q_ref[first:limit, pl.ds(lane, width)]
            ok = allowed_t(limit, first, start_ref[:, first:limit])
            s = jnp.where(ok, mm(k_ref[:limit], q, NT), NEG)
            top = jnp.max(s, axis=0, keepdims=True)
            w = jnp.exp2((s - top) * (scale * LOG2E))
            stat_ref[0:1, col] = top
            stat_ref[1:2, col] = jnp.sum(w, axis=0, keepdims=True)
            acc_ref[:, col] = mm(vt_ref[:, :limit], w.astype(BF))
            qf = feature_t(mm(wq_ref[h], q, NT))
            qf_ref[:, col] = qf
            pr = jnp.where(ok, mm(kfb_ref[:limit], qf.astype(BF)), 0.0)
            stat_ref[2:3, col] = jnp.sum(pr, axis=0, keepdims=True)
            num_ref[:, col] = mm(vt_ref[:, :limit], pr.astype(BF))
        return carry

    lax.fori_loop(0, heads, head, 0)


def main_kernel(
    scale, grad_scale,
    doc_ref, q_ref, k_ref, v_ref, start_ref, wk_ref,
    qf_ref, kf_ref, vt_ref, acc_in, num_ref, stat_ref,
    two_ref, four_ref, own_ref, swap_two_ref, swap_four_ref,
    stu_ref, gkf_ref, out_ref,
    wink, winv, wcode, wkf, wvt, gwq_ref, gwk_ref, adj_ref, adjs_ref,
    state_ref, statet_ref, csum_ref, acc_ref, st2_ref, run_ref, racc_ref, sbuf_ref, smax_ref, sem,
):
    n, width = k_ref.shape
    heads = q_ref.shape[1] // width
    half = wk_ref.shape[0]
    total = REACH * n
    odd = lax.rem(lax.axis_index("seq"), 2)

    def copies(src, slot):
        return (
            pltpu.make_async_copy(src.at[0:n], wink.at[pl.ds(slot * n, n)], sem.at[slot, 0]),
            pltpu.make_async_copy(src.at[n : 2 * n], winv.at[pl.ds(slot * n, n)], sem.at[slot, 1]),
            pltpu.make_async_copy(src.at[2 * n : 2 * n + 16], wcode.at[slot], sem.at[slot, 2]),
        )

    def begin(src, slot):
        for c in copies(src, slot):
            c.start()

    begin(four_ref, 0)
    begin(two_ref, 2)

    @pl.when(odd == 0)
    def _():
        begin(swap_four_ref, 1)
        begin(swap_two_ref, 3)

    @pl.when(odd == 1)
    def _():
        begin(swap_two_ref, 1)
        begin(own_ref, 3)

    gkf_ref[...] = jnp.zeros_like(gkf_ref)
    gwq_ref[...] = jnp.zeros_like(gwq_ref)
    gwk_ref[...] = jnp.zeros_like(gwk_ref)
    adj_ref[...] = jnp.zeros_like(adj_ref)
    adjs_ref[...] = jnp.zeros_like(adjs_ref)
    state_ref[...] = jnp.zeros_like(state_ref)
    statet_ref[...] = jnp.zeros_like(statet_ref)
    csum_ref[...] = jnp.zeros_like(csum_ref)
    acc_ref[...] = acc_in[...]
    st2_ref[...] = stat_ref[...]
    lead_code = (doc_ref[0] + 1).astype(F32)
    lead_rows = jnp.sum((start_ref[...] == 0).astype(jnp.int32))
    for slot in range(REACH):
        for c in copies(two_ref, slot):
            c.wait()
    length = jnp.sum((wcode[...].astype(F32) == lead_code).astype(jnp.int32))
    begin_key = total - length
    tile0 = begin_key // TK
    tiles = total // TK
    linked = length > 0

    @pl.when(linked)
    def _():
        def prepare(kt, carry):
            row = pl.ds(pl.multiple_of(kt * TK, TK), TK)
            kf = feature_t(mm(wk_ref[...], wink[row], NT))
            wkf[:, row] = kf
            j = lax.broadcasted_iota(jnp.int32, (1, TK), 1) + kt * TK
            kfm = jnp.where(j >= begin_key, kf, 0.0).astype(BF)
            vt = transposed(winv[row]).astype(BF)
            wvt[:, row] = vt
            statet_ref[...] += mm(vt, kfm, NT)
            part = kfm.astype(F32)
            for c in range(TK // 128):
                csum_ref[...] += part[:, c * 128 : (c + 1) * 128]
            return carry

        lax.fori_loop(tile0, tiles, prepare, 0)
        state_ref[...] = statet_ref[...].T
        csum_ref[...] = jnp.broadcast_to(
            jnp.sum(csum_ref[...], axis=1, keepdims=True), csum_ref.shape
        )

        wq = max(TC, 2 * TC // heads)
        chains = [(h, c) for h in range(heads) for c in range(wq // TC)]
        factor = scale * LOG2E

        def qtile(qt, carry):
            first = pl.multiple_of(qt * wq, wq)

            def column(h, c):
                return pl.ds(pl.multiple_of(h * n + first + c * TC, TC), TC)

            for x, (h, c) in enumerate(chains):
                col = column(h, c)
                run_ref[x, 0:1] = st2_ref[0:1, col]
                run_ref[x, 1:2] = st2_ref[1:2, col]
                racc_ref[x] = acc_ref[:, col]

            def scores(x, kt, part, masked):
                h, c = chains[x]
                q = q_ref[pl.ds(first + c * TC, TC), h * width : (h + 1) * width]
                row = pl.multiple_of(kt * TK + part * CH, CH)
                s = mm(wink[pl.ds(row, CH)], q, NT)
                if masked:
                    j = lax.broadcasted_iota(jnp.int32, (CH, 1), 0) + row
                    s = jnp.where(j >= begin_key, s, NEG)
                sbuf_ref[x, part * CH : (part + 1) * CH] = s
                return jnp.max(s.reshape(CH // 8, 8, TC), axis=0)

            def stage(cur, kt, nxt, kt_nxt, masked):
                old = run_ref[cur, 0:1]
                new = jnp.maximum(old, jnp.max(smax_ref[cur], axis=0, keepdims=True))
                tops, sums, parts = [], [], []
                for part in range(TK // CH):
                    tops.append(scores(nxt, kt_nxt, part, masked))
                    w = jnp.exp2((sbuf_ref[cur, part * CH : (part + 1) * CH] - new) * factor)
                    sums.append(jnp.sum(w.reshape(CH // 8, 8, TC), axis=0))
                    parts.append(w.astype(BF))
                smax_ref[nxt] = functools.reduce(jnp.maximum, tops)
                f = jnp.exp2((old - new) * factor)
                total_w = jnp.sum(functools.reduce(jnp.add, sums), axis=0, keepdims=True)
                run_ref[cur, 0:1] = new
                run_ref[cur, 1:2] = run_ref[cur, 1:2] * f + total_w
                row = pl.ds(pl.multiple_of(kt * TK, TK), TK)
                racc_ref[cur] = racc_ref[cur] * f + mm(
                    wvt[:, row], jnp.concatenate(parts, axis=0)
                )

            def sweep(kt, masked):
                for x in range(len(chains) - 1):
                    stage(x, kt, x + 1, kt, masked)
                stage(len(chains) - 1, kt, 0, jnp.minimum(kt + 1, tiles - 1), False)

            smax_ref[0] = functools.reduce(
                jnp.maximum, [scores(0, tile0, part, True) for part in range(TK // CH)]
            )
            sweep(tile0, True)

            def step(kt, carry):
                sweep(kt, False)
                return carry

            lax.fori_loop(tile0 + 1, tiles, step, 0)
            i = lax.broadcasted_iota(jnp.int32, (1, wq), 1) + first
            live = i < lead_rows
            for x, (h, c) in enumerate(chains):
                col = column(h, c)
                ok = live[:, c * TC : (c + 1) * TC]
                st2_ref[1:2, col] = jnp.where(ok, run_ref[x, 1:2], st2_ref[1:2, col])
                acc_ref[:, col] = jnp.where(ok, racc_ref[x], acc_ref[:, col])
            return carry

        lax.fori_loop(0, (lead_rows + wq - 1) // wq, qtile, 0)

    state_b = state_ref[...].astype(BF)
    statet_b = statet_ref[...].astype(BF)
    kft_b = kf_ref[...].astype(BF)
    link = linked.astype(F32)

    def head(h, carry):
        lane = pl.multiple_of(h * width, width)
        csum = jnp.concatenate([csum_ref[...]] * (TQ // 128), axis=1)
        for qt in range(n // TQ):
            first = qt * TQ
            limit = first + TQ
            col = pl.ds(pl.multiple_of(h * n + first, TQ), TQ)
            q = q_ref[first:limit, pl.ds(lane, width)]
            start = start_ref[:, first:limit]
            lead = (start == 0).astype(F32)
            r = lead * link
            qf = qf_ref[:, col]
            qf_b = qf.astype(BF)
            qf_f = qf_b.astype(F32)
            teacher = acc_ref[:, col] * (1.0 / st2_ref[1:2, col])
            num = num_ref[:, col] + r * mm(statet_b, qf_b)
            den = st2_ref[2:3, col] + r * jnp.sum(qf_f * csum, axis=0, keepdims=True)
            inv = 1.0 / den
            est = num * inv
            stu_ref[first:limit, pl.ds(lane, width)] = est.T.astype(BF)
            g = grad_scale * (est - teacher)
            gd = -jnp.sum(g * est, axis=0, keepdims=True) * inv
            gn_b = (g * inv).astype(BF)
            ok = allowed_t(limit, first, start)
            gp = jnp.where(ok, mm(v_ref[:limit], gn_b) + gd, 0.0).astype(BF)
            gq = mm(kft_b[:, :limit], gp) + r * (mm(state_b, gn_b) + csum * gd)
            gkf_ref[:, :limit] += mm(qf_b, gp, NT)
            adj_ref[...] += mm((qf_f * lead).astype(BF), gn_b, NT)
            weighted = qf_f * (lead * gd)
            for c in range(TQ // 128):
                adjs_ref[...] += weighted[:, c * 128 : (c + 1) * 128]
            ga = feature_back_t(qf, gq).astype(BF)
            gwq_ref[h] += mm(ga, q)
        return carry

    lax.fori_loop(0, heads, head, 0)

    gl = feature_back_t(kf_ref[...], gkf_ref[...]).astype(BF)
    gwk_ref[...] += mm(gl, k_ref[...])
    adj_b = adj_ref[...].astype(BF)
    adjs_col = jnp.sum(adjs_ref[...], axis=1, keepdims=True)

    @pl.when(linked)
    def _():
        def back(kt, carry):
            row = pl.ds(pl.multiple_of(kt * TK, TK), TK)
            more = mm(adj_b, winv[row], NT) + adjs_col
            j = lax.broadcasted_iota(jnp.int32, (1, TK), 1) + kt * TK
            gl = feature_back_t(wkf[:, row], more)
            gl = jnp.where(j >= begin_key, gl, 0.0).astype(BF)
            gwk_ref[...] += mm(gl, wink[row])
            return carry

        lax.fori_loop(tile0, tiles, back, 0)

    for h in range(heads):
        out_ref[h * half : (h + 1) * half] = gwq_ref[h].astype(BF)
    at = heads * half
    gwk = gwk_ref[...]
    hi = gwk.astype(BF)
    out_ref[at : at + half] = hi
    out_ref[at + half : at + 2 * half] = (gwk - hi.astype(F32)).astype(BF)
    at += 2 * half
    out_ref[at : at + width] = adj_b
    at += width
    row = jnp.sum(adjs_ref[...].T, axis=0, keepdims=True)
    row_hi = row.astype(BF).astype(F32)
    index = lax.broadcasted_iota(jnp.int32, (16, width), 0)
    tail = jnp.where(index == 0, row_hi, jnp.where(index == 1, row - row_hi, lead_code))
    out_ref[at : at + 16] = tail.astype(BF)


def join_kernel(
    seq, tensor, heads, back_scale,
    doc_ref, edge_ref, gath_ref, gkf_ref, v_ref,
    gwq_ref, *rest,
):
    outs, (tot_ref, adj_ref, adjs_ref, gwk_ref) = rest[:tensor], rest[tensor:]
    n, width = v_ref.shape
    half = width // 2
    me = lax.axis_index("seq")
    mine = lax.axis_index("tensor")
    last_code = (doc_ref[n - 1] + 1).astype(F32)
    edge = edge_ref[n - 1]
    at = heads * half
    for h in range(heads):
        s = gath_ref[0, h * half : (h + 1) * half].astype(F32)
        for d in range(1, seq):
            s = s + gath_ref[d, h * half : (h + 1) * half].astype(F32)
        gwq_ref[h] = s
    w = gath_ref[0, at : at + 2 * half].astype(F32)
    for d in range(1, seq):
        w = w + gath_ref[d, at : at + 2 * half].astype(F32)
    w = w[:half] + w[half:]
    w_hi = w.astype(BF).astype(F32)
    gwk_ref[...] = jnp.concatenate([w_hi, w - w_hi], axis=0).astype(BF)
    at += 2 * half
    adj_ref[...] = jnp.zeros_like(adj_ref)
    adjs_ref[...] = jnp.zeros_like(adjs_ref)

    def later(s, carry):
        a = gath_ref[s, at : at + width].astype(F32)
        t = gath_ref[s, at + width : at + width + 16].astype(F32)
        same = t[2:3] == last_code
        adj_ref[...] += jnp.where(same, a, 0.0)
        adjs_ref[...] += jnp.where(same, t[0:1] + t[1:2], 0.0)
        return carry

    lax.fori_loop(me + 1, jnp.minimum(me + REACH + 1, seq), later, 0)
    adj = adj_ref[...]
    a_hi = adj.astype(BF)
    a_lo = (adj - a_hi.astype(F32)).astype(BF)
    col = jnp.broadcast_to(adjs_ref[...], (width, width)).T[:, 0:1]
    j = lax.broadcasted_iota(jnp.int32, (1, n), 1)
    more = mm(a_hi, v_ref[...], NT) + mm(a_lo, v_ref[...], NT) + col
    tot_ref[...] = (gkf_ref[...] + jnp.where(j >= edge, more, 0.0)) * back_scale
    rows = width // tensor
    for k in range(tensor):
        piece = lax.rem(mine + k, tensor)
        outs[k][0:rows] = tot_ref[pl.ds(pl.multiple_of(piece * rows, rows), rows)].astype(BF)
        for c in range(n // width):
            outs[k][rows:, c * width : (c + 1) * width] = gwk_ref[c * 16 : (c + 1) * 16]


def last_kernel(tensor, *refs):
    ins, (kfg_ref, gwk_ref) = refs[:tensor], refs[tensor:]
    total = ins[0][...].astype(F32)
    for k in range(1, tensor):
        total = total + ins[k][...].astype(F32)
    rows = kfg_ref.shape[0]
    width = gwk_ref.shape[1]
    kfg_ref[...] = total[:rows]
    w = total[rows:]
    w = jnp.concatenate(
        [w[:, c * width : (c + 1) * width] for c in range(w.shape[1] // width)], axis=0
    )
    half = w.shape[0] // 2
    gwk_ref[...] = w[:half] + w[half:]


VM = pl.BlockSpec(memory_space=pltpu.VMEM)
SM = pl.BlockSpec(memory_space=pltpu.SMEM)
ANY = pl.BlockSpec(memory_space=pl.ANY)


def grant(mib):
    return pltpu.CompilerParams(vmem_limit_bytes=mib << 20)


def cost(flops, size):
    return pl.CostEstimate(flops=flops, bytes_accessed=size, transcendentals=0)


def shards(queries, keys, values, doc_ids, w_query, w_key):
    n, heads, width = queries.shape
    half = w_key.shape[1]
    seq = lax.axis_size("seq")
    tensor = lax.axis_size("tensor")
    scale = width ** (-0.5)
    everyone = range(seq)
    assert n // width <= 16 and n // width * 16 == width

    codes = (doc_ids + 1).astype(BF).reshape(n // width, width)
    codes = jnp.pad(codes, ((0, 16 - n // width), (0, 0)))
    pack = jnp.concatenate([keys, values, codes], axis=0)

    def hop(x, distance):
        return lax.ppermute(x, "seq", [(i, i + distance) for i in everyone if i + distance < seq])

    own = lax.ppermute(pack, "seq", [(i, i + 1) for i in everyone if i % 2 == 0])
    four = hop(pack, 4)
    two = hop(pack, 2)

    qs = queries.reshape(n, heads * width)
    starts = jnp.sum((doc_ids[None, :] < doc_ids[:, None]).astype(jnp.int32), axis=1)
    start_row = starts.reshape(1, n)
    wq_t = jnp.transpose(w_query, (0, 2, 1))
    wk_t = w_key.T
    sds = jax.ShapeDtypeStruct
    cols = heads * n
    qf, kf, vt, acc, num, stat = pl.pallas_call(
        functools.partial(local_kernel, scale),
        out_shape=(
            sds((width, cols), F32), sds((width, n), F32), sds((width, n), BF),
            sds((width, cols), F32), sds((width, cols), F32), sds((8, cols), F32),
        ),
        in_specs=[VM] * 6,
        out_specs=[VM] * 6,
        scratch_shapes=[pltpu.VMEM((n, width), BF)],
        compiler_params=grant(16),
        cost_estimate=cost(8 * n * n * width * heads, 8 << 20),
    )(qs, keys, values, start_row, wq_t, wk_t)

    two, four, qf = lax.optimization_barrier((two, four, qf))
    swap_two = lax.ppermute(two, "seq", [(i, i ^ 1) for i in everyone])
    swap_four = lax.ppermute(four, "seq", [(i, i - 1) for i in everyone if i % 2 == 1])

    packed = heads * half + 2 * half + width + 16
    total = REACH * n
    student, gkf, out = pl.pallas_call(
        functools.partial(main_kernel, scale, 2.0 / (n * seq)),
        out_shape=(sds((n, heads * width), BF), sds((width, n), F32), sds((packed, width), BF)),
        in_specs=[SM] + [VM] * 11 + [ANY] * 5,
        out_specs=[VM] * 3,
        scratch_shapes=[
            pltpu.VMEM((total, width), BF),
            pltpu.VMEM((total, width), BF),
            pltpu.VMEM((REACH, 16, width), BF),
            pltpu.VMEM((width, total), F32),
            pltpu.VMEM((width, total), BF),
            pltpu.VMEM((heads, half, width), F32),
            pltpu.VMEM((half, width), F32),
            pltpu.VMEM((width, width), F32),
            pltpu.VMEM((width, 128), F32),
            pltpu.VMEM((width, width), F32),
            pltpu.VMEM((width, width), F32),
            pltpu.VMEM((width, 128), F32),
            pltpu.VMEM((width, cols), F32),
            pltpu.VMEM((8, cols), F32),
            pltpu.VMEM((max(heads, 2), 8, TC), F32),
            pltpu.VMEM((max(heads, 2), width, TC), F32),
            pltpu.VMEM((max(heads, 2), TK, TC), F32),
            pltpu.VMEM((max(heads, 2), 8, TC), F32),
            pltpu.SemaphoreType.DMA((REACH, 3)),
        ],
        compiler_params=grant(30),
        cost_estimate=cost(16 * n * n * width * heads, 8 << 20),
    )(
        doc_ids, qs, keys, values, start_row, wk_t, qf, kf, vt, acc, num, stat,
        two, four, own, swap_two, swap_four,
    )

    gathered = lax.all_gather(out, "seq")
    rows = width // tensor
    gwq, *pieces = pl.pallas_call(
        functools.partial(join_kernel, seq, tensor, heads, float(n * seq)),
        out_shape=[sds((heads, half, width), F32)] + [sds((rows + 16, n), BF)] * tensor,
        in_specs=[SM, SM, VM, VM, VM],
        out_specs=[VM] * (tensor + 1),
        scratch_shapes=[
            pltpu.VMEM((width, n), F32),
            pltpu.VMEM((width, width), F32),
            pltpu.VMEM((1, width), F32),
            pltpu.VMEM((width, width), BF),
        ],
        compiler_params=grant(12),
        cost_estimate=cost(4 * n * width * width, 2 << 20),
    )(doc_ids, starts, gathered, gkf, values)

    arrived = [pieces[0]]
    for k in range(1, tensor):
        arrived.append(
            lax.ppermute(pieces[k], "tensor", [(i, (i + k) % tensor) for i in range(tensor)])
        )
    key_grads, gwk = pl.pallas_call(
        functools.partial(last_kernel, tensor),
        out_shape=(sds((rows, n), F32), sds((half, width), F32)),
        in_specs=[VM] * tensor,
        out_specs=[VM] * 2,
        compiler_params=grant(8),
        cost_estimate=cost(n * width, 1 << 20),
    )(*arrived)
    return student.reshape(n, heads, width), jnp.transpose(gwq, (0, 2, 1)), gwk.T, key_grads.T


def solution(mesh):
    placed = (
        P("seq", "tensor", None),
        P("seq", None),
        P("seq", None),
        P("seq"),
        P("tensor", None, None),
        P(),
    )
    return jax.shard_map(
        shards,
        mesh=mesh,
        in_specs=placed,
        out_specs=(P("seq", "tensor", None), P("tensor", None, None), P(), P("seq", "tensor")),
        check_vma=False,
    )
```

```python
import functools

import jax
import jax.numpy as jnp
from jax import lax
from jax.experimental import pallas as pl
from jax.experimental.pallas import tpu as pltpu
from jax.sharding import PartitionSpec as P

REACH = 4
NEG = -1e30
LOG2E = 1.4426950408889634
TQ = 256
TK = 1024
TC = 256
CH = 256
BF = jnp.bfloat16
F32 = jnp.float32

NT = (((1,), (1,)), ((), ()))
NN = (((1,), (0,)), ((), ()))


def mm(a, b, dims=NN):
    return lax.dot_general(a, b, dims, preferred_element_type=F32)


def feature_t(logits):
    top = jnp.max(logits, axis=0, keepdims=True)
    low = jnp.min(logits, axis=0, keepdims=True)
    up = jnp.exp(logits - top)
    down = jnp.exp(low - logits)
    up = up * (1.0 / jnp.sum(up, axis=0, keepdims=True))
    down = down * (1.0 / jnp.sum(down, axis=0, keepdims=True))
    return jnp.concatenate([up, down], axis=0)


def feature_back_t(feat, grad):
    half = feat.shape[0] // 2
    p, m = feat[:half], feat[half:]
    a, b = grad[:half], grad[half:]
    return p * (a - jnp.sum(a * p, axis=0, keepdims=True)) - m * (
        b - jnp.sum(b * m, axis=0, keepdims=True)
    )


def allowed_t(limit, first, start):
    j = lax.broadcasted_iota(jnp.int32, (limit, TQ), 0)
    i = lax.broadcasted_iota(jnp.int32, (1, TQ), 1) + first
    return (j <= i) & (j >= start)


def transposed(x):
    return x.astype(F32).T


def local_kernel(
    scale, q_ref, k_ref, v_ref, start_ref, wq_ref, wk_ref,
    qf_ref, kf_ref, vt_ref, acc_ref, num_ref, stat_ref, kfb_ref,
):
    n, width = k_ref.shape
    heads = q_ref.shape[1] // width
    kf = feature_t(mm(wk_ref[...], k_ref[...], NT))
    kf_ref[...] = kf
    kfb_ref[...] = kf.T.astype(BF)
    vt_ref[...] = transposed(v_ref[...]).astype(BF)

    def head(h, carry):
        lane = pl.multiple_of(h * width, width)
        for qt in range(n // TQ):
            first = qt * TQ
            limit = first + TQ
            col = pl.ds(pl.multiple_of(h * n + first, TQ), TQ)
            q = q_ref[first:limit, pl.ds(lane, width)]
            ok = allowed_t(limit, first, start_ref[:, first:limit])
            s = jnp.where(ok, mm(k_ref[:limit], q, NT), NEG)
            top = jnp.max(s, axis=0, keepdims=True)
            w = jnp.exp2((s - top) * (scale * LOG2E))
            stat_ref[0:1, col] = top
            stat_ref[1:2, col] = jnp.sum(w, axis=0, keepdims=True)
            acc_ref[:, col] = mm(vt_ref[:, :limit], w.astype(BF))
            qf = feature_t(mm(wq_ref[h], q, NT))
            qf_ref[:, col] = qf
            pr = jnp.where(ok, mm(kfb_ref[:limit], qf.astype(BF)), 0.0)
            stat_ref[2:3, col] = jnp.sum(pr, axis=0, keepdims=True)
            num_ref[:, col] = mm(vt_ref[:, :limit], pr.astype(BF))
        return carry

    lax.fori_loop(0, heads, head, 0)


def main_kernel(
    scale, grad_scale, back_scale, tensor_size,
    doc_ref, q_ref, k_ref, v_ref, start_ref, wk_ref,
    qf_ref, kf_ref, vt_ref, acc_in, num_ref, stat_ref,
    two_ref, four_ref, own_ref, swap_two_ref, swap_four_ref,
    stu_ref, wq_ref, *rest,
):
    outs = rest[:tensor_size]
    (
        wink, winv, wcode, wkf, wvt, gwq_ref, gwk_ref, adj_ref, adjs_ref, gkf_ref, gkf2_ref,
        state_ref, statet_ref, csum_ref, acc_ref, st2_ref, run_ref, racc_ref, sbuf_ref, smax_ref, sem,
    ) = rest[tensor_size:]
    n, width = k_ref.shape
    heads = q_ref.shape[1] // width
    half = wk_ref.shape[0]
    total = REACH * n
    odd = lax.rem(lax.axis_index("seq"), 2)

    def copies(src, slot):
        return (
            pltpu.make_async_copy(src.at[0:n], wink.at[pl.ds(slot * n, n)], sem.at[slot, 0]),
            pltpu.make_async_copy(src.at[n : 2 * n], winv.at[pl.ds(slot * n, n)], sem.at[slot, 1]),
            pltpu.make_async_copy(src.at[2 * n : 2 * n + 16], wcode.at[slot], sem.at[slot, 2]),
        )

    def begin(src, slot):
        for c in copies(src, slot):
            c.start()

    begin(four_ref, 0)
    begin(two_ref, 2)

    @pl.when(odd == 0)
    def _():
        begin(swap_four_ref, 1)
        begin(swap_two_ref, 3)

    @pl.when(odd == 1)
    def _():
        begin(swap_two_ref, 1)
        begin(own_ref, 3)

    gkf2_ref[...] = jnp.zeros_like(gkf2_ref)
    gwq_ref[...] = jnp.zeros_like(gwq_ref)
    gwk_ref[...] = jnp.zeros_like(gwk_ref)
    adj_ref[...] = jnp.zeros_like(adj_ref)
    state_ref[...] = jnp.zeros_like(state_ref)
    statet_ref[...] = jnp.zeros_like(statet_ref)
    csum_ref[...] = jnp.zeros_like(csum_ref)
    acc_ref[...] = acc_in[...]
    st2_ref[...] = stat_ref[...]
    lead_code = (doc_ref[0] + 1).astype(F32)
    lead_rows = jnp.sum((start_ref[...] == 0).astype(jnp.int32))
    for slot in range(REACH):
        for c in copies(two_ref, slot):
            c.wait()
    length = jnp.sum((wcode[...].astype(F32) == lead_code).astype(jnp.int32))
    begin_key = total - length
    tile0 = begin_key // TK
    tiles = total // TK
    linked = length > 0

    @pl.when(linked)
    def _():
        def prepare(kt, carry):
            row = pl.ds(pl.multiple_of(kt * TK, TK), TK)
            kf = feature_t(mm(wk_ref[...], wink[row], NT))
            wkf[:, row] = kf
            j = lax.broadcasted_iota(jnp.int32, (1, TK), 1) + kt * TK
            kfm = jnp.where(j >= begin_key, kf, 0.0).astype(BF)
            vt = transposed(winv[row]).astype(BF)
            wvt[:, row] = vt
            statet_ref[...] += mm(vt, kfm, NT)
            part = kfm.astype(F32)
            for c in range(TK // 128):
                csum_ref[...] += part[:, c * 128 : (c + 1) * 128]
            return carry

        lax.fori_loop(tile0, tiles, prepare, 0)
        state_ref[...] = statet_ref[...].T
        csum_ref[...] = jnp.broadcast_to(
            jnp.sum(csum_ref[...], axis=1, keepdims=True), csum_ref.shape
        )

        wq = max(TC, 2 * TC // heads)
        chains = [(h, c) for h in range(heads) for c in range(wq // TC)]
        factor = scale * LOG2E

        def qtile(qt, carry):
            first = pl.multiple_of(qt * wq, wq)

            def column(h, c):
                return pl.ds(pl.multiple_of(h * n + first + c * TC, TC), TC)

            for x, (h, c) in enumerate(chains):
                col = column(h, c)
                run_ref[x, 0:1] = st2_ref[0:1, col]
                run_ref[x, 1:2] = st2_ref[1:2, col]
                racc_ref[x] = acc_ref[:, col]

            def scores(x, kt, part, masked):
                h, c = chains[x]
                q = q_ref[pl.ds(first + c * TC, TC), h * width : (h + 1) * width]
                row = pl.multiple_of(kt * TK + part * CH, CH)
                s = mm(wink[pl.ds(row, CH)], q, NT)
                if masked:
                    j = lax.broadcasted_iota(jnp.int32, (CH, 1), 0) + row
                    s = jnp.where(j >= begin_key, s, NEG)
                sbuf_ref[x, part * CH : (part + 1) * CH] = s
                return jnp.max(s.reshape(CH // 8, 8, TC), axis=0)

            def stage(cur, kt, nxt, kt_nxt, masked):
                old = run_ref[cur, 0:1]
                new = jnp.maximum(old, jnp.max(smax_ref[cur], axis=0, keepdims=True))
                tops, sums, parts = [], [], []
                for part in range(TK // CH):
                    tops.append(scores(nxt, kt_nxt, part, masked))
                    w = jnp.exp2((sbuf_ref[cur, part * CH : (part + 1) * CH] - new) * factor)
                    sums.append(jnp.sum(w.reshape(CH // 8, 8, TC), axis=0))
                    parts.append(w.astype(BF))
                smax_ref[nxt] = functools.reduce(jnp.maximum, tops)
                f = jnp.exp2((old - new) * factor)
                total_w = jnp.sum(functools.reduce(jnp.add, sums), axis=0, keepdims=True)
                run_ref[cur, 0:1] = new
                run_ref[cur, 1:2] = run_ref[cur, 1:2] * f + total_w
                row = pl.ds(pl.multiple_of(kt * TK, TK), TK)
                racc_ref[cur] = racc_ref[cur] * f + mm(
                    wvt[:, row], jnp.concatenate(parts, axis=0)
                )

            def sweep(kt, masked):
                for x in range(len(chains) - 1):
                    stage(x, kt, x + 1, kt, masked)
                stage(len(chains) - 1, kt, 0, jnp.minimum(kt + 1, tiles - 1), False)

            smax_ref[0] = functools.reduce(
                jnp.maximum, [scores(0, tile0, part, True) for part in range(TK // CH)]
            )
            sweep(tile0, True)

            def step(kt, carry):
                sweep(kt, False)
                return carry

            lax.fori_loop(tile0 + 1, tiles, step, 0)
            i = lax.broadcasted_iota(jnp.int32, (1, wq), 1) + first
            live = i < lead_rows
            for x, (h, c) in enumerate(chains):
                col = column(h, c)
                ok = live[:, c * TC : (c + 1) * TC]
                st2_ref[1:2, col] = jnp.where(ok, run_ref[x, 1:2], st2_ref[1:2, col])
                acc_ref[:, col] = jnp.where(ok, racc_ref[x], acc_ref[:, col])
            return carry

        lax.fori_loop(0, (lead_rows + wq - 1) // wq, qtile, 0)

    link = linked.astype(F32)
    pad = lax.broadcasted_iota(jnp.int32, (n, 16), 1)
    v_aug = jnp.concatenate([v_ref[...], (pad < 2).astype(F32).astype(BF)], axis=1)
    statet_b = statet_ref[...].astype(BF)
    csum_b = csum_ref[:, :16].astype(BF)
    csum_b = jnp.where(pad[:width] < 2, csum_b.astype(F32), 0.0).astype(BF)
    state_aug = jnp.concatenate([state_ref[...].astype(BF), csum_b], axis=1)
    csum_row = jnp.sum(jnp.where(lax.broadcasted_iota(jnp.int32, csum_ref.shape, 1) == 0, csum_ref[...], 0.0).T, axis=0, keepdims=True)
    edge_row = lax.broadcasted_iota(jnp.int32, (16, width), 0)
    csum_hi = csum_row.astype(BF).astype(F32)
    csum_rows = jnp.where(edge_row == 0, csum_hi, jnp.where(edge_row == 1, csum_row - csum_hi, 0.0))
    statet_aug = jnp.concatenate([statet_b, csum_rows.astype(BF)], axis=0)
    kft_b = kf_ref[...].astype(BF)
    steps = [(qt, h) for qt in range(n // TQ) for h in range(heads)]
    held = {}

    def before(t):
        qt, h = steps[t]
        first = qt * TQ
        limit = first + TQ
        col = slice(h * n + first, h * n + limit)
        r = (start_ref[:, first:limit] == 0).astype(F32) * link
        qf = qf_ref[:, col]
        qf_b = qf.astype(BF)
        qf_r = (qf * r).astype(BF)
        carried = mm(statet_aug, qf_r)
        teacher = acc_ref[:, col] * (1.0 / st2_ref[1:2, col])
        inv = 1.0 / (st2_ref[2:3, col] + carried[width : width + 1] + carried[width + 1 : width + 2])
        est = (num_ref[:, col] + carried[:width]) * inv
        stu_ref[first:limit, h * width : (h + 1) * width] = est.T.astype(BF)
        diff = est - teacher
        inv = inv * grad_scale
        gd = -jnp.sum(diff * est, axis=0, keepdims=True) * inv
        gd_hi = gd.astype(BF).astype(F32)
        row = lax.broadcasted_iota(jnp.int32, (16, TQ), 0)
        gd_rows = jnp.where(row == 0, gd_hi, jnp.where(row == 1, gd - gd_hi, 0.0))
        gn = diff * inv
        g = jnp.concatenate([gn.astype(BF), gd_rows.astype(BF)], axis=0)
        g_r = jnp.concatenate([(gn * r).astype(BF), (gd_rows * r).astype(BF)], axis=0)
        held[t] = (first, limit, h, qf_b, qf_r, g, g_r)

    def first_product(t):
        held[t] += (mm(v_aug[: held[t][1]], held[t][5]),)

    def second_product(t):
        first, limit, h, qf_b, qf_r, g, g_r, raw = held[t]
        start = start_ref[:, first:limit]
        j = lax.broadcasted_iota(jnp.int32, (TQ, TQ), 0) + first
        i = lax.broadcasted_iota(jnp.int32, (1, TQ), 1) + first
        gp = jnp.where((j <= i) & (j >= start), raw[first:], 0.0).astype(BF)
        if first:
            j = lax.broadcasted_iota(jnp.int32, (first, TQ), 0)
            gp = jnp.concatenate([jnp.where(j >= start, raw[:first], 0.0).astype(BF), gp], axis=0)
        gkf2_ref[:limit] += mm(gp, qf_b, NT)
        adj_ref[...] += mm(qf_r, g, NT)
        held[t] = (first, limit, h, mm(jnp.concatenate([kft_b[:, :limit], state_aug], axis=1), jnp.concatenate([gp, g_r], axis=0)))

    def after(t):
        first, limit, h, gq = held.pop(t)
        col = slice(h * n + first, h * n + limit)
        ga = feature_back_t(qf_ref[:, col], gq).astype(BF)
        gwq_ref[h] += mm(ga, q_ref[first:limit, h * width : (h + 1) * width])

    count = len(steps)
    before(0)
    first_product(0)
    for t in range(count):
        if t + 1 < count:
            before(t + 1)
            first_product(t + 1)
        second_product(t)
        if t:
            after(t - 1)
    after(count - 1)

    gkf = gkf2_ref[...].T
    gkf_ref[...] = gkf * back_scale
    gl = feature_back_t(kf_ref[...], gkf).astype(BF)
    gwk_ref[...] += mm(gl, k_ref[...])
    adj_b = adj_ref[:, :width].astype(BF)
    adjs_col = adj_ref[:, width : width + 1] + adj_ref[:, width + 1 : width + 2]

    @pl.when(linked)
    def _():
        def back(kt, carry):
            row = pl.ds(pl.multiple_of(kt * TK, TK), TK)
            more = mm(adj_b, winv[row], NT) + adjs_col
            j = lax.broadcasted_iota(jnp.int32, (1, TK), 1) + kt * TK
            gl = feature_back_t(wkf[:, row], more)
            gl = jnp.where(j >= begin_key, gl, 0.0).astype(BF)
            gwk_ref[...] += mm(gl, wink[row])
            return carry

        lax.fori_loop(tile0, tiles, back, 0)

    for h in range(heads):
        wq_ref[h * half : (h + 1) * half] = gwq_ref[h].astype(BF)
    adjs_ref[...] = jnp.broadcast_to(adjs_col, adjs_ref.shape)
    row = jnp.max(adjs_ref[...].T, axis=0, keepdims=True)
    row_hi = row.astype(BF).astype(F32)
    tail = jnp.where(edge_row == 0, row_hi, jnp.where(edge_row == 1, row - row_hi, 0.0)).astype(BF)
    gwk_b = gwk_ref[...].astype(BF)
    tensor = len(outs)
    rows = width // tensor
    mine = lax.axis_index("tensor")
    for k in range(tensor):
        piece = pl.ds(pl.multiple_of(lax.rem(mine + k, tensor) * rows, rows), rows)
        outs[k][0:rows] = gkf_ref[piece].astype(BF)
        part = adj_ref[piece, :width].astype(BF)
        blocks = [part[c * 16 : (c + 1) * 16] for c in range(rows // 16)] + [tail]
        blocks += [gwk_b[c * 16 : (c + 1) * 16] for c in range(half // 16)]
        outs[k][rows:] = jnp.zeros_like(outs[k][rows:])
        for c, block in enumerate(blocks):
            outs[k][rows:, c * width : (c + 1) * width] = block


def join_kernel(tensor, doc_ref, wq_ref, *refs):
    ins, (sum_ref, out_ref) = refs[:tensor], refs[tensor:]
    rows = sum_ref.shape[0]
    width = out_ref.shape[1]
    half = width // 2
    total = ins[0][...].astype(F32)
    for k in range(1, tensor):
        total = total + ins[k][...].astype(F32)
    sum_ref[...] = total[:rows]
    at = wq_ref.shape[0]
    out_ref[0:at] = wq_ref[...]
    pieces = [total[rows:, c * width : (c + 1) * width] for c in range(total.shape[1] // width)]
    parts = rows // 16
    out_ref[at : at + rows] = jnp.concatenate(pieces[:parts], axis=0).astype(BF)
    at += rows
    tail = pieces[parts]
    row = tail[0:1] + tail[1:2]
    row_hi = row.astype(BF).astype(F32)
    index = lax.broadcasted_iota(jnp.int32, (16, width), 0)
    code = (doc_ref[0] + 1).astype(F32)
    tail = jnp.where(index == 0, row_hi, jnp.where(index == 1, row - row_hi, code))
    out_ref[at : at + 16] = tail.astype(BF)
    at += 16
    gwk = jnp.concatenate(pieces[parts + 1 : parts + 1 + half // 16], axis=0)
    hi = gwk.astype(BF)
    out_ref[at : at + half] = hi
    out_ref[at + half : at + 2 * half] = (gwk - hi.astype(F32)).astype(BF)


def last_kernel(
    seq, tensor, back_scale,
    doc_ref, edge_ref, gath_ref, sum_ref, v_ref,
    kfg_ref, gwq_ref, gwk_ref,
    adj_ref, adjs_ref, col_ref,
):
    n, width = v_ref.shape
    heads, half = gwq_ref.shape[:2]
    rows = sum_ref.shape[0]
    me = lax.axis_index("seq")
    mine = lax.axis_index("tensor")
    last_code = (doc_ref[n - 1] + 1).astype(F32)
    edge = edge_ref[n - 1]

    def gathered(first, size):
        x = gath_ref[0, first : first + size].astype(F32)
        for d in range(1, seq):
            x = x + gath_ref[d, first : first + size].astype(F32)
        return x

    for h in range(heads):
        gwq_ref[h] = gathered(h * half, half)
    at = heads * half
    gwk_ref[...] = gathered(at + rows + 16, half) + gathered(at + rows + 16 + half, half)
    adj_ref[...] = jnp.zeros_like(adj_ref)
    adjs_ref[...] = jnp.zeros_like(adjs_ref)

    def later(s, carry):
        a = gath_ref[s, at : at + rows].astype(F32)
        t = gath_ref[s, at + rows : at + rows + 16].astype(F32)
        same = t[2:3] == last_code
        adj_ref[...] += jnp.where(same, a, 0.0)
        adjs_ref[...] += jnp.where(same, t[0:1] + t[1:2], 0.0)
        return carry

    lax.fori_loop(me + 1, jnp.minimum(me + REACH + 1, seq), later, 0)
    adj = adj_ref[...]
    a_hi = adj.astype(BF)
    a_lo = (adj - a_hi.astype(F32)).astype(BF)
    col_ref[...] = jnp.broadcast_to(adjs_ref[...], (width, width)).T
    col = col_ref[pl.ds(pl.multiple_of(mine * rows, rows), rows), 0:1]
    j = lax.broadcasted_iota(jnp.int32, (1, n), 1)
    more = mm(a_hi, v_ref[...], NT) + mm(a_lo, v_ref[...], NT) + col
    kfg_ref[...] = sum_ref[...] + jnp.where(j >= edge, more, 0.0) * back_scale


VM = pl.BlockSpec(memory_space=pltpu.VMEM)
SM = pl.BlockSpec(memory_space=pltpu.SMEM)
ANY = pl.BlockSpec(memory_space=pl.ANY)


def grant(mib):
    return pltpu.CompilerParams(vmem_limit_bytes=mib << 20)


def cost(flops, size):
    return pl.CostEstimate(flops=flops, bytes_accessed=size, transcendentals=0)


def shards(queries, keys, values, doc_ids, w_query, w_key):
    n, heads, width = queries.shape
    half = w_key.shape[1]
    seq = lax.axis_size("seq")
    tensor = lax.axis_size("tensor")
    scale = width ** (-0.5)
    everyone = range(seq)
    assert n // width <= 16 and n // width * 16 == width

    codes = (doc_ids + 1).astype(BF).reshape(n // width, width)
    codes = jnp.pad(codes, ((0, 16 - n // width), (0, 0)))
    pack = jnp.concatenate([keys, values, codes], axis=0)

    def hop(x, distance):
        return lax.ppermute(x, "seq", [(i, i + distance) for i in everyone if i + distance < seq])

    own = lax.ppermute(pack, "seq", [(i, i + 1) for i in everyone if i % 2 == 0])
    four = hop(pack, 4)
    two = hop(pack, 2)

    qs = queries.reshape(n, heads * width)
    starts = jnp.sum((doc_ids[None, :] < doc_ids[:, None]).astype(jnp.int32), axis=1)
    start_row = starts.reshape(1, n)
    wq_t = jnp.transpose(w_query, (0, 2, 1))
    wk_t = w_key.T
    sds = jax.ShapeDtypeStruct
    cols = heads * n
    qf, kf, vt, acc, num, stat = pl.pallas_call(
        functools.partial(local_kernel, scale),
        out_shape=(
            sds((width, cols), F32), sds((width, n), F32), sds((width, n), BF),
            sds((width, cols), F32), sds((width, cols), F32), sds((8, cols), F32),
        ),
        in_specs=[VM] * 6,
        out_specs=[VM] * 6,
        scratch_shapes=[pltpu.VMEM((n, width), BF)],
        compiler_params=grant(16),
        cost_estimate=cost(8 * n * n * width * heads, 8 << 20),
    )(qs, keys, values, start_row, wq_t, wk_t)

    two, four, qf = lax.optimization_barrier((two, four, qf))
    swap_two = lax.ppermute(two, "seq", [(i, i ^ 1) for i in everyone])
    swap_four = lax.ppermute(four, "seq", [(i, i - 1) for i in everyone if i % 2 == 1])

    rows = width // tensor
    total = REACH * n
    chains = max(heads, 2)
    student, wq_part, *pieces = pl.pallas_call(
        functools.partial(main_kernel, scale, 2.0 / (n * seq), float(n * seq), tensor),
        out_shape=[sds((n, heads * width), BF), sds((heads * half, width), BF)]
        + [sds((rows + 16, n), BF)] * tensor,
        in_specs=[SM] + [VM] * 11 + [ANY] * 5,
        out_specs=[VM] * (2 + tensor),
        scratch_shapes=[
            pltpu.VMEM((total, width), BF),
            pltpu.VMEM((total, width), BF),
            pltpu.VMEM((REACH, 16, width), BF),
            pltpu.VMEM((width, total), F32),
            pltpu.VMEM((width, total), BF),
            pltpu.VMEM((heads, half, width), F32),
            pltpu.VMEM((half, width), F32),
            pltpu.VMEM((width, width + 16), F32),
            pltpu.VMEM((width, 128), F32),
            pltpu.VMEM((width, n), F32),
            pltpu.VMEM((n, width), F32),
            pltpu.VMEM((width, width), F32),
            pltpu.VMEM((width, width), F32),
            pltpu.VMEM((width, 128), F32),
            pltpu.VMEM((width, cols), F32),
            pltpu.VMEM((8, cols), F32),
            pltpu.VMEM((chains, 8, TC), F32),
            pltpu.VMEM((chains, width, TC), F32),
            pltpu.VMEM((chains, TK, TC), F32),
            pltpu.VMEM((chains, 8, TC), F32),
            pltpu.SemaphoreType.DMA((REACH, 3)),
        ],
        compiler_params=grant(36),
        cost_estimate=cost(16 * n * n * width * heads, 8 << 20),
    )(
        doc_ids, qs, keys, values, start_row, wk_t, qf, kf, vt, acc, num, stat,
        two, four, own, swap_two, swap_four,
    )

    arrived = [pieces[0]]
    for k in range(1, tensor):
        arrived.append(
            lax.ppermute(pieces[k], "tensor", [(i, (i + k) % tensor) for i in range(tensor)])
        )
    packed = heads * half + rows + 16 + 2 * half
    part, out = pl.pallas_call(
        functools.partial(join_kernel, tensor),
        out_shape=(sds((rows, n), F32), sds((packed, width), BF)),
        in_specs=[SM] + [VM] * (tensor + 1),
        out_specs=[VM] * 2,
        compiler_params=grant(8),
        cost_estimate=cost(n * width, 1 << 20),
    )(doc_ids, wq_part, *arrived)
    gathered = lax.all_gather(out, "seq")
    key_grads, gwq, gwk = pl.pallas_call(
        functools.partial(last_kernel, seq, tensor, float(n * seq)),
        out_shape=(sds((rows, n), F32), sds((heads, half, width), F32), sds((half, width), F32)),
        in_specs=[SM, SM, VM, VM, VM],
        out_specs=[VM] * 3,
        scratch_shapes=[
            pltpu.VMEM((rows, width), F32),
            pltpu.VMEM((1, width), F32),
            pltpu.VMEM((width, width), F32),
        ],
        compiler_params=grant(12),
        cost_estimate=cost(4 * n * width * width, 2 << 20),
    )(doc_ids, starts, gathered, part, values)
    return student.reshape(n, heads, width), jnp.transpose(gwq, (0, 2, 1)), gwk.T, key_grads.T


def solution(mesh):
    placed = (
        P("seq", "tensor", None),
        P("seq", None),
        P("seq", None),
        P("seq"),
        P("tensor", None, None),
        P(),
    )
    return jax.shard_map(
        shards,
        mesh=mesh,
        in_specs=placed,
        out_specs=(P("seq", "tensor", None), P("tensor", None, None), P(), P("seq", "tensor")),
        check_vma=False,
    )
```

```python
import functools

import jax
import jax.numpy as jnp
from jax import lax
from jax.experimental import pallas as pl
from jax.experimental.pallas import tpu as pltpu
from jax.sharding import PartitionSpec as P


REACH = 4
NEG = -1e30
LOG2E = 1.4426950408889634
TQ = 256
TK = 1024
TC = 256
CH = 256
BF = jnp.bfloat16
F32 = jnp.float32

NT = (((1,), (1,)), ((), ()))
NN = (((1,), (0,)), ((), ()))


def mm(a, b, dims=NN):
    return lax.dot_general(a, b, dims, preferred_element_type=F32)


def feature_t(logits):
    top = jnp.max(logits, axis=0, keepdims=True)
    low = jnp.min(logits, axis=0, keepdims=True)
    up = jnp.exp(logits - top)
    down = jnp.exp(low - logits)
    up = up * (1.0 / jnp.sum(up, axis=0, keepdims=True))
    down = down * (1.0 / jnp.sum(down, axis=0, keepdims=True))
    return jnp.concatenate([up, down], axis=0)


def feature_back_t(feat, grad):
    half = feat.shape[0] // 2
    p, m = feat[:half], feat[half:]
    a, b = grad[:half], grad[half:]
    return p * (a - jnp.sum(a * p, axis=0, keepdims=True)) - m * (
        b - jnp.sum(b * m, axis=0, keepdims=True)
    )


def allowed_t(limit, first, start):
    j = lax.broadcasted_iota(jnp.int32, (limit, TQ), 0)
    i = lax.broadcasted_iota(jnp.int32, (1, TQ), 1) + first
    return (j <= i) & (j >= start)


def transposed(x):
    return x.astype(F32).T


def teacher_kernel(scale, q_ref, k_ref, v_ref, start_ref, vt_ref, acc_ref, stat_ref):
    n, width = k_ref.shape
    heads = q_ref.shape[1] // width
    vt_ref[...] = transposed(v_ref[...]).astype(BF)

    def head(h, carry):
        lane = pl.multiple_of(h * width, width)
        for qt in range(n // TQ):
            first = qt * TQ
            limit = first + TQ
            col = pl.ds(pl.multiple_of(h * n + first, TQ), TQ)
            q = q_ref[first:limit, pl.ds(lane, width)]
            ok = allowed_t(limit, first, start_ref[:, first:limit])
            s = jnp.where(ok, mm(k_ref[:limit], q, NT), NEG)
            top = jnp.max(s, axis=0, keepdims=True)
            w = jnp.exp2((s - top) * (scale * LOG2E))
            stat_ref[0:1, col] = top
            stat_ref[1:2, col] = jnp.sum(w, axis=0, keepdims=True)
            acc_ref[:, col] = mm(vt_ref[:, :limit], w.astype(BF))
        return carry

    lax.fori_loop(0, heads, head, 0)


def student_kernel(
    q_ref, k_ref, vt_ref, start_ref, wq_ref, wk_ref, qf_ref, kf_ref, num_ref, den_ref, kfb_ref
):
    n, width = k_ref.shape
    heads = q_ref.shape[1] // width
    kf = feature_t(mm(wk_ref[...], k_ref[...], NT))
    kf_ref[...] = kf
    kfb_ref[...] = kf.T.astype(BF)

    def head(h, carry):
        lane = pl.multiple_of(h * width, width)
        for qt in range(n // TQ):
            first = qt * TQ
            limit = first + TQ
            col = pl.ds(pl.multiple_of(h * n + first, TQ), TQ)
            q = q_ref[first:limit, pl.ds(lane, width)]
            ok = allowed_t(limit, first, start_ref[:, first:limit])
            qf = feature_t(mm(wq_ref[h], q, NT))
            qf_ref[:, col] = qf
            pr = jnp.where(ok, mm(kfb_ref[:limit], qf.astype(BF)), 0.0)
            den_ref[0:1, col] = jnp.sum(pr, axis=0, keepdims=True)
            num_ref[:, col] = mm(vt_ref[:, :limit], pr.astype(BF))
        return carry

    lax.fori_loop(0, heads, head, 0)


def load(src, slot, keys, values, codes, sem):
    n = keys.shape[0] // codes.shape[0]
    return (
        pltpu.make_async_copy(src.at[0:n], keys.at[slot * n : (slot + 1) * n], sem.at[slot, 0]),
        pltpu.make_async_copy(src.at[n : 2 * n], values.at[slot * n : (slot + 1) * n], sem.at[slot, 1]),
        pltpu.make_async_copy(src.at[2 * n : 2 * n + 16], codes.at[slot], sem.at[slot, 2]),
    )


def begin(copies):
    for c in copies:
        c.start()


def finish(copies):
    for c in copies:
        c.wait()


def matching(codes, code):
    return jnp.sum((codes[...].astype(F32) == code).astype(jnp.int32))


def window_part(
    scale, n, heads, begin_key, stop_key, lead_rows,
    q_ref, wk_ref, wink, winv, wkf, wvt, statet_ref, csum_ref,
    acc_ref, st2_ref, run_ref, racc_ref, sbuf_ref, smax_ref,
):
    width = wink.shape[1]
    tile0 = begin_key // TK
    tiles = stop_key // TK

    @pl.when(begin_key < stop_key)
    def _():
        def prepare(kt, carry):
            row = pl.ds(pl.multiple_of(kt * TK, TK), TK)
            kf = feature_t(mm(wk_ref[...], wink[row], NT))
            wkf[:, row] = kf
            j = lax.broadcasted_iota(jnp.int32, (1, TK), 1) + kt * TK
            kfm = jnp.where(j >= begin_key, kf, 0.0).astype(BF)
            vt = transposed(winv[row]).astype(BF)
            wvt[:, row] = vt
            statet_ref[...] += mm(vt, kfm, NT)
            part = kfm.astype(F32)
            for c in range(TK // 128):
                csum_ref[...] += part[:, c * 128 : (c + 1) * 128]
            return carry

        lax.fori_loop(tile0, tiles, prepare, 0)
        wq = max(TC, 2 * TC // heads)
        chains = [(h, c) for h in range(heads) for c in range(wq // TC)]
        factor = scale * LOG2E

        def qtile(qt, carry):
            first = pl.multiple_of(qt * wq, wq)

            def column(h, c):
                return pl.ds(pl.multiple_of(h * n + first + c * TC, TC), TC)

            for x, (h, c) in enumerate(chains):
                col = column(h, c)
                run_ref[x, 0:1] = st2_ref[0:1, col]
                run_ref[x, 1:2] = st2_ref[1:2, col]
                racc_ref[x] = acc_ref[:, col]

            def scores(x, kt, part, masked):
                h, c = chains[x]
                q = q_ref[pl.ds(first + c * TC, TC), h * width : (h + 1) * width]
                row = pl.multiple_of(kt * TK + part * CH, CH)
                s = mm(wink[pl.ds(row, CH)], q, NT)
                if masked:
                    j = lax.broadcasted_iota(jnp.int32, (CH, 1), 0) + row
                    s = jnp.where(j >= begin_key, s, NEG)
                sbuf_ref[x, part * CH : (part + 1) * CH] = s
                return jnp.max(s.reshape(CH // 8, 8, TC), axis=0)

            def stage(cur, kt, nxt, kt_nxt, masked):
                old = run_ref[cur, 0:1]
                new = jnp.maximum(old, jnp.max(smax_ref[cur], axis=0, keepdims=True))
                tops, sums, parts = [], [], []
                for part in range(TK // CH):
                    tops.append(scores(nxt, kt_nxt, part, masked))
                    w = jnp.exp2((sbuf_ref[cur, part * CH : (part + 1) * CH] - new) * factor)
                    sums.append(jnp.sum(w.reshape(CH // 8, 8, TC), axis=0))
                    parts.append(w.astype(BF))
                smax_ref[nxt] = functools.reduce(jnp.maximum, tops)
                f = jnp.exp2((old - new) * factor)
                total_w = jnp.sum(functools.reduce(jnp.add, sums), axis=0, keepdims=True)
                run_ref[cur, 0:1] = new
                run_ref[cur, 1:2] = run_ref[cur, 1:2] * f + total_w
                row = pl.ds(pl.multiple_of(kt * TK, TK), TK)
                racc_ref[cur] = racc_ref[cur] * f + mm(
                    wvt[:, row], jnp.concatenate(parts, axis=0)
                )

            def sweep(kt, masked):
                for x in range(len(chains) - 1):
                    stage(x, kt, x + 1, kt, masked)
                stage(len(chains) - 1, kt, 0, jnp.minimum(kt + 1, tiles - 1), False)

            smax_ref[0] = functools.reduce(
                jnp.maximum, [scores(0, tile0, part, True) for part in range(TK // CH)]
            )
            sweep(tile0, True)

            def step(kt, carry):
                sweep(kt, False)
                return carry

            lax.fori_loop(tile0 + 1, tiles, step, 0)
            i = lax.broadcasted_iota(jnp.int32, (1, wq), 1) + first
            live = i < lead_rows
            for x, (h, c) in enumerate(chains):
                col = column(h, c)
                ok = live[:, c * TC : (c + 1) * TC]
                st2_ref[0:2, col] = jnp.where(ok, run_ref[x, 0:2], st2_ref[0:2, col])
                acc_ref[:, col] = jnp.where(ok, racc_ref[x], acc_ref[:, col])
            return carry

        lax.fori_loop(0, (lead_rows + wq - 1) // wq, qtile, 0)


def window_kernel(
    scale,
    doc_ref, q_ref, start_ref, wk_ref, acc_in, stat_in, own_ref, two_ref, swap_two_ref,
    acc_ref, st2_ref, wkf, statet_ref, csum_ref,
    wink, winv, wcode, wvt, run_ref, racc_ref, sbuf_ref, smax_ref, sem,
):
    width = wk_ref.shape[1]
    n = start_ref.shape[1]
    heads = q_ref.shape[1] // width
    odd = lax.rem(lax.axis_index("seq"), 2)
    begin(load(two_ref, 1, wink, winv, wcode, sem))

    @pl.when(odd == 0)
    def _():
        begin(load(swap_two_ref, 2, wink, winv, wcode, sem))
        wcode[0] = jnp.zeros_like(wcode[0])

    @pl.when(odd == 1)
    def _():
        begin(load(own_ref, 2, wink, winv, wcode, sem))
        begin(load(swap_two_ref, 0, wink, winv, wcode, sem))

    acc_ref[...] = acc_in[...]
    st2_ref[...] = stat_in[...]
    statet_ref[...] = jnp.zeros_like(statet_ref)
    csum_ref[...] = jnp.zeros_like(csum_ref)
    lead_code = (doc_ref[0] + 1).astype(F32)
    lead_rows = jnp.sum((start_ref[...] == 0).astype(jnp.int32))
    finish(load(two_ref, 1, wink, winv, wcode, sem))
    finish(load(two_ref, 2, wink, winv, wcode, sem))

    @pl.when(odd == 1)
    def _():
        finish(load(two_ref, 0, wink, winv, wcode, sem))

    stop_key = wink.shape[0]
    window_part(
        scale, n, heads, stop_key - matching(wcode, lead_code), stop_key, lead_rows,
        q_ref, wk_ref, wink, winv, wkf, wvt, statet_ref, csum_ref,
        acc_ref, st2_ref, run_ref, racc_ref, sbuf_ref, smax_ref,
    )


def main_kernel(
    scale, grad_scale, back_scale, tensor_size,
    doc_ref, q_ref, k_ref, v_ref, start_ref, wk_ref,
    qf_ref, kf_ref, acc_in, num_ref, stat_in, den_ref, near_kf, statet_in, csum_in,
    two_ref, four_ref, own_ref, swap_two_ref, swap_four_ref,
    stu_ref, wq_ref, *rest,
):
    outs = rest[:tensor_size]
    (
        neark, nearv, nearc, wink, winv, wcode, wkf, wvt,
        gwq_ref, gwk_ref, adj_ref, adjs_ref, gkf_ref, gkf2_ref,
        state_ref, statet_ref, csum_ref, acc_ref, st2_ref, run_ref, racc_ref, sbuf_ref, smax_ref,
        near_sem, sem,
    ) = rest[tensor_size:]
    n, width = k_ref.shape
    heads = q_ref.shape[1] // width
    half = wk_ref.shape[0]
    odd = lax.rem(lax.axis_index("seq"), 2)
    begin(load(four_ref, 0, wink, winv, wcode, sem))
    begin(load(two_ref, 1, neark, nearv, nearc, near_sem))

    @pl.when(odd == 0)
    def _():
        begin(load(swap_four_ref, 1, wink, winv, wcode, sem))
        begin(load(swap_two_ref, 2, neark, nearv, nearc, near_sem))
        nearc[0] = jnp.zeros_like(nearc[0])

    @pl.when(odd == 1)
    def _():
        begin(load(own_ref, 2, neark, nearv, nearc, near_sem))
        begin(load(swap_two_ref, 0, neark, nearv, nearc, near_sem))
        wcode[1] = jnp.zeros_like(wcode[1])

    gkf2_ref[...] = jnp.zeros_like(gkf2_ref)
    gwq_ref[...] = jnp.zeros_like(gwq_ref)
    gwk_ref[...] = jnp.zeros_like(gwk_ref)
    adj_ref[...] = jnp.zeros_like(adj_ref)
    statet_ref[...] = statet_in[...]
    csum_ref[...] = csum_in[...]
    acc_ref[...] = acc_in[...]
    st2_ref[...] = stat_in[...]
    lead_code = (doc_ref[0] + 1).astype(F32)
    lead_rows = jnp.sum((start_ref[...] == 0).astype(jnp.int32))
    finish(load(four_ref, 0, wink, winv, wcode, sem))
    finish(load(two_ref, 1, neark, nearv, nearc, near_sem))
    finish(load(two_ref, 2, neark, nearv, nearc, near_sem))

    @pl.when(odd == 0)
    def _():
        finish(load(four_ref, 1, wink, winv, wcode, sem))

    @pl.when(odd == 1)
    def _():
        finish(load(two_ref, 0, neark, nearv, nearc, near_sem))

    near_stop = neark.shape[0]
    near_begin = near_stop - matching(nearc, lead_code)
    far_stop = jnp.where(odd == 1, n, 2 * n)
    far_begin = far_stop - matching(wcode, lead_code)
    linked = near_begin < near_stop
    window_part(
        scale, n, heads, far_begin, far_stop, lead_rows,
        q_ref, wk_ref, wink, winv, wkf, wvt, statet_ref, csum_ref,
        acc_ref, st2_ref, run_ref, racc_ref, sbuf_ref, smax_ref,
    )
    state_ref[...] = statet_ref[...].T
    csum_ref[...] = jnp.broadcast_to(
        jnp.sum(csum_ref[...], axis=1, keepdims=True), csum_ref.shape
    )

    link = linked.astype(F32)
    pad = lax.broadcasted_iota(jnp.int32, (n, 16), 1)
    v_aug = jnp.concatenate([v_ref[...], (pad < 2).astype(F32).astype(BF)], axis=1)
    statet_b = statet_ref[...].astype(BF)
    csum_b = csum_ref[:, :16].astype(BF)
    csum_b = jnp.where(pad[:width] < 2, csum_b.astype(F32), 0.0).astype(BF)
    state_aug = jnp.concatenate([state_ref[...].astype(BF), csum_b], axis=1)
    csum_row = jnp.sum(jnp.where(lax.broadcasted_iota(jnp.int32, csum_ref.shape, 1) == 0, csum_ref[...], 0.0).T, axis=0, keepdims=True)
    edge_row = lax.broadcasted_iota(jnp.int32, (16, width), 0)
    csum_hi = csum_row.astype(BF).astype(F32)
    csum_rows = jnp.where(edge_row == 0, csum_hi, jnp.where(edge_row == 1, csum_row - csum_hi, 0.0))
    statet_aug = jnp.concatenate([statet_b, csum_rows.astype(BF)], axis=0)
    kft_b = kf_ref[...].astype(BF)
    steps = [(qt, h) for qt in range(n // TQ) for h in range(heads)]
    held = {}

    def before(t):
        qt, h = steps[t]
        first = qt * TQ
        limit = first + TQ
        col = slice(h * n + first, h * n + limit)
        r = (start_ref[:, first:limit] == 0).astype(F32) * link
        qf = qf_ref[:, col]
        qf_b = qf.astype(BF)
        qf_r = (qf * r).astype(BF)
        carried = mm(statet_aug, qf_r)
        teacher = acc_ref[:, col] * (1.0 / st2_ref[1:2, col])
        inv = 1.0 / (den_ref[0:1, col] + carried[width : width + 1] + carried[width + 1 : width + 2])
        est = (num_ref[:, col] + carried[:width]) * inv
        stu_ref[first:limit, h * width : (h + 1) * width] = est.T.astype(BF)
        diff = est - teacher
        inv = inv * grad_scale
        gd = -jnp.sum(diff * est, axis=0, keepdims=True) * inv
        gd_hi = gd.astype(BF).astype(F32)
        row = lax.broadcasted_iota(jnp.int32, (16, TQ), 0)
        gd_rows = jnp.where(row == 0, gd_hi, jnp.where(row == 1, gd - gd_hi, 0.0))
        gn = diff * inv
        g = jnp.concatenate([gn.astype(BF), gd_rows.astype(BF)], axis=0)
        g_r = jnp.concatenate([(gn * r).astype(BF), (gd_rows * r).astype(BF)], axis=0)
        held[t] = (first, limit, h, qf_b, qf_r, g, g_r)

    def first_product(t):
        held[t] += (mm(v_aug[: held[t][1]], held[t][5]),)

    def second_product(t):
        first, limit, h, qf_b, qf_r, g, g_r, raw = held[t]
        start = start_ref[:, first:limit]
        j = lax.broadcasted_iota(jnp.int32, (TQ, TQ), 0) + first
        i = lax.broadcasted_iota(jnp.int32, (1, TQ), 1) + first
        gp = jnp.where((j <= i) & (j >= start), raw[first:], 0.0).astype(BF)
        if first:
            j = lax.broadcasted_iota(jnp.int32, (first, TQ), 0)
            gp = jnp.concatenate([jnp.where(j >= start, raw[:first], 0.0).astype(BF), gp], axis=0)
        gkf2_ref[:limit] += mm(gp, qf_b, NT)
        adj_ref[...] += mm(qf_r, g, NT)
        held[t] = (first, limit, h, mm(jnp.concatenate([kft_b[:, :limit], state_aug], axis=1), jnp.concatenate([gp, g_r], axis=0)))

    def after(t):
        first, limit, h, gq = held.pop(t)
        col = slice(h * n + first, h * n + limit)
        ga = feature_back_t(qf_ref[:, col], gq).astype(BF)
        gwq_ref[h] += mm(ga, q_ref[first:limit, h * width : (h + 1) * width])

    count = len(steps)
    before(0)
    first_product(0)
    for t in range(count):
        if t + 1 < count:
            before(t + 1)
            first_product(t + 1)
        second_product(t)
        if t:
            after(t - 1)
    after(count - 1)

    gkf = gkf2_ref[...].T
    gkf_ref[...] = gkf * back_scale
    gl = feature_back_t(kf_ref[...], gkf).astype(BF)
    gwk_ref[...] += mm(gl, k_ref[...])
    adj_b = adj_ref[:, :width].astype(BF)
    adjs_col = adj_ref[:, width : width + 1] + adj_ref[:, width + 1 : width + 2]

    def back_over(begin_key, stop_key, keys, values, feats):
        def back(kt, carry):
            row = pl.ds(pl.multiple_of(kt * TK, TK), TK)
            more = mm(adj_b, values[row], NT) + adjs_col
            j = lax.broadcasted_iota(jnp.int32, (1, TK), 1) + kt * TK
            gl = feature_back_t(feats[:, row], more)
            gl = jnp.where(j >= begin_key, gl, 0.0).astype(BF)
            gwk_ref[...] += mm(gl, keys[row])
            return carry

        lax.fori_loop(begin_key // TK, stop_key // TK, back, 0)

    back_over(near_begin, near_stop, neark, nearv, near_kf)
    back_over(far_begin, far_stop, wink, winv, wkf)

    for h in range(heads):
        wq_ref[h * half : (h + 1) * half] = gwq_ref[h].astype(BF)
    adjs_ref[...] = jnp.broadcast_to(adjs_col, adjs_ref.shape)
    row = jnp.max(adjs_ref[...].T, axis=0, keepdims=True)
    row_hi = row.astype(BF).astype(F32)
    tail = jnp.where(edge_row == 0, row_hi, jnp.where(edge_row == 1, row - row_hi, 0.0)).astype(BF)
    gwk_b = gwk_ref[...].astype(BF)
    tensor = len(outs)
    rows = width // tensor
    mine = lax.axis_index("tensor")
    for k in range(tensor):
        piece = pl.ds(pl.multiple_of(lax.rem(mine + k, tensor) * rows, rows), rows)
        outs[k][0:rows] = gkf_ref[piece].astype(BF)
        part = adj_ref[piece, :width].astype(BF)
        blocks = [part[c * 16 : (c + 1) * 16] for c in range(rows // 16)] + [tail]
        blocks += [gwk_b[c * 16 : (c + 1) * 16] for c in range(half // 16)]
        outs[k][rows:] = jnp.zeros_like(outs[k][rows:])
        for c, block in enumerate(blocks):
            outs[k][rows:, c * width : (c + 1) * width] = block


def join_kernel(tensor, doc_ref, wq_ref, *refs):
    ins, (sum_ref, out_ref) = refs[:tensor], refs[tensor:]
    rows = sum_ref.shape[0]
    width = out_ref.shape[1]
    half = width // 2
    total = ins[0][...].astype(F32)
    for k in range(1, tensor):
        total = total + ins[k][...].astype(F32)
    sum_ref[...] = total[:rows]
    at = wq_ref.shape[0]
    out_ref[0:at] = wq_ref[...]
    pieces = [total[rows:, c * width : (c + 1) * width] for c in range(total.shape[1] // width)]
    parts = rows // 16
    out_ref[at : at + rows] = jnp.concatenate(pieces[:parts], axis=0).astype(BF)
    at += rows
    tail = pieces[parts]
    row = tail[0:1] + tail[1:2]
    row_hi = row.astype(BF).astype(F32)
    index = lax.broadcasted_iota(jnp.int32, (16, width), 0)
    code = (doc_ref[0] + 1).astype(F32)
    tail = jnp.where(index == 0, row_hi, jnp.where(index == 1, row - row_hi, code))
    out_ref[at : at + 16] = tail.astype(BF)
    at += 16
    gwk = jnp.concatenate(pieces[parts + 1 : parts + 1 + half // 16], axis=0)
    hi = gwk.astype(BF)
    out_ref[at : at + half] = hi
    out_ref[at + half : at + 2 * half] = (gwk - hi.astype(F32)).astype(BF)


def last_kernel(
    seq, back_scale,
    doc_ref, edge_ref, gath_ref, sum_ref, v_ref,
    kfg_ref, gwq_ref, gwk_ref,
    adj_ref, adjs_ref, col_ref,
):
    n, width = v_ref.shape
    heads, half = gwq_ref.shape[:2]
    rows = sum_ref.shape[0]
    me = lax.axis_index("seq")
    mine = lax.axis_index("tensor")
    last_code = (doc_ref[n - 1] + 1).astype(F32)
    edge = edge_ref[n - 1]

    def gathered(first, size):
        x = gath_ref[0, first : first + size].astype(F32)
        for d in range(1, seq):
            x = x + gath_ref[d, first : first + size].astype(F32)
        return x

    for h in range(heads):
        gwq_ref[h] = gathered(h * half, half)
    at = heads * half
    gwk_ref[...] = gathered(at + rows + 16, half) + gathered(at + rows + 16 + half, half)
    adj_ref[...] = jnp.zeros_like(adj_ref)
    adjs_ref[...] = jnp.zeros_like(adjs_ref)

    def later(s, carry):
        a = gath_ref[s, at : at + rows].astype(F32)
        t = gath_ref[s, at + rows : at + rows + 16].astype(F32)
        same = t[2:3] == last_code
        adj_ref[...] += jnp.where(same, a, 0.0)
        adjs_ref[...] += jnp.where(same, t[0:1] + t[1:2], 0.0)
        return carry

    lax.fori_loop(me + 1, jnp.minimum(me + REACH + 1, seq), later, 0)
    adj = adj_ref[...]
    a_hi = adj.astype(BF)
    a_lo = (adj - a_hi.astype(F32)).astype(BF)
    col_ref[...] = jnp.broadcast_to(adjs_ref[...], (width, width)).T
    col = col_ref[pl.ds(pl.multiple_of(mine * rows, rows), rows), 0:1]
    j = lax.broadcasted_iota(jnp.int32, (1, n), 1)
    more = mm(a_hi, v_ref[...], NT) + mm(a_lo, v_ref[...], NT) + col
    kfg_ref[...] = sum_ref[...] + jnp.where(j >= edge, more, 0.0) * back_scale


VM = pl.BlockSpec(memory_space=pltpu.VMEM)
SM = pl.BlockSpec(memory_space=pltpu.SMEM)
ANY = pl.BlockSpec(memory_space=pl.ANY)


def grant(mib):
    return pltpu.CompilerParams(vmem_limit_bytes=mib << 20)


def cost(flops, size):
    return pl.CostEstimate(flops=flops, bytes_accessed=size, transcendentals=0)


def shards(queries, keys, values, doc_ids, w_query, w_key):
    n, heads, width = queries.shape
    half = w_key.shape[1]
    seq = lax.axis_size("seq")
    tensor = lax.axis_size("tensor")
    scale = width ** (-0.5)
    everyone = range(seq)
    assert n // width <= 16 and n // width * 16 == width

    codes = (doc_ids + 1).astype(BF).reshape(n // width, width)
    codes = jnp.pad(codes, ((0, 16 - n // width), (0, 0)))
    pack = jnp.concatenate([keys, values, codes], axis=0)

    def hop(x, distance):
        return lax.ppermute(x, "seq", [(i, i + distance) for i in everyone if i + distance < seq])

    two = hop(pack, 2)
    own = lax.ppermute(pack, "seq", [(i, i + 1) for i in everyone if i % 2 == 0])

    qs = queries.reshape(n, heads * width)
    starts = jnp.sum((doc_ids[None, :] < doc_ids[:, None]).astype(jnp.int32), axis=1)
    start_row = starts.reshape(1, n)
    wq_t = jnp.transpose(w_query, (0, 2, 1))
    wk_t = w_key.T
    sds = jax.ShapeDtypeStruct
    cols = heads * n
    rows = width // tensor
    near = REACH - 1
    chains = max(heads, 2)
    square = sds((width, width), F32)
    wide = sds((width, cols), F32)
    flat = sds((8, cols), F32)
    scan = [
        pltpu.VMEM((chains, 8, TC), F32),
        pltpu.VMEM((chains, width, TC), F32),
        pltpu.VMEM((chains, TK, TC), F32),
        pltpu.VMEM((chains, 8, TC), F32),
    ]
    vt, acc, stat = pl.pallas_call(
        functools.partial(teacher_kernel, scale),
        out_shape=(sds((width, n), BF), wide, flat),
        in_specs=[VM] * 4,
        out_specs=[VM] * 3,
        compiler_params=grant(12),
        cost_estimate=cost(4 * n * n * width * heads, 4 << 20),
    )(qs, keys, values, start_row)
    four = hop(pack, 4)
    qf, kf, num, den = pl.pallas_call(
        student_kernel,
        out_shape=(wide, sds((width, n), F32), wide, flat),
        in_specs=[VM] * 6,
        out_specs=[VM] * 4,
        scratch_shapes=[pltpu.VMEM((n, width), BF)],
        compiler_params=grant(12),
        cost_estimate=cost(4 * n * n * width * heads, 4 << 20),
    )(qs, keys, vt, start_row, wq_t, wk_t)

    swap_two = lax.ppermute(two, "seq", [(i, i ^ 1) for i in everyone])
    acc, stat, near_kf, statet, csum = pl.pallas_call(
        functools.partial(window_kernel, scale),
        out_shape=(wide, flat, sds((width, near * n), F32), square, square),
        in_specs=[SM] + [VM] * 5 + [ANY] * 3,
        out_specs=[VM] * 5,
        scratch_shapes=[
            pltpu.VMEM((near * n, width), BF),
            pltpu.VMEM((near * n, width), BF),
            pltpu.VMEM((near, 16, width), BF),
            pltpu.VMEM((width, near * n), BF),
        ]
        + scan
        + [pltpu.SemaphoreType.DMA((near, 3))],
        compiler_params=grant(20),
        cost_estimate=cost(8 * n * n * width * heads, 4 << 20),
    )(doc_ids, qs, start_row, wk_t, acc, stat, own, two, swap_two)

    swap_four = lax.ppermute(four, "seq", [(i, i - 1) for i in everyone if i % 2 == 1])
    student, wq_part, *pieces = pl.pallas_call(
        functools.partial(main_kernel, scale, 2.0 / (n * seq), float(n * seq), tensor),
        out_shape=[sds((n, heads * width), BF), sds((heads * half, width), BF)]
        + [sds((rows + 16, n), BF)] * tensor,
        in_specs=[SM] + [VM] * 14 + [ANY] * 5,
        out_specs=[VM] * (2 + tensor),
        scratch_shapes=[
            pltpu.VMEM((near * n, width), BF),
            pltpu.VMEM((near * n, width), BF),
            pltpu.VMEM((near, 16, width), BF),
            pltpu.VMEM((2 * n, width), BF),
            pltpu.VMEM((2 * n, width), BF),
            pltpu.VMEM((2, 16, width), BF),
            pltpu.VMEM((width, 2 * n), F32),
            pltpu.VMEM((width, 2 * n), BF),
            pltpu.VMEM((heads, half, width), F32),
            pltpu.VMEM((half, width), F32),
            pltpu.VMEM((width, width + 16), F32),
            pltpu.VMEM((width, 128), F32),
            pltpu.VMEM((width, n), F32),
            pltpu.VMEM((n, width), F32),
            pltpu.VMEM((width, width), F32),
            pltpu.VMEM((width, width), F32),
            pltpu.VMEM((width, 128), F32),
            pltpu.VMEM((width, cols), F32),
            pltpu.VMEM((8, cols), F32),
        ]
        + scan
        + [pltpu.SemaphoreType.DMA((near, 3)), pltpu.SemaphoreType.DMA((2, 3))],
        compiler_params=grant(32),
        cost_estimate=cost(16 * n * n * width * heads, 8 << 20),
    )(
        doc_ids, qs, keys, values, start_row, wk_t,
        qf, kf, acc, num, stat, den, near_kf, statet, csum,
        two, four, own, swap_two, swap_four,
    )

    arrived = [pieces[0]]
    for k in range(1, tensor):
        arrived.append(
            lax.ppermute(pieces[k], "tensor", [(i, (i + k) % tensor) for i in range(tensor)])
        )
    packed = heads * half + rows + 16 + 2 * half
    part, out = pl.pallas_call(
        functools.partial(join_kernel, tensor),
        out_shape=(sds((rows, n), F32), sds((packed, width), BF)),
        in_specs=[SM] + [VM] * (tensor + 1),
        out_specs=[VM] * 2,
        compiler_params=grant(8),
        cost_estimate=cost(n * width, 1 << 20),
    )(doc_ids, wq_part, *arrived)
    gathered = lax.all_gather(out, "seq")
    key_grads, gwq, gwk = pl.pallas_call(
        functools.partial(last_kernel, seq, float(n * seq)),
        out_shape=(sds((rows, n), F32), sds((heads, half, width), F32), sds((half, width), F32)),
        in_specs=[SM, SM, VM, VM, VM],
        out_specs=[VM] * 3,
        scratch_shapes=[
            pltpu.VMEM((rows, width), F32),
            pltpu.VMEM((1, width), F32),
            pltpu.VMEM((width, width), F32),
        ],
        compiler_params=grant(12),
        cost_estimate=cost(4 * n * width * width, 2 << 20),
    )(doc_ids, starts, gathered, part, values)
    return student.reshape(n, heads, width), jnp.transpose(gwq, (0, 2, 1)), gwk.T, key_grads.T


def solution(mesh):
    placed = (
        P("seq", "tensor", None),
        P("seq", None),
        P("seq", None),
        P("seq"),
        P("tensor", None, None),
        P(),
    )

    return jax.shard_map(
        shards,
        mesh=mesh,
        in_specs=placed,
        out_specs=(P("seq", "tensor", None), P("tensor", None, None), P(), P("seq", "tensor")),
        check_vma=False,
    )
```

```python
import functools

import jax
import jax.numpy as jnp
from jax import lax
from jax.experimental import pallas as pl
from jax.experimental.pallas import tpu as pltpu
from jax.sharding import PartitionSpec as P


REACH = 4
NEG = -1e30
LOG2E = 1.4426950408889634
TQ = 256
TK = 1024
TC = 256
CH = 512
CHAINS = 4
BF = jnp.bfloat16
F32 = jnp.float32

NT = (((1,), (1,)), ((), ()))
NN = (((1,), (0,)), ((), ()))


def mm(a, b, dims=NN):
    return lax.dot_general(a, b, dims, preferred_element_type=F32)


def feature_t(logits):
    top = jnp.max(logits, axis=0, keepdims=True)
    low = jnp.min(logits, axis=0, keepdims=True)
    up = jnp.exp(logits - top)
    down = jnp.exp(low - logits)
    up = up * (1.0 / jnp.sum(up, axis=0, keepdims=True))
    down = down * (1.0 / jnp.sum(down, axis=0, keepdims=True))
    return jnp.concatenate([up, down], axis=0)


def feature_back_t(feat, grad):
    half = feat.shape[0] // 2
    p, m = feat[:half], feat[half:]
    a, b = grad[:half], grad[half:]
    return p * (a - jnp.sum(a * p, axis=0, keepdims=True)) - m * (
        b - jnp.sum(b * m, axis=0, keepdims=True)
    )


def allowed_t(limit, first, start):
    j = lax.broadcasted_iota(jnp.int32, (limit, TQ), 0)
    i = lax.broadcasted_iota(jnp.int32, (1, TQ), 1) + first
    return (j <= i) & (j >= start)


def transposed(x):
    return x.astype(F32).T


def teacher_kernel(scale, q_ref, k_ref, v_ref, start_ref, vt_ref, acc_ref, stat_ref):
    n, width = k_ref.shape
    heads = q_ref.shape[1] // width
    vt_ref[...] = transposed(v_ref[...]).astype(BF)

    def head(h, carry):
        lane = pl.multiple_of(h * width, width)
        for qt in range(n // TQ):
            first = qt * TQ
            limit = first + TQ
            col = pl.ds(pl.multiple_of(h * n + first, TQ), TQ)
            q = q_ref[first:limit, pl.ds(lane, width)]
            ok = allowed_t(limit, first, start_ref[:, first:limit])
            s = jnp.where(ok, mm(k_ref[:limit], q, NT), NEG)
            top = jnp.max(s, axis=0, keepdims=True)
            w = jnp.exp2((s - top) * (scale * LOG2E))
            stat_ref[0:1, col] = top
            stat_ref[1:2, col] = jnp.sum(w, axis=0, keepdims=True)
            acc_ref[:, col] = mm(vt_ref[:, :limit], w.astype(BF))
        return carry

    lax.fori_loop(0, heads, head, 0)


def student_kernel(
    q_ref, k_ref, vt_ref, start_ref, wq_ref, wk_ref, qf_ref, kf_ref, num_ref, den_ref, kfb_ref
):
    n, width = k_ref.shape
    heads = q_ref.shape[1] // width
    kf = feature_t(mm(wk_ref[...], k_ref[...], NT))
    kf_ref[...] = kf
    kfb_ref[...] = kf.T.astype(BF)

    def head(h, carry):
        lane = pl.multiple_of(h * width, width)
        for qt in range(n // TQ):
            first = qt * TQ
            limit = first + TQ
            col = pl.ds(pl.multiple_of(h * n + first, TQ), TQ)
            q = q_ref[first:limit, pl.ds(lane, width)]
            ok = allowed_t(limit, first, start_ref[:, first:limit])
            qf = feature_t(mm(wq_ref[h], q, NT))
            qf_ref[:, col] = qf
            pr = jnp.where(ok, mm(kfb_ref[:limit], qf.astype(BF)), 0.0)
            den_ref[0:1, col] = jnp.sum(pr, axis=0, keepdims=True)
            num_ref[:, col] = mm(vt_ref[:, :limit], pr.astype(BF))
        return carry

    lax.fori_loop(0, heads, head, 0)


def load(src, slot, keys, values, codes, sem):
    n = keys.shape[0] // codes.shape[0]
    return (
        pltpu.make_async_copy(src.at[0:n], keys.at[slot * n : (slot + 1) * n], sem.at[slot, 0]),
        pltpu.make_async_copy(src.at[n : 2 * n], values.at[slot * n : (slot + 1) * n], sem.at[slot, 1]),
        pltpu.make_async_copy(src.at[2 * n : 2 * n + 16], codes.at[slot], sem.at[slot, 2]),
    )


def begin(copies):
    for c in copies:
        c.start()


def finish(copies):
    for c in copies:
        c.wait()


def matching(codes, code):
    return jnp.sum((codes[...].astype(F32) == code).astype(jnp.int32))


def window_part(
    scale, n, heads, begin_key, stop_key, lead_rows,
    q_ref, wk_ref, wink, winv, wkf, wvt, statet_ref, csum_ref,
    acc_ref, st2_ref, run_ref, racc_ref, sbuf_ref, smax_ref,
):
    width = wink.shape[1]
    tile0 = begin_key // TK
    tiles = stop_key // TK
    cut = jnp.minimum(begin_key - tile0 * TK, 1)

    @pl.when(begin_key < stop_key)
    def _():
        def prepare(kt, carry):
            row = pl.ds(pl.multiple_of(kt * TK, TK), TK)
            kf = feature_t(mm(wk_ref[...], wink[row], NT))
            wkf[:, row] = kf
            j = lax.broadcasted_iota(jnp.int32, (1, TK), 1) + kt * TK
            kfm = jnp.where(j >= begin_key, kf, 0.0).astype(BF)
            vt = transposed(winv[row]).astype(BF)
            wvt[:, row] = vt
            statet_ref[...] += mm(vt, kfm, NT)
            part = kfm.astype(F32)
            for c in range(TK // 128):
                csum_ref[...] += part[:, c * 128 : (c + 1) * 128]
            return carry

        lax.fori_loop(tile0, tiles, prepare, 0)
        wq = min(n, CHAINS * TC // heads)
        chains = [(h, c) for h in range(heads) for c in range(wq // TC)]
        factor = scale * LOG2E

        def qtile(qt, carry):
            first = pl.multiple_of(qt * wq, wq)

            def column(h, c):
                return pl.ds(pl.multiple_of(h * n + first + c * TC, TC), TC)

            for x, (h, c) in enumerate(chains):
                col = column(h, c)
                run_ref[x, 0:1] = st2_ref[0:1, col]
                run_ref[x, 1:2] = st2_ref[1:2, col]
                racc_ref[x] = acc_ref[:, col]

            def scores(x, kt, part, masked):
                h, c = chains[x]
                q = q_ref[pl.ds(first + c * TC, TC), h * width : (h + 1) * width]
                row = pl.multiple_of(kt * TK + part * CH, CH)
                s = mm(wink[pl.ds(row, CH)], q, NT)
                if masked:
                    j = lax.broadcasted_iota(jnp.int32, (CH, 1), 0) + row
                    s = jnp.where(j >= begin_key, s, NEG)
                sbuf_ref[x, part * CH : (part + 1) * CH] = s
                return jnp.max(s.reshape(CH // 8, 8, TC), axis=0)

            def stage(cur, kt, nxt, kt_nxt, masked):
                old = run_ref[cur, 0:1]
                new = jnp.maximum(old, jnp.max(smax_ref[cur], axis=0, keepdims=True))
                tops, sums, parts = [], [], []
                for part in range(TK // CH):
                    tops.append(scores(nxt, kt_nxt, part, masked))
                    w = jnp.exp2((sbuf_ref[cur, part * CH : (part + 1) * CH] - new) * factor)
                    sums.append(jnp.sum(w.reshape(CH // 8, 8, TC), axis=0))
                    parts.append(w.astype(BF))
                smax_ref[nxt] = functools.reduce(jnp.maximum, tops)
                f = jnp.exp2((old - new) * factor)
                total_w = jnp.sum(functools.reduce(jnp.add, sums), axis=0, keepdims=True)
                run_ref[cur, 0:1] = new
                run_ref[cur, 1:2] = run_ref[cur, 1:2] * f + total_w
                row = pl.ds(pl.multiple_of(kt * TK, TK), TK)
                racc_ref[cur] = racc_ref[cur] * f + mm(
                    wvt[:, row], jnp.concatenate(parts, axis=0)
                )

            def sweep(kt, masked):
                for x in range(len(chains) - 1):
                    stage(x, kt, x + 1, kt, masked)
                stage(len(chains) - 1, kt, 0, jnp.minimum(kt + 1, tiles - 1), False)

            def prime(masked):
                smax_ref[0] = functools.reduce(
                    jnp.maximum, [scores(0, tile0, part, masked) for part in range(TK // CH)]
                )

            @pl.when(cut > 0)
            def _():
                prime(True)
                sweep(tile0, True)

            @pl.when(cut == 0)
            def _():
                prime(False)


            def step(kt, carry):
                sweep(kt, False)
                return carry

            lax.fori_loop(tile0 + cut, tiles, step, 0)
            i = lax.broadcasted_iota(jnp.int32, (1, wq), 1) + first
            live = i < lead_rows
            for x, (h, c) in enumerate(chains):
                col = column(h, c)
                ok = live[:, c * TC : (c + 1) * TC]
                st2_ref[0:2, col] = jnp.where(ok, run_ref[x, 0:2], st2_ref[0:2, col])
                acc_ref[:, col] = jnp.where(ok, racc_ref[x], acc_ref[:, col])
            return carry

        lax.fori_loop(0, (lead_rows + wq - 1) // wq, qtile, 0)


def window_kernel(
    scale,
    doc_ref, q_ref, start_ref, wk_ref, acc_in, stat_in, own_ref, two_ref, swap_two_ref,
    acc_ref, st2_ref, wkf, statet_ref, csum_ref,
    wink, winv, wcode, wvt, run_ref, racc_ref, sbuf_ref, smax_ref, sem,
):
    width = wk_ref.shape[1]
    n = start_ref.shape[1]
    heads = q_ref.shape[1] // width
    odd = lax.rem(lax.axis_index("seq"), 2)
    begin(load(two_ref, 0, wink, winv, wcode, sem))

    @pl.when(odd == 0)
    def _():
        begin(load(swap_two_ref, 1, wink, winv, wcode, sem))

    @pl.when(odd == 1)
    def _():
        begin(load(own_ref, 1, wink, winv, wcode, sem))

    acc_ref[...] = acc_in[...]
    st2_ref[...] = stat_in[...]
    statet_ref[...] = jnp.zeros_like(statet_ref)
    csum_ref[...] = jnp.zeros_like(csum_ref)
    lead_code = (doc_ref[0] + 1).astype(F32)
    lead_rows = jnp.sum((start_ref[...] == 0).astype(jnp.int32))
    finish(load(two_ref, 0, wink, winv, wcode, sem))
    finish(load(two_ref, 1, wink, winv, wcode, sem))

    stop_key = wink.shape[0]
    window_part(
        scale, n, heads, stop_key - matching(wcode, lead_code), stop_key, lead_rows,
        q_ref, wk_ref, wink, winv, wkf, wvt, statet_ref, csum_ref,
        acc_ref, st2_ref, run_ref, racc_ref, sbuf_ref, smax_ref,
    )


def main_kernel(
    scale, grad_scale, back_scale, tensor_size,
    doc_ref, q_ref, k_ref, v_ref, start_ref, wk_ref,
    qf_ref, kf_ref, acc_in, num_ref, stat_in, den_ref, near_kf, statet_in, csum_in,
    two_ref, four_ref, own_ref, swap_two_ref, swap_four_ref,
    stu_ref, wq_ref, *rest,
):
    outs = rest[:tensor_size]
    (
        neark, nearv, nearc, wink, winv, wcode, wkf, wvt,
        gwq_ref, gwk_ref, adj_ref, adjs_ref, gkf_ref, gkf2_ref,
        state_ref, statet_ref, csum_ref, acc_ref, st2_ref, run_ref, racc_ref, sbuf_ref, smax_ref,
        near_sem, sem,
    ) = rest[tensor_size:]
    n, width = k_ref.shape
    heads = q_ref.shape[1] // width
    half = wk_ref.shape[0]
    odd = lax.rem(lax.axis_index("seq"), 2)
    begin(load(four_ref, 0, wink, winv, wcode, sem))
    begin(load(two_ref, 0, neark, nearv, nearc, near_sem))

    @pl.when(odd == 0)
    def _():
        begin(load(swap_four_ref, 1, wink, winv, wcode, sem))
        begin(load(swap_two_ref, 1, neark, nearv, nearc, near_sem))

    @pl.when(odd == 1)
    def _():
        begin(load(swap_two_ref, 1, wink, winv, wcode, sem))
        begin(load(own_ref, 1, neark, nearv, nearc, near_sem))

    gkf2_ref[...] = jnp.zeros_like(gkf2_ref)
    gwq_ref[...] = jnp.zeros_like(gwq_ref)
    gwk_ref[...] = jnp.zeros_like(gwk_ref)
    adj_ref[...] = jnp.zeros_like(adj_ref)
    statet_ref[...] = statet_in[...]
    csum_ref[...] = csum_in[...]
    acc_ref[...] = acc_in[...]
    st2_ref[...] = stat_in[...]
    lead_code = (doc_ref[0] + 1).astype(F32)
    lead_rows = jnp.sum((start_ref[...] == 0).astype(jnp.int32))
    for slot in range(2):
        finish(load(four_ref, slot, wink, winv, wcode, sem))
        finish(load(two_ref, slot, neark, nearv, nearc, near_sem))

    near_stop = neark.shape[0]
    near_begin = near_stop - matching(nearc, lead_code)
    far_stop = wink.shape[0]
    far_begin = far_stop - matching(wcode, lead_code)
    linked = near_begin < near_stop
    window_part(
        scale, n, heads, far_begin, far_stop, lead_rows,
        q_ref, wk_ref, wink, winv, wkf, wvt, statet_ref, csum_ref,
        acc_ref, st2_ref, run_ref, racc_ref, sbuf_ref, smax_ref,
    )
    state_ref[...] = statet_ref[...].T
    csum_ref[...] = jnp.broadcast_to(
        jnp.sum(csum_ref[...], axis=1, keepdims=True), csum_ref.shape
    )

    link = linked.astype(F32)
    pad = lax.broadcasted_iota(jnp.int32, (n, 16), 1)
    v_aug = jnp.concatenate([v_ref[...], (pad < 2).astype(F32).astype(BF)], axis=1)
    statet_b = statet_ref[...].astype(BF)
    csum_b = csum_ref[:, :16].astype(BF)
    csum_b = jnp.where(pad[:width] < 2, csum_b.astype(F32), 0.0).astype(BF)
    state_aug = jnp.concatenate([state_ref[...].astype(BF), csum_b], axis=1)
    csum_row = jnp.sum(jnp.where(lax.broadcasted_iota(jnp.int32, csum_ref.shape, 1) == 0, csum_ref[...], 0.0).T, axis=0, keepdims=True)
    edge_row = lax.broadcasted_iota(jnp.int32, (16, width), 0)
    csum_hi = csum_row.astype(BF).astype(F32)
    csum_rows = jnp.where(edge_row == 0, csum_hi, jnp.where(edge_row == 1, csum_row - csum_hi, 0.0))
    statet_aug = jnp.concatenate([statet_b, csum_rows.astype(BF)], axis=0)
    kft_b = kf_ref[...].astype(BF)
    steps = [(qt, h) for qt in range(n // TQ) for h in range(heads)]
    held = {}

    def before(t):
        qt, h = steps[t]
        first = qt * TQ
        limit = first + TQ
        col = slice(h * n + first, h * n + limit)
        r = (start_ref[:, first:limit] == 0).astype(F32) * link
        qf = qf_ref[:, col]
        qf_b = qf.astype(BF)
        qf_r = (qf * r).astype(BF)
        carried = mm(statet_aug, qf_r)
        teacher = acc_ref[:, col] * (1.0 / st2_ref[1:2, col])
        inv = 1.0 / (den_ref[0:1, col] + carried[width : width + 1] + carried[width + 1 : width + 2])
        est = (num_ref[:, col] + carried[:width]) * inv
        stu_ref[first:limit, h * width : (h + 1) * width] = est.T.astype(BF)
        diff = est - teacher
        inv = inv * grad_scale
        gd = -jnp.sum(diff * est, axis=0, keepdims=True) * inv
        gd_hi = gd.astype(BF).astype(F32)
        row = lax.broadcasted_iota(jnp.int32, (16, TQ), 0)
        gd_rows = jnp.where(row == 0, gd_hi, jnp.where(row == 1, gd - gd_hi, 0.0))
        gn = diff * inv
        g = jnp.concatenate([gn.astype(BF), gd_rows.astype(BF)], axis=0)
        g_r = jnp.concatenate([(gn * r).astype(BF), (gd_rows * r).astype(BF)], axis=0)
        held[t] = (first, limit, h, qf_b, qf_r, g, g_r)

    def first_product(t):
        held[t] += (mm(v_aug[: held[t][1]], held[t][5]),)

    def second_product(t):
        first, limit, h, qf_b, qf_r, g, g_r, raw = held[t]
        start = start_ref[:, first:limit]
        j = lax.broadcasted_iota(jnp.int32, (TQ, TQ), 0) + first
        i = lax.broadcasted_iota(jnp.int32, (1, TQ), 1) + first
        gp = jnp.where((j <= i) & (j >= start), raw[first:], 0.0).astype(BF)
        if first:
            j = lax.broadcasted_iota(jnp.int32, (first, TQ), 0)
            gp = jnp.concatenate([jnp.where(j >= start, raw[:first], 0.0).astype(BF), gp], axis=0)
        gkf2_ref[:limit] += mm(gp, qf_b, NT)
        adj_ref[...] += mm(qf_r, g, NT)
        held[t] = (first, limit, h, mm(jnp.concatenate([kft_b[:, :limit], state_aug], axis=1), jnp.concatenate([gp, g_r], axis=0)))

    def after(t):
        first, limit, h, gq = held.pop(t)
        col = slice(h * n + first, h * n + limit)
        ga = feature_back_t(qf_ref[:, col], gq).astype(BF)
        gwq_ref[h] += mm(ga, q_ref[first:limit, h * width : (h + 1) * width])

    count = len(steps)
    before(0)
    first_product(0)
    for t in range(count):
        if t + 1 < count:
            before(t + 1)
            first_product(t + 1)
        second_product(t)
        if t:
            after(t - 1)
    after(count - 1)

    gkf = gkf2_ref[...].T
    gkf_ref[...] = gkf * back_scale
    gl = feature_back_t(kf_ref[...], gkf).astype(BF)
    gwk_ref[...] += mm(gl, k_ref[...])
    adj_b = adj_ref[:, :width].astype(BF)
    adjs_col = adj_ref[:, width : width + 1] + adj_ref[:, width + 1 : width + 2]

    def back_over(begin_key, stop_key, keys, values, feats):
        def back(kt, carry):
            row = pl.ds(pl.multiple_of(kt * TK, TK), TK)
            more = mm(adj_b, values[row], NT) + adjs_col
            j = lax.broadcasted_iota(jnp.int32, (1, TK), 1) + kt * TK
            gl = feature_back_t(feats[:, row], more)
            gl = jnp.where(j >= begin_key, gl, 0.0).astype(BF)
            gwk_ref[...] += mm(gl, keys[row])
            return carry

        lax.fori_loop(begin_key // TK, stop_key // TK, back, 0)

    back_over(near_begin, near_stop, neark, nearv, near_kf)
    back_over(far_begin, far_stop, wink, winv, wkf)

    for h in range(heads):
        wq_ref[h * half : (h + 1) * half] = gwq_ref[h].astype(BF)
    adjs_ref[...] = jnp.broadcast_to(adjs_col, adjs_ref.shape)
    row = jnp.max(adjs_ref[...].T, axis=0, keepdims=True)
    row_hi = row.astype(BF).astype(F32)
    tail = jnp.where(edge_row == 0, row_hi, jnp.where(edge_row == 1, row - row_hi, 0.0)).astype(BF)
    gwk_b = gwk_ref[...].astype(BF)
    tensor = len(outs)
    rows = width // tensor
    mine = lax.axis_index("tensor")
    for k in range(tensor):
        piece = pl.ds(pl.multiple_of(lax.rem(mine + k, tensor) * rows, rows), rows)
        outs[k][0:rows] = gkf_ref[piece].astype(BF)
        part = adj_ref[piece, :width].astype(BF)
        blocks = [part[c * 16 : (c + 1) * 16] for c in range(rows // 16)] + [tail]
        blocks += [gwk_b[c * 16 : (c + 1) * 16] for c in range(half // 16)]
        outs[k][rows:] = jnp.zeros_like(outs[k][rows:])
        for c, block in enumerate(blocks):
            outs[k][rows:, c * width : (c + 1) * width] = block


def join_kernel(tensor, doc_ref, wq_ref, *refs):
    ins, (sum_ref, out_ref) = refs[:tensor], refs[tensor:]
    rows = sum_ref.shape[0]
    width = out_ref.shape[1]
    half = width // 2
    total = ins[0][...].astype(F32)
    for k in range(1, tensor):
        total = total + ins[k][...].astype(F32)
    sum_ref[...] = total[:rows]
    at = wq_ref.shape[0]
    out_ref[0:at] = wq_ref[...]
    pieces = [total[rows:, c * width : (c + 1) * width] for c in range(total.shape[1] // width)]
    parts = rows // 16
    out_ref[at : at + rows] = jnp.concatenate(pieces[:parts], axis=0).astype(BF)
    at += rows
    tail = pieces[parts]
    row = tail[0:1] + tail[1:2]
    row_hi = row.astype(BF).astype(F32)
    index = lax.broadcasted_iota(jnp.int32, (16, width), 0)
    code = (doc_ref[0] + 1).astype(F32)
    tail = jnp.where(index == 0, row_hi, jnp.where(index == 1, row - row_hi, code))
    out_ref[at : at + 16] = tail.astype(BF)
    at += 16
    gwk = jnp.concatenate(pieces[parts + 1 : parts + 1 + half // 16], axis=0)
    hi = gwk.astype(BF)
    out_ref[at : at + half] = hi
    out_ref[at + half : at + 2 * half] = (gwk - hi.astype(F32)).astype(BF)


def last_kernel(
    seq, back_scale,
    doc_ref, edge_ref, gath_ref, sum_ref, v_ref,
    kfg_ref, gwq_ref, gwk_ref,
    adj_ref, adjs_ref, col_ref,
):
    n, width = v_ref.shape
    heads, half = gwq_ref.shape[:2]
    rows = sum_ref.shape[0]
    me = lax.axis_index("seq")
    mine = lax.axis_index("tensor")
    last_code = (doc_ref[n - 1] + 1).astype(F32)
    edge = edge_ref[n - 1]

    def gathered(first, size):
        x = gath_ref[0, first : first + size].astype(F32)
        for d in range(1, seq):
            x = x + gath_ref[d, first : first + size].astype(F32)
        return x

    for h in range(heads):
        gwq_ref[h] = gathered(h * half, half)
    at = heads * half
    gwk_ref[...] = gathered(at + rows + 16, half) + gathered(at + rows + 16 + half, half)
    adj_ref[...] = jnp.zeros_like(adj_ref)
    adjs_ref[...] = jnp.zeros_like(adjs_ref)

    def later(s, carry):
        a = gath_ref[s, at : at + rows].astype(F32)
        t = gath_ref[s, at + rows : at + rows + 16].astype(F32)
        same = t[2:3] == last_code
        adj_ref[...] += jnp.where(same, a, 0.0)
        adjs_ref[...] += jnp.where(same, t[0:1] + t[1:2], 0.0)
        return carry

    lax.fori_loop(me + 1, jnp.minimum(me + REACH + 1, seq), later, 0)
    adj = adj_ref[...]
    a_hi = adj.astype(BF)
    a_lo = (adj - a_hi.astype(F32)).astype(BF)
    col_ref[...] = jnp.broadcast_to(adjs_ref[...], (width, width)).T
    col = col_ref[pl.ds(pl.multiple_of(mine * rows, rows), rows), 0:1]
    j = lax.broadcasted_iota(jnp.int32, (1, n), 1)
    more = mm(a_hi, v_ref[...], NT) + mm(a_lo, v_ref[...], NT) + col
    kfg_ref[...] = sum_ref[...] + jnp.where(j >= edge, more, 0.0) * back_scale


VM = pl.BlockSpec(memory_space=pltpu.VMEM)
SM = pl.BlockSpec(memory_space=pltpu.SMEM)
ANY = pl.BlockSpec(memory_space=pl.ANY)


def grant(mib):
    return pltpu.CompilerParams(vmem_limit_bytes=mib << 20)


def cost(flops, size):
    return pl.CostEstimate(flops=flops, bytes_accessed=size, transcendentals=0)


def shards(queries, keys, values, doc_ids, w_query, w_key):
    n, heads, width = queries.shape
    half = w_key.shape[1]
    seq = lax.axis_size("seq")
    tensor = lax.axis_size("tensor")
    scale = width ** (-0.5)
    everyone = range(seq)
    assert n // width <= 16 and n // width * 16 == width

    codes = (doc_ids + 1).astype(BF).reshape(n // width, width)
    codes = jnp.pad(codes, ((0, 16 - n // width), (0, 0)))
    pack = jnp.concatenate([keys, values, codes], axis=0)

    def hop(x, distance):
        return lax.ppermute(x, "seq", [(i, i + distance) for i in everyone if i + distance < seq])

    two = hop(pack, 2)
    own = lax.ppermute(pack, "seq", [(i, i + 1) for i in everyone if i % 2 == 0])

    qs = queries.reshape(n, heads * width)
    starts = jnp.sum((doc_ids[None, :] < doc_ids[:, None]).astype(jnp.int32), axis=1)
    start_row = starts.reshape(1, n)
    wq_t = jnp.transpose(w_query, (0, 2, 1))
    wk_t = w_key.T
    sds = jax.ShapeDtypeStruct
    cols = heads * n
    rows = width // tensor
    near = REACH // 2
    chains = heads * min(n, CHAINS * TC // heads) // TC
    square = sds((width, width), F32)
    wide = sds((width, cols), F32)
    flat = sds((8, cols), F32)
    scan = [
        pltpu.VMEM((chains, 8, TC), F32),
        pltpu.VMEM((chains, width, TC), F32),
        pltpu.VMEM((chains, TK, TC), F32),
        pltpu.VMEM((chains, 8, TC), F32),
    ]
    vt, acc, stat = pl.pallas_call(
        functools.partial(teacher_kernel, scale),
        out_shape=(sds((width, n), BF), wide, flat),
        in_specs=[VM] * 4,
        out_specs=[VM] * 3,
        compiler_params=grant(12),
        cost_estimate=cost(4 * n * n * width * heads, 4 << 20),
    )(qs, keys, values, start_row)
    four = hop(pack, 4)
    qf, kf, num, den = pl.pallas_call(
        student_kernel,
        out_shape=(wide, sds((width, n), F32), wide, flat),
        in_specs=[VM] * 6,
        out_specs=[VM] * 4,
        scratch_shapes=[pltpu.VMEM((n, width), BF)],
        compiler_params=grant(12),
        cost_estimate=cost(4 * n * n * width * heads, 4 << 20),
    )(qs, keys, vt, start_row, wq_t, wk_t)

    swap_two = lax.ppermute(two, "seq", [(i, i ^ 1) for i in everyone])
    acc, stat, near_kf, statet, csum = pl.pallas_call(
        functools.partial(window_kernel, scale),
        out_shape=(wide, flat, sds((width, near * n), F32), square, square),
        in_specs=[SM] + [VM] * 5 + [ANY] * 3,
        out_specs=[VM] * 5,
        scratch_shapes=[
            pltpu.VMEM((near * n, width), BF),
            pltpu.VMEM((near * n, width), BF),
            pltpu.VMEM((near, 16, width), BF),
            pltpu.VMEM((width, near * n), BF),
        ]
        + scan
        + [pltpu.SemaphoreType.DMA((near, 3))],
        compiler_params=grant(20),
        cost_estimate=cost(8 * n * n * width * heads, 4 << 20),
    )(doc_ids, qs, start_row, wk_t, acc, stat, own, two, swap_two)

    swap_four = lax.ppermute(four, "seq", [(i, i - 1) for i in everyone if i % 2 == 1])
    student, wq_part, *pieces = pl.pallas_call(
        functools.partial(main_kernel, scale, 2.0 / (n * seq), float(n * seq), tensor),
        out_shape=[sds((n, heads * width), BF), sds((heads * half, width), BF)]
        + [sds((rows + 16, n), BF)] * tensor,
        in_specs=[SM] + [VM] * 14 + [ANY] * 5,
        out_specs=[VM] * (2 + tensor),
        scratch_shapes=[
            pltpu.VMEM((near * n, width), BF),
            pltpu.VMEM((near * n, width), BF),
            pltpu.VMEM((near, 16, width), BF),
            pltpu.VMEM((2 * n, width), BF),
            pltpu.VMEM((2 * n, width), BF),
            pltpu.VMEM((2, 16, width), BF),
            pltpu.VMEM((width, 2 * n), F32),
            pltpu.VMEM((width, 2 * n), BF),
            pltpu.VMEM((heads, half, width), F32),
            pltpu.VMEM((half, width), F32),
            pltpu.VMEM((width, width + 16), F32),
            pltpu.VMEM((width, 128), F32),
            pltpu.VMEM((width, n), F32),
            pltpu.VMEM((n, width), F32),
            pltpu.VMEM((width, width), F32),
            pltpu.VMEM((width, width), F32),
            pltpu.VMEM((width, 128), F32),
            pltpu.VMEM((width, cols), F32),
            pltpu.VMEM((8, cols), F32),
        ]
        + scan
        + [pltpu.SemaphoreType.DMA((near, 3)), pltpu.SemaphoreType.DMA((2, 3))],
        compiler_params=grant(32),
        cost_estimate=cost(16 * n * n * width * heads, 8 << 20),
    )(
        doc_ids, qs, keys, values, start_row, wk_t,
        qf, kf, acc, num, stat, den, near_kf, statet, csum,
        two, four, own, swap_two, swap_four,
    )

    arrived = [pieces[0]]
    for k in range(1, tensor):
        arrived.append(
            lax.ppermute(pieces[k], "tensor", [(i, (i + k) % tensor) for i in range(tensor)])
        )
    packed = heads * half + rows + 16 + 2 * half
    part, out = pl.pallas_call(
        functools.partial(join_kernel, tensor),
        out_shape=(sds((rows, n), F32), sds((packed, width), BF)),
        in_specs=[SM] + [VM] * (tensor + 1),
        out_specs=[VM] * 2,
        compiler_params=grant(8),
        cost_estimate=cost(n * width, 1 << 20),
    )(doc_ids, wq_part, *arrived)
    gathered = lax.all_gather(out, "seq")
    key_grads, gwq, gwk = pl.pallas_call(
        functools.partial(last_kernel, seq, float(n * seq)),
        out_shape=(sds((rows, n), F32), sds((heads, half, width), F32), sds((half, width), F32)),
        in_specs=[SM, SM, VM, VM, VM],
        out_specs=[VM] * 3,
        scratch_shapes=[
            pltpu.VMEM((rows, width), F32),
            pltpu.VMEM((1, width), F32),
            pltpu.VMEM((width, width), F32),
        ],
        compiler_params=grant(12),
        cost_estimate=cost(4 * n * width * width, 2 << 20),
    )(doc_ids, starts, gathered, part, values)
    return student.reshape(n, heads, width), jnp.transpose(gwq, (0, 2, 1)), gwk.T, key_grads.T


def solution(mesh):
    placed = (
        P("seq", "tensor", None),
        P("seq", None),
        P("seq", None),
        P("seq"),
        P("tensor", None, None),
        P(),
    )

    return jax.shard_map(
        shards,
        mesh=mesh,
        in_specs=placed,
        out_specs=(P("seq", "tensor", None), P("tensor", None, None), P(), P("seq", "tensor")),
        check_vma=False,
    )
```

```python
import functools

import jax
import jax.numpy as jnp
from jax import lax
from jax.experimental import pallas as pl
from jax.experimental.pallas import tpu as pltpu
from jax.sharding import PartitionSpec as P


REACH = 4
NEG = -1e30
LOG2E = 1.4426950408889634
TQ = 256
TK = 1024
TC = 256
CH = 512
CHAINS = 4
BF = jnp.bfloat16
F32 = jnp.float32

NT = (((1,), (1,)), ((), ()))
NN = (((1,), (0,)), ((), ()))


def mm(a, b, dims=NN):
    return lax.dot_general(a, b, dims, preferred_element_type=F32)


def feature_t(logits):
    top = jnp.max(logits, axis=0, keepdims=True)
    low = jnp.min(logits, axis=0, keepdims=True)
    up = jnp.exp(logits - top)
    down = jnp.exp(low - logits)
    up = up * (1.0 / jnp.sum(up, axis=0, keepdims=True))
    down = down * (1.0 / jnp.sum(down, axis=0, keepdims=True))
    return jnp.concatenate([up, down], axis=0)


def feature_back_t(feat, grad):
    half = feat.shape[0] // 2
    p, m = feat[:half], feat[half:]
    a, b = grad[:half], grad[half:]
    return p * (a - jnp.sum(a * p, axis=0, keepdims=True)) - m * (
        b - jnp.sum(b * m, axis=0, keepdims=True)
    )


def allowed_t(limit, first, start):
    j = lax.broadcasted_iota(jnp.int32, (limit, TQ), 0)
    i = lax.broadcasted_iota(jnp.int32, (1, TQ), 1) + first
    return (j <= i) & (j >= start)


def transposed(x):
    return x.astype(F32).T


def teacher_kernel(scale, q_ref, k_ref, v_ref, start_ref, vt_ref, acc_ref, stat_ref):
    n, width = k_ref.shape
    heads = q_ref.shape[1] // width
    vt_ref[...] = transposed(v_ref[...]).astype(BF)

    def head(h, carry):
        lane = pl.multiple_of(h * width, width)
        for qt in range(n // TQ):
            first = qt * TQ
            limit = first + TQ
            col = pl.ds(pl.multiple_of(h * n + first, TQ), TQ)
            q = q_ref[first:limit, pl.ds(lane, width)]
            ok = allowed_t(limit, first, start_ref[:, first:limit])
            s = jnp.where(ok, mm(k_ref[:limit], q, NT), NEG)
            top = jnp.max(s, axis=0, keepdims=True)
            w = jnp.exp2((s - top) * (scale * LOG2E))
            stat_ref[0:1, col] = top
            stat_ref[1:2, col] = jnp.sum(w, axis=0, keepdims=True)
            acc_ref[:, col] = mm(vt_ref[:, :limit], w.astype(BF))
        return carry

    lax.fori_loop(0, heads, head, 0)


def student_kernel(
    q_ref, k_ref, vt_ref, start_ref, wq_ref, wk_ref, qf_ref, kf_ref, num_ref, den_ref, kfb_ref
):
    n, width = k_ref.shape
    heads = q_ref.shape[1] // width
    kf = feature_t(mm(wk_ref[...], k_ref[...], NT))
    kf_ref[...] = kf
    kfb_ref[...] = kf.T.astype(BF)

    def head(h, carry):
        lane = pl.multiple_of(h * width, width)
        for qt in range(n // TQ):
            first = qt * TQ
            limit = first + TQ
            col = pl.ds(pl.multiple_of(h * n + first, TQ), TQ)
            q = q_ref[first:limit, pl.ds(lane, width)]
            ok = allowed_t(limit, first, start_ref[:, first:limit])
            qf = feature_t(mm(wq_ref[h], q, NT))
            qf_ref[:, col] = qf
            pr = jnp.where(ok, mm(kfb_ref[:limit], qf.astype(BF)), 0.0)
            den_ref[0:1, col] = jnp.sum(pr, axis=0, keepdims=True)
            num_ref[:, col] = mm(vt_ref[:, :limit], pr.astype(BF))
        return carry

    lax.fori_loop(0, heads, head, 0)


def load(src, slot, keys, values, codes, sem):
    n = keys.shape[0] // codes.shape[0]
    return (
        pltpu.make_async_copy(src.at[0:n], keys.at[slot * n : (slot + 1) * n], sem.at[slot, 0]),
        pltpu.make_async_copy(src.at[n : 2 * n], values.at[slot * n : (slot + 1) * n], sem.at[slot, 1]),
        pltpu.make_async_copy(src.at[2 * n : 2 * n + 16], codes.at[slot], sem.at[slot, 2]),
    )


def begin(copies):
    for c in copies:
        c.start()


def finish(copies):
    for c in copies:
        c.wait()


def matching(codes, code):
    return jnp.sum((codes[...].astype(F32) == code).astype(jnp.int32))


def window_part(
    scale, n, heads, begin_key, stop_key, lead_rows,
    q_ref, wk_ref, wink, winv, wkf, wvt, statet_ref, csum_ref,
    acc_ref, st2_ref, run_ref, racc_ref, sbuf_ref, smax_ref, bias_ref,
):
    width = wink.shape[1]
    tile0 = begin_key // TK
    tiles = stop_key // TK
    cut = jnp.minimum(begin_key - tile0 * TK, 1)

    @pl.when(begin_key < stop_key)
    def _():
        def prepare(kt, carry):
            row = pl.ds(pl.multiple_of(kt * TK, TK), TK)
            kf = feature_t(mm(wk_ref[...], wink[row], NT))
            wkf[:, row] = kf
            j = lax.broadcasted_iota(jnp.int32, (1, TK), 1) + kt * TK
            kfm = jnp.where(j >= begin_key, kf, 0.0).astype(BF)
            vt = transposed(winv[row]).astype(BF)
            wvt[:, row] = vt
            statet_ref[...] += mm(vt, kfm, NT)
            part = kfm.astype(F32)
            for c in range(TK // 128):
                csum_ref[...] += part[:, c * 128 : (c + 1) * 128]
            return carry

        lax.fori_loop(tile0, tiles, prepare, 0)
        key = lax.broadcasted_iota(jnp.int32, bias_ref.shape, 0) + tile0 * TK
        bias_ref[...] = jnp.where(key >= begin_key, 0.0, NEG)
        wq = min(n, CHAINS * TC // heads)
        chains = [(h, c) for h in range(heads) for c in range(wq // TC)]
        factor = scale * LOG2E

        def qtile(qt, carry):
            first = pl.multiple_of(qt * wq, wq)

            def column(h, c):
                return pl.ds(pl.multiple_of(h * n + first + c * TC, TC), TC)

            for x, (h, c) in enumerate(chains):
                col = column(h, c)
                run_ref[x, 0:1] = st2_ref[0:1, col]
                run_ref[x, 1:2] = st2_ref[1:2, col]
                racc_ref[x] = acc_ref[:, col]

            def scores(x, kt, part, masked):
                h, c = chains[x]
                q = q_ref[pl.ds(first + c * TC, TC), h * width : (h + 1) * width]
                row = pl.multiple_of(kt * TK + part * CH, CH)
                s = mm(wink[pl.ds(row, CH)], q, NT)
                if masked:
                    bias = bias_ref[part * CH : (part + 1) * CH]
                    s = s + jnp.concatenate([bias] * (TC // 128), axis=1)
                sbuf_ref[x, part * CH : (part + 1) * CH] = s
                return jnp.max(s.reshape(CH // 8, 8, TC), axis=0)

            def stage(cur, kt, nxt, kt_nxt, masked):
                old = run_ref[cur, 0:1]
                new = jnp.maximum(old, jnp.max(smax_ref[cur], axis=0, keepdims=True))
                tops, sums, parts = [], [], []
                for part in range(TK // CH):
                    tops.append(scores(nxt, kt_nxt, part, masked))
                    w = jnp.exp2((sbuf_ref[cur, part * CH : (part + 1) * CH] - new) * factor)
                    sums.append(jnp.sum(w.reshape(CH // 8, 8, TC), axis=0))
                    parts.append(w.astype(BF))
                smax_ref[nxt] = functools.reduce(jnp.maximum, tops)
                f = jnp.exp2((old - new) * factor)
                total_w = jnp.sum(functools.reduce(jnp.add, sums), axis=0, keepdims=True)
                run_ref[cur, 0:1] = new
                run_ref[cur, 1:2] = run_ref[cur, 1:2] * f + total_w
                row = pl.ds(pl.multiple_of(kt * TK, TK), TK)
                racc_ref[cur] = racc_ref[cur] * f + mm(
                    wvt[:, row], jnp.concatenate(parts, axis=0)
                )

            def sweep(kt, masked):
                for x in range(len(chains) - 1):
                    stage(x, kt, x + 1, kt, masked)
                stage(len(chains) - 1, kt, 0, jnp.minimum(kt + 1, tiles - 1), False)

            def prime(masked):
                smax_ref[0] = functools.reduce(
                    jnp.maximum, [scores(0, tile0, part, masked) for part in range(TK // CH)]
                )

            @pl.when(cut > 0)
            def _():
                prime(True)
                sweep(tile0, True)

            @pl.when(cut == 0)
            def _():
                prime(False)


            def step(kt, carry):
                sweep(kt, False)
                return carry

            lax.fori_loop(tile0 + cut, tiles, step, 0)
            i = lax.broadcasted_iota(jnp.int32, (1, wq), 1) + first
            live = i < lead_rows
            for x, (h, c) in enumerate(chains):
                col = column(h, c)
                ok = live[:, c * TC : (c + 1) * TC]
                st2_ref[0:2, col] = jnp.where(ok, run_ref[x, 0:2], st2_ref[0:2, col])
                acc_ref[:, col] = jnp.where(ok, racc_ref[x], acc_ref[:, col])
            return carry

        lax.fori_loop(0, (lead_rows + wq - 1) // wq, qtile, 0)


def window_kernel(
    scale,
    doc_ref, q_ref, start_ref, wk_ref, acc_in, stat_in, own_ref, two_ref, swap_two_ref,
    acc_ref, st2_ref, wkf, statet_ref, csum_ref,
    wink, winv, wcode, wvt, run_ref, racc_ref, sbuf_ref, smax_ref, bias_ref, sem,
):
    width = wk_ref.shape[1]
    n = start_ref.shape[1]
    heads = q_ref.shape[1] // width
    odd = lax.rem(lax.axis_index("seq"), 2)
    begin(load(two_ref, 0, wink, winv, wcode, sem))

    @pl.when(odd == 0)
    def _():
        begin(load(swap_two_ref, 1, wink, winv, wcode, sem))

    @pl.when(odd == 1)
    def _():
        begin(load(own_ref, 1, wink, winv, wcode, sem))

    acc_ref[...] = acc_in[...]
    st2_ref[...] = stat_in[...]
    statet_ref[...] = jnp.zeros_like(statet_ref)
    csum_ref[...] = jnp.zeros_like(csum_ref)
    lead_code = (doc_ref[0] + 1).astype(F32)
    lead_rows = jnp.sum((start_ref[...] == 0).astype(jnp.int32))
    finish(load(two_ref, 0, wink, winv, wcode, sem))
    finish(load(two_ref, 1, wink, winv, wcode, sem))

    stop_key = wink.shape[0]
    window_part(
        scale, n, heads, stop_key - matching(wcode, lead_code), stop_key, lead_rows,
        q_ref, wk_ref, wink, winv, wkf, wvt, statet_ref, csum_ref,
        acc_ref, st2_ref, run_ref, racc_ref, sbuf_ref, smax_ref, bias_ref,
    )


def main_kernel(
    scale, grad_scale, back_scale, tensor_size,
    doc_ref, q_ref, k_ref, v_ref, start_ref, wk_ref,
    qf_ref, kf_ref, acc_in, num_ref, stat_in, den_ref, near_kf, statet_in, csum_in,
    two_ref, four_ref, own_ref, swap_two_ref, swap_four_ref,
    stu_ref, wq_ref, *rest,
):
    outs = rest[:tensor_size]
    (
        neark, nearv, nearc, wink, winv, wcode, wkf, wvt,
        gwq_ref, gwk_ref, adj_ref, adjs_ref, gkf_ref, gkf2_ref,
        state_ref, statet_ref, csum_ref, acc_ref, st2_ref, run_ref, racc_ref, sbuf_ref, smax_ref,
        bias_ref, near_sem, sem,
    ) = rest[tensor_size:]
    n, width = k_ref.shape
    heads = q_ref.shape[1] // width
    half = wk_ref.shape[0]
    odd = lax.rem(lax.axis_index("seq"), 2)
    begin(load(four_ref, 0, wink, winv, wcode, sem))
    begin(load(two_ref, 0, neark, nearv, nearc, near_sem))

    @pl.when(odd == 0)
    def _():
        begin(load(swap_four_ref, 1, wink, winv, wcode, sem))
        begin(load(swap_two_ref, 1, neark, nearv, nearc, near_sem))

    @pl.when(odd == 1)
    def _():
        begin(load(swap_two_ref, 1, wink, winv, wcode, sem))
        begin(load(own_ref, 1, neark, nearv, nearc, near_sem))

    gkf2_ref[...] = jnp.zeros_like(gkf2_ref)
    gwq_ref[...] = jnp.zeros_like(gwq_ref)
    gwk_ref[...] = jnp.zeros_like(gwk_ref)
    adj_ref[...] = jnp.zeros_like(adj_ref)
    statet_ref[...] = statet_in[...]
    csum_ref[...] = csum_in[...]
    acc_ref[...] = acc_in[...]
    st2_ref[...] = stat_in[...]
    lead_code = (doc_ref[0] + 1).astype(F32)
    lead_rows = jnp.sum((start_ref[...] == 0).astype(jnp.int32))
    for slot in range(2):
        finish(load(four_ref, slot, wink, winv, wcode, sem))
        finish(load(two_ref, slot, neark, nearv, nearc, near_sem)[2:])

    near_stop = neark.shape[0]
    near_begin = near_stop - matching(nearc, lead_code)
    far_stop = wink.shape[0]
    far_begin = far_stop - matching(wcode, lead_code)
    linked = near_begin < near_stop
    window_part(
        scale, n, heads, far_begin, far_stop, lead_rows,
        q_ref, wk_ref, wink, winv, wkf, wvt, statet_ref, csum_ref,
        acc_ref, st2_ref, run_ref, racc_ref, sbuf_ref, smax_ref, bias_ref,
    )
    state_ref[...] = statet_ref[...].T
    csum_ref[...] = jnp.broadcast_to(
        jnp.sum(csum_ref[...], axis=1, keepdims=True), csum_ref.shape
    )

    link = linked.astype(F32)
    pad = lax.broadcasted_iota(jnp.int32, (n, 16), 1)
    v_aug = jnp.concatenate([v_ref[...], (pad < 2).astype(F32).astype(BF)], axis=1)
    statet_b = statet_ref[...].astype(BF)
    csum_b = csum_ref[:, :16].astype(BF)
    csum_b = jnp.where(pad[:width] < 2, csum_b.astype(F32), 0.0).astype(BF)
    state_aug = jnp.concatenate([state_ref[...].astype(BF), csum_b], axis=1)
    csum_row = jnp.sum(jnp.where(lax.broadcasted_iota(jnp.int32, csum_ref.shape, 1) == 0, csum_ref[...], 0.0).T, axis=0, keepdims=True)
    edge_row = lax.broadcasted_iota(jnp.int32, (16, width), 0)
    csum_hi = csum_row.astype(BF).astype(F32)
    csum_rows = jnp.where(edge_row == 0, csum_hi, jnp.where(edge_row == 1, csum_row - csum_hi, 0.0))
    statet_aug = jnp.concatenate([statet_b, csum_rows.astype(BF)], axis=0)
    kft_b = kf_ref[...].astype(BF)
    steps = [(qt, h) for qt in range(n // TQ) for h in range(heads)]
    held = {}

    def before(t):
        qt, h = steps[t]
        first = qt * TQ
        limit = first + TQ
        col = slice(h * n + first, h * n + limit)
        r = (start_ref[:, first:limit] == 0).astype(F32) * link
        qf = qf_ref[:, col]
        qf_b = qf.astype(BF)
        qf_r = (qf * r).astype(BF)
        carried = mm(statet_aug, qf_r)
        teacher = acc_ref[:, col] * (1.0 / st2_ref[1:2, col])
        inv = 1.0 / (den_ref[0:1, col] + carried[width : width + 1] + carried[width + 1 : width + 2])
        est = (num_ref[:, col] + carried[:width]) * inv
        stu_ref[first:limit, h * width : (h + 1) * width] = est.T.astype(BF)
        diff = est - teacher
        inv = inv * grad_scale
        gd = -jnp.sum(diff * est, axis=0, keepdims=True) * inv
        gd_hi = gd.astype(BF).astype(F32)
        row = lax.broadcasted_iota(jnp.int32, (16, TQ), 0)
        gd_rows = jnp.where(row == 0, gd_hi, jnp.where(row == 1, gd - gd_hi, 0.0))
        gn = diff * inv
        g = jnp.concatenate([gn.astype(BF), gd_rows.astype(BF)], axis=0)
        g_r = jnp.concatenate([(gn * r).astype(BF), (gd_rows * r).astype(BF)], axis=0)
        held[t] = (first, limit, h, qf_b, qf_r, g, g_r)

    def second_product(t):
        first, limit, h, qf_b, qf_r, g, g_r = held[t]
        start = start_ref[:, first:limit]
        i = lax.broadcasted_iota(jnp.int32, (1, TQ), 1) + first
        parts = []
        for at in range(0, limit, TQ):
            j = lax.broadcasted_iota(jnp.int32, (TQ, TQ), 0) + at
            ok = j >= start
            if at == first:
                ok = ok & (j <= i)
            parts.append(jnp.where(ok, mm(v_aug[at : at + TQ], g), 0.0).astype(BF))
        gp = jnp.concatenate(parts, axis=0)
        gkf2_ref[:limit] += mm(gp, qf_b, NT)
        adj_ref[...] += mm(qf_r, g, NT)
        held[t] = (first, limit, h, mm(jnp.concatenate([kft_b[:, :limit], state_aug], axis=1), jnp.concatenate([gp, g_r], axis=0)))

    def after(t):
        first, limit, h, gq = held.pop(t)
        col = slice(h * n + first, h * n + limit)
        ga = feature_back_t(qf_ref[:, col], gq).astype(BF)
        gwq_ref[h] += mm(ga, q_ref[first:limit, h * width : (h + 1) * width])

    count = len(steps)
    before(0)
    for t in range(count):
        if t + 1 < count:
            before(t + 1)
        second_product(t)
        if t:
            after(t - 1)
    after(count - 1)

    gkf = gkf2_ref[...].T
    gkf_ref[...] = gkf * back_scale
    gl = feature_back_t(kf_ref[...], gkf).astype(BF)
    gwk_ref[...] += mm(gl, k_ref[...])
    adj_b = adj_ref[:, :width].astype(BF)
    adjs_col = adj_ref[:, width : width + 1] + adj_ref[:, width + 1 : width + 2]

    def back_over(begin_key, stop_key, keys, values, feats):
        def back(kt, carry):
            row = pl.ds(pl.multiple_of(kt * TK, TK), TK)
            more = mm(adj_b, values[row], NT) + adjs_col
            j = lax.broadcasted_iota(jnp.int32, (1, TK), 1) + kt * TK
            gl = feature_back_t(feats[:, row], more)
            gl = jnp.where(j >= begin_key, gl, 0.0).astype(BF)
            gwk_ref[...] += mm(gl, keys[row])
            return carry

        lax.fori_loop(begin_key // TK, stop_key // TK, back, 0)

    for slot in range(2):
        finish(load(two_ref, slot, neark, nearv, nearc, near_sem)[:2])
    back_over(near_begin, near_stop, neark, nearv, near_kf)
    back_over(far_begin, far_stop, wink, winv, wkf)

    for h in range(heads):
        wq_ref[h * half : (h + 1) * half] = gwq_ref[h].astype(BF)
    adjs_ref[...] = jnp.broadcast_to(adjs_col, adjs_ref.shape)
    row = jnp.max(adjs_ref[...].T, axis=0, keepdims=True)
    row_hi = row.astype(BF).astype(F32)
    tail = jnp.where(edge_row == 0, row_hi, jnp.where(edge_row == 1, row - row_hi, 0.0)).astype(BF)
    gwk_b = gwk_ref[...].astype(BF)
    tensor = len(outs)
    rows = width // tensor
    mine = lax.axis_index("tensor")
    for k in range(tensor):
        piece = pl.ds(pl.multiple_of(lax.rem(mine + k, tensor) * rows, rows), rows)
        outs[k][0:rows] = gkf_ref[piece].astype(BF)
        part = adj_ref[piece, :width].astype(BF)
        blocks = [part[c * 16 : (c + 1) * 16] for c in range(rows // 16)] + [tail]
        blocks += [gwk_b[c * 16 : (c + 1) * 16] for c in range(half // 16)]
        outs[k][rows:] = jnp.zeros_like(outs[k][rows:])
        for c, block in enumerate(blocks):
            outs[k][rows:, c * width : (c + 1) * width] = block


def join_kernel(tensor, doc_ref, wq_ref, *refs):
    ins, (sum_ref, out_ref) = refs[:tensor], refs[tensor:]
    rows = sum_ref.shape[0]
    width = out_ref.shape[1]
    half = width // 2
    total = ins[0][...].astype(F32)
    for k in range(1, tensor):
        total = total + ins[k][...].astype(F32)
    sum_ref[...] = total[:rows]
    at = wq_ref.shape[0]
    out_ref[0:at] = wq_ref[...]
    pieces = [total[rows:, c * width : (c + 1) * width] for c in range(total.shape[1] // width)]
    parts = rows // 16
    out_ref[at : at + rows] = jnp.concatenate(pieces[:parts], axis=0).astype(BF)
    at += rows
    tail = pieces[parts]
    row = tail[0:1] + tail[1:2]
    row_hi = row.astype(BF).astype(F32)
    index = lax.broadcasted_iota(jnp.int32, (16, width), 0)
    code = (doc_ref[0] + 1).astype(F32)
    tail = jnp.where(index == 0, row_hi, jnp.where(index == 1, row - row_hi, code))
    out_ref[at : at + 16] = tail.astype(BF)
    at += 16
    gwk = jnp.concatenate(pieces[parts + 1 : parts + 1 + half // 16], axis=0)
    hi = gwk.astype(BF)
    out_ref[at : at + half] = hi
    out_ref[at + half : at + 2 * half] = (gwk - hi.astype(F32)).astype(BF)


def last_kernel(
    seq, back_scale,
    doc_ref, edge_ref, gath_ref, sum_ref, v_ref,
    kfg_ref, gwq_ref, gwk_ref,
    adj_ref, adjs_ref, col_ref,
):
    n, width = v_ref.shape
    heads, half = gwq_ref.shape[:2]
    rows = sum_ref.shape[0]
    me = lax.axis_index("seq")
    mine = lax.axis_index("tensor")
    last_code = (doc_ref[n - 1] + 1).astype(F32)
    edge = edge_ref[n - 1]

    def gathered(first, size):
        x = gath_ref[0, first : first + size].astype(F32)
        for d in range(1, seq):
            x = x + gath_ref[d, first : first + size].astype(F32)
        return x

    for h in range(heads):
        gwq_ref[h] = gathered(h * half, half)
    at = heads * half
    gwk_ref[...] = gathered(at + rows + 16, half) + gathered(at + rows + 16 + half, half)
    adj_ref[...] = jnp.zeros_like(adj_ref)
    adjs_ref[...] = jnp.zeros_like(adjs_ref)

    def later(s, carry):
        a = gath_ref[s, at : at + rows].astype(F32)
        t = gath_ref[s, at + rows : at + rows + 16].astype(F32)
        same = t[2:3] == last_code
        adj_ref[...] += jnp.where(same, a, 0.0)
        adjs_ref[...] += jnp.where(same, t[0:1] + t[1:2], 0.0)
        return carry

    lax.fori_loop(me + 1, jnp.minimum(me + REACH + 1, seq), later, 0)
    adj = adj_ref[...]
    a_hi = adj.astype(BF)
    a_lo = (adj - a_hi.astype(F32)).astype(BF)
    col_ref[...] = jnp.broadcast_to(adjs_ref[...], (width, width)).T
    col = col_ref[pl.ds(pl.multiple_of(mine * rows, rows), rows), 0:1]
    j = lax.broadcasted_iota(jnp.int32, (1, n), 1)
    more = mm(a_hi, v_ref[...], NT) + mm(a_lo, v_ref[...], NT) + col
    kfg_ref[...] = sum_ref[...] + jnp.where(j >= edge, more, 0.0) * back_scale


VM = pl.BlockSpec(memory_space=pltpu.VMEM)
SM = pl.BlockSpec(memory_space=pltpu.SMEM)
ANY = pl.BlockSpec(memory_space=pl.ANY)


def grant(mib):
    return pltpu.CompilerParams(vmem_limit_bytes=mib << 20)


def cost(flops, size):
    return pl.CostEstimate(flops=flops, bytes_accessed=size, transcendentals=0)


def shards(queries, keys, values, doc_ids, w_query, w_key):
    n, heads, width = queries.shape
    half = w_key.shape[1]
    seq = lax.axis_size("seq")
    tensor = lax.axis_size("tensor")
    scale = width ** (-0.5)
    everyone = range(seq)
    assert n // width <= 16 and n // width * 16 == width

    codes = (doc_ids.reshape(n // width, width) + 1).astype(BF)
    codes = jnp.pad(codes, ((0, 16 - n // width), (0, 0)))
    pack = jnp.concatenate([keys, values, codes], axis=0)

    def hop(x, distance):
        return lax.ppermute(x, "seq", [(i, i + distance) for i in everyone if i + distance < seq])

    two = hop(pack, 2)
    own = lax.ppermute(pack, "seq", [(i, i + 1) for i in everyone if i % 2 == 0])

    qs = queries.reshape(n, heads * width)
    starts = jnp.sum((doc_ids[None, :] < doc_ids[:, None]).astype(jnp.int32), axis=1)
    start_row = starts.reshape(1, n)
    wq_t = jnp.transpose(w_query, (0, 2, 1))
    wk_t = w_key.T
    sds = jax.ShapeDtypeStruct
    cols = heads * n
    rows = width // tensor
    near = REACH // 2
    chains = heads * min(n, CHAINS * TC // heads) // TC
    square = sds((width, width), F32)
    wide = sds((width, cols), F32)
    flat = sds((8, cols), F32)
    scan = [
        pltpu.VMEM((chains, 8, TC), F32),
        pltpu.VMEM((chains, width, TC), F32),
        pltpu.VMEM((chains, TK, TC), F32),
        pltpu.VMEM((chains, 8, TC), F32),
        pltpu.VMEM((TK, 128), F32),
    ]
    vt, acc, stat = pl.pallas_call(
        functools.partial(teacher_kernel, scale),
        out_shape=(sds((width, n), BF), wide, flat),
        in_specs=[VM] * 4,
        out_specs=[VM] * 3,
        compiler_params=grant(12),
        cost_estimate=cost(4 * n * n * width * heads, 4 << 20),
    )(qs, keys, values, start_row)
    four = hop(pack, 4)
    qf, kf, num, den = pl.pallas_call(
        student_kernel,
        out_shape=(wide, sds((width, n), F32), wide, flat),
        in_specs=[VM] * 6,
        out_specs=[VM] * 4,
        scratch_shapes=[pltpu.VMEM((n, width), BF)],
        compiler_params=grant(12),
        cost_estimate=cost(4 * n * n * width * heads, 4 << 20),
    )(qs, keys, vt, start_row, wq_t, wk_t)

    swap_two = lax.ppermute(two, "seq", [(i, i ^ 1) for i in everyone])
    acc, stat, near_kf, statet, csum = pl.pallas_call(
        functools.partial(window_kernel, scale),
        out_shape=(wide, flat, sds((width, near * n), F32), square, square),
        in_specs=[SM] + [VM] * 5 + [ANY] * 3,
        out_specs=[VM] * 5,
        scratch_shapes=[
            pltpu.VMEM((near * n, width), BF),
            pltpu.VMEM((near * n, width), BF),
            pltpu.VMEM((near, 16, width), BF),
            pltpu.VMEM((width, near * n), BF),
        ]
        + scan
        + [pltpu.SemaphoreType.DMA((near, 3))],
        compiler_params=grant(20),
        cost_estimate=cost(8 * n * n * width * heads, 4 << 20),
    )(doc_ids, qs, start_row, wk_t, acc, stat, own, two, swap_two)

    swap_four = lax.ppermute(four, "seq", [(i, i - 1) for i in everyone if i % 2 == 1])
    student, wq_part, *pieces = pl.pallas_call(
        functools.partial(main_kernel, scale, 2.0 / (n * seq), float(n * seq), tensor),
        out_shape=[sds((n, heads * width), BF), sds((heads * half, width), BF)]
        + [sds((rows + 16, n), BF)] * tensor,
        in_specs=[SM] + [VM] * 14 + [ANY] * 5,
        out_specs=[VM] * (2 + tensor),
        scratch_shapes=[
            pltpu.VMEM((near * n, width), BF),
            pltpu.VMEM((near * n, width), BF),
            pltpu.VMEM((near, 16, width), BF),
            pltpu.VMEM((2 * n, width), BF),
            pltpu.VMEM((2 * n, width), BF),
            pltpu.VMEM((2, 16, width), BF),
            pltpu.VMEM((width, 2 * n), F32),
            pltpu.VMEM((width, 2 * n), BF),
            pltpu.VMEM((heads, half, width), F32),
            pltpu.VMEM((half, width), F32),
            pltpu.VMEM((width, width + 16), F32),
            pltpu.VMEM((width, 128), F32),
            pltpu.VMEM((width, n), F32),
            pltpu.VMEM((n, width), F32),
            pltpu.VMEM((width, width), F32),
            pltpu.VMEM((width, width), F32),
            pltpu.VMEM((width, 128), F32),
            pltpu.VMEM((width, cols), F32),
            pltpu.VMEM((8, cols), F32),
        ]
        + scan
        + [pltpu.SemaphoreType.DMA((near, 3)), pltpu.SemaphoreType.DMA((2, 3))],
        compiler_params=grant(32),
        cost_estimate=cost(16 * n * n * width * heads, 8 << 20),
    )(
        doc_ids, qs, keys, values, start_row, wk_t,
        qf, kf, acc, num, stat, den, near_kf, statet, csum,
        two, four, own, swap_two, swap_four,
    )

    arrived = [pieces[0]]
    for k in range(1, tensor):
        arrived.append(
            lax.ppermute(pieces[k], "tensor", [(i, (i + k) % tensor) for i in range(tensor)])
        )
    packed = heads * half + rows + 16 + 2 * half
    part, out = pl.pallas_call(
        functools.partial(join_kernel, tensor),
        out_shape=(sds((rows, n), F32), sds((packed, width), BF)),
        in_specs=[SM] + [VM] * (tensor + 1),
        out_specs=[VM] * 2,
        compiler_params=grant(8),
        cost_estimate=cost(n * width, 1 << 20),
    )(doc_ids, wq_part, *arrived)
    gathered = lax.all_gather(out, "seq")
    key_grads, gwq, gwk = pl.pallas_call(
        functools.partial(last_kernel, seq, float(n * seq)),
        out_shape=(sds((rows, n), F32), sds((heads, half, width), F32), sds((half, width), F32)),
        in_specs=[SM, SM, VM, VM, VM],
        out_specs=[VM] * 3,
        scratch_shapes=[
            pltpu.VMEM((rows, width), F32),
            pltpu.VMEM((1, width), F32),
            pltpu.VMEM((width, width), F32),
        ],
        compiler_params=grant(12),
        cost_estimate=cost(4 * n * width * width, 2 << 20),
    )(doc_ids, starts, gathered, part, values)
    return student.reshape(n, heads, width), jnp.transpose(gwq, (0, 2, 1)), gwk.T, key_grads.T


def solution(mesh):
    placed = (
        P("seq", "tensor", None),
        P("seq", None),
        P("seq", None),
        P("seq"),
        P("tensor", None, None),
        P(),
    )

    return jax.shard_map(
        shards,
        mesh=mesh,
        in_specs=placed,
        out_specs=(P("seq", "tensor", None), P("tensor", None, None), P(), P("seq", "tensor")),
        check_vma=False,
    )
```

```python
import functools

import jax
import jax.numpy as jnp
from jax import lax
from jax.experimental import pallas as pl
from jax.experimental.pallas import tpu as pltpu
from jax.sharding import PartitionSpec as P


REACH = 4
NEG = -1e30
LOG2E = 1.4426950408889634
TQ = 256
TK = 1024
TC = 256
CH = 512
CHAINS = 4
BF = jnp.bfloat16
F32 = jnp.float32

NT = (((1,), (1,)), ((), ()))
NN = (((1,), (0,)), ((), ()))


def mm(a, b, dims=NN):
    return lax.dot_general(a, b, dims, preferred_element_type=F32)


def feature_t(logits):
    top = jnp.max(logits, axis=0, keepdims=True)
    low = jnp.min(logits, axis=0, keepdims=True)
    up = jnp.exp(logits - top)
    down = jnp.exp(low - logits)
    up = up * (1.0 / jnp.sum(up, axis=0, keepdims=True))
    down = down * (1.0 / jnp.sum(down, axis=0, keepdims=True))
    return jnp.concatenate([up, down], axis=0)


def feature_back_t(feat, grad):
    half = feat.shape[0] // 2
    p, m = feat[:half], feat[half:]
    a, b = grad[:half], grad[half:]
    return p * (a - jnp.sum(a * p, axis=0, keepdims=True)) - m * (
        b - jnp.sum(b * m, axis=0, keepdims=True)
    )


def allowed_t(limit, first, start):
    j = lax.broadcasted_iota(jnp.int32, (limit, TQ), 0)
    i = lax.broadcasted_iota(jnp.int32, (1, TQ), 1) + first
    return (j <= i) & (j >= start)


def transposed(x):
    return x.astype(F32).T


def teacher_kernel(scale, q_ref, k_ref, v_ref, start_ref, vt_ref, acc_ref, stat_ref):
    n, width = k_ref.shape
    heads = q_ref.shape[1] // width
    vt_ref[...] = transposed(v_ref[...]).astype(BF)

    def head(h, carry):
        lane = pl.multiple_of(h * width, width)
        for qt in range(n // TQ):
            first = qt * TQ
            limit = first + TQ
            col = pl.ds(pl.multiple_of(h * n + first, TQ), TQ)
            q = q_ref[first:limit, pl.ds(lane, width)]
            ok = allowed_t(limit, first, start_ref[:, first:limit])
            s = jnp.where(ok, mm(k_ref[:limit], q, NT), NEG)
            top = jnp.max(s, axis=0, keepdims=True)
            w = jnp.exp2((s - top) * (scale * LOG2E))
            stat_ref[0:1, col] = top
            stat_ref[1:2, col] = jnp.sum(w, axis=0, keepdims=True)
            acc_ref[:, col] = mm(vt_ref[:, :limit], w.astype(BF))
        return carry

    lax.fori_loop(0, heads, head, 0)


def student_kernel(
    q_ref, k_ref, vt_ref, start_ref, wq_ref, wk_ref, qf_ref, kf_ref, num_ref, den_ref, kfb_ref
):
    n, width = k_ref.shape
    heads = q_ref.shape[1] // width
    kf = feature_t(mm(wk_ref[...], k_ref[...], NT))
    kf_ref[...] = kf
    kfb_ref[...] = kf.T.astype(BF)

    def head(h, carry):
        lane = pl.multiple_of(h * width, width)
        for qt in range(n // TQ):
            first = qt * TQ
            limit = first + TQ
            col = pl.ds(pl.multiple_of(h * n + first, TQ), TQ)
            q = q_ref[first:limit, pl.ds(lane, width)]
            ok = allowed_t(limit, first, start_ref[:, first:limit])
            qf = feature_t(mm(wq_ref[h], q, NT))
            qf_ref[:, col] = qf
            pr = jnp.where(ok, mm(kfb_ref[:limit], qf.astype(BF)), 0.0)
            den_ref[0:1, col] = jnp.sum(pr, axis=0, keepdims=True)
            num_ref[:, col] = mm(vt_ref[:, :limit], pr.astype(BF))
        return carry

    lax.fori_loop(0, heads, head, 0)


def load(src, slot, keys, values, codes, sem):
    n = keys.shape[0] // codes.shape[0]
    return (
        pltpu.make_async_copy(src.at[0:n], keys.at[slot * n : (slot + 1) * n], sem.at[slot, 0]),
        pltpu.make_async_copy(src.at[n : 2 * n], values.at[slot * n : (slot + 1) * n], sem.at[slot, 1]),
        pltpu.make_async_copy(src.at[2 * n : 2 * n + 16], codes.at[slot], sem.at[slot, 2]),
    )


def begin(copies):
    for c in copies:
        c.start()


def finish(copies):
    for c in copies:
        c.wait()


def matching(codes, code):
    return jnp.sum((codes[...].astype(F32) == code).astype(jnp.int32))


def window_part(
    scale, n, heads, begin_key, stop_key, lead_rows,
    q_ref, wk_ref, wink, winv, wkf, wvt, statet_ref, csum_ref,
    acc_ref, st2_ref, run_ref, racc_ref, sbuf_ref, smax_ref, bias_ref,
):
    width = wink.shape[1]
    tile0 = begin_key // TK
    tiles = stop_key // TK
    cut = jnp.minimum(begin_key - tile0 * TK, 1)

    @pl.when(begin_key < stop_key)
    def _():
        def prepare(kt, carry):
            row = pl.ds(pl.multiple_of(kt * TK, TK), TK)
            kf = feature_t(mm(wk_ref[...], wink[row], NT))
            wkf[:, row] = kf
            j = lax.broadcasted_iota(jnp.int32, (1, TK), 1) + kt * TK
            kfm = jnp.where(j >= begin_key, kf, 0.0).astype(BF)
            vt = transposed(winv[row]).astype(BF)
            wvt[:, row] = vt
            statet_ref[...] += mm(vt, kfm, NT)
            part = kfm.astype(F32)
            for c in range(TK // 128):
                csum_ref[...] += part[:, c * 128 : (c + 1) * 128]
            return carry

        lax.fori_loop(tile0, tiles, prepare, 0)
        key = lax.broadcasted_iota(jnp.int32, bias_ref.shape, 0) + tile0 * TK
        bias_ref[...] = jnp.where(key >= begin_key, 0.0, NEG)
        wq = min(n, CHAINS * TC // heads)
        chains = [(h, c) for h in range(heads) for c in range(wq // TC)]
        factor = scale * LOG2E

        def qtile(qt, carry):
            first = pl.multiple_of(qt * wq, wq)

            def column(h, c):
                return pl.ds(pl.multiple_of(h * n + first + c * TC, TC), TC)

            for x, (h, c) in enumerate(chains):
                col = column(h, c)
                run_ref[x, 0:1] = st2_ref[0:1, col]
                run_ref[x, 1:2] = st2_ref[1:2, col]
                racc_ref[x] = acc_ref[:, col]

            def scores(x, base, kt, part, masked):
                h, c = chains[x]
                q = q_ref[pl.ds(base + c * TC, TC), h * width : (h + 1) * width]
                row = pl.multiple_of(kt * TK + part * CH, CH)
                s = mm(wink[pl.ds(row, CH)], q, NT)
                if masked:
                    bias = bias_ref[part * CH : (part + 1) * CH]
                    s = s + jnp.concatenate([bias] * (TC // 128), axis=1)
                sbuf_ref[x, part * CH : (part + 1) * CH] = s
                return jnp.max(s.reshape(CH // 8, 8, TC), axis=0)

            def stage(cur, kt, nxt, base, kt_nxt, masked):
                old = run_ref[cur, 0:1]
                new = jnp.maximum(old, jnp.max(smax_ref[cur], axis=0, keepdims=True))
                tops, sums, parts = [], [], []
                for part in range(TK // CH):
                    tops.append(scores(nxt, base, kt_nxt, part, masked))
                    w = jnp.exp2((sbuf_ref[cur, part * CH : (part + 1) * CH] - new) * factor)
                    sums.append(jnp.sum(w.reshape(CH // 8, 8, TC), axis=0))
                    parts.append(w.astype(BF))
                smax_ref[nxt] = functools.reduce(jnp.maximum, tops)
                f = jnp.exp2((old - new) * factor)
                total_w = jnp.sum(functools.reduce(jnp.add, sums), axis=0, keepdims=True)
                run_ref[cur, 0:1] = new
                run_ref[cur, 1:2] = run_ref[cur, 1:2] * f + total_w
                row = pl.ds(pl.multiple_of(kt * TK, TK), TK)
                racc_ref[cur] = racc_ref[cur] * f + mm(
                    wvt[:, row], jnp.concatenate(parts, axis=0)
                )

            def sweep(kt, masked):
                for x in range(len(chains) - 1):
                    stage(x, kt, x + 1, first, kt, masked)
                turn = (kt + 1 == tiles) & (cut == 0)
                after_kt = jnp.where(turn, tile0, jnp.minimum(kt + 1, tiles - 1))
                after_first = jnp.where(turn, jnp.minimum(first + wq, n - wq), first)
                base = pl.multiple_of(after_first, wq)
                stage(len(chains) - 1, kt, 0, base, after_kt, False)

            def prime(masked):
                smax_ref[0] = functools.reduce(
                    jnp.maximum, [scores(0, first, tile0, part, masked) for part in range(TK // CH)]
                )

            @pl.when(cut > 0)
            def _():
                prime(True)
                sweep(tile0, True)

            @pl.when((cut == 0) & (qt == 0))
            def _():
                prime(False)


            def step(kt, carry):
                sweep(kt, False)
                return carry

            lax.fori_loop(tile0 + cut, tiles, step, 0)
            i = lax.broadcasted_iota(jnp.int32, (1, wq), 1) + first
            live = i < lead_rows
            for x, (h, c) in enumerate(chains):
                col = column(h, c)
                ok = live[:, c * TC : (c + 1) * TC]
                st2_ref[0:2, col] = jnp.where(ok, run_ref[x, 0:2], st2_ref[0:2, col])
                acc_ref[:, col] = jnp.where(ok, racc_ref[x], acc_ref[:, col])
            return carry

        lax.fori_loop(0, (lead_rows + wq - 1) // wq, qtile, 0)


def window_kernel(
    scale,
    doc_ref, q_ref, start_ref, wk_ref, acc_in, stat_in, own_ref, two_ref, swap_two_ref,
    acc_ref, st2_ref, wkf, statet_ref, csum_ref,
    wink, winv, wcode, wvt, run_ref, racc_ref, sbuf_ref, smax_ref, bias_ref, sem,
):
    width = wk_ref.shape[1]
    n = start_ref.shape[1]
    heads = q_ref.shape[1] // width
    odd = lax.rem(lax.axis_index("seq"), 2)
    begin(load(two_ref, 0, wink, winv, wcode, sem))

    @pl.when(odd == 0)
    def _():
        begin(load(swap_two_ref, 1, wink, winv, wcode, sem))

    @pl.when(odd == 1)
    def _():
        begin(load(own_ref, 1, wink, winv, wcode, sem))

    acc_ref[...] = acc_in[...]
    st2_ref[...] = stat_in[...]
    statet_ref[...] = jnp.zeros_like(statet_ref)
    csum_ref[...] = jnp.zeros_like(csum_ref)
    lead_code = (doc_ref[0] + 1).astype(F32)
    lead_rows = jnp.sum((start_ref[...] == 0).astype(jnp.int32))
    finish(load(two_ref, 0, wink, winv, wcode, sem))
    finish(load(two_ref, 1, wink, winv, wcode, sem))

    stop_key = wink.shape[0]
    window_part(
        scale, n, heads, stop_key - matching(wcode, lead_code), stop_key, lead_rows,
        q_ref, wk_ref, wink, winv, wkf, wvt, statet_ref, csum_ref,
        acc_ref, st2_ref, run_ref, racc_ref, sbuf_ref, smax_ref, bias_ref,
    )


def main_kernel(
    scale, grad_scale, back_scale, tensor_size,
    doc_ref, q_ref, k_ref, v_ref, start_ref, wk_ref,
    qf_ref, kf_ref, acc_in, num_ref, stat_in, den_ref, near_kf, statet_in, csum_in,
    two_ref, four_ref, own_ref, swap_two_ref, swap_four_ref,
    stu_ref, wq_ref, *rest,
):
    outs = rest[:tensor_size]
    (
        neark, nearv, nearc, wink, winv, wcode, wkf, wvt,
        gwq_ref, gwk_ref, adj_ref, adjs_ref, gkf_ref, gkf2_ref,
        state_ref, statet_ref, csum_ref, acc_ref, st2_ref, run_ref, racc_ref, sbuf_ref, smax_ref,
        bias_ref, near_sem, sem,
    ) = rest[tensor_size:]
    n, width = k_ref.shape
    heads = q_ref.shape[1] // width
    half = wk_ref.shape[0]
    odd = lax.rem(lax.axis_index("seq"), 2)
    begin(load(four_ref, 0, wink, winv, wcode, sem))
    begin(load(two_ref, 0, neark, nearv, nearc, near_sem))

    @pl.when(odd == 0)
    def _():
        begin(load(swap_four_ref, 1, wink, winv, wcode, sem))
        begin(load(swap_two_ref, 1, neark, nearv, nearc, near_sem))

    @pl.when(odd == 1)
    def _():
        begin(load(swap_two_ref, 1, wink, winv, wcode, sem))
        begin(load(own_ref, 1, neark, nearv, nearc, near_sem))

    gkf2_ref[...] = jnp.zeros_like(gkf2_ref)
    gwq_ref[...] = jnp.zeros_like(gwq_ref)
    gwk_ref[...] = jnp.zeros_like(gwk_ref)
    adj_ref[...] = jnp.zeros_like(adj_ref)
    statet_ref[...] = statet_in[...]
    csum_ref[...] = csum_in[...]
    acc_ref[...] = acc_in[...]
    st2_ref[...] = stat_in[...]
    lead_code = (doc_ref[0] + 1).astype(F32)
    lead_rows = jnp.sum((start_ref[...] == 0).astype(jnp.int32))
    for slot in range(2):
        finish(load(four_ref, slot, wink, winv, wcode, sem))
        finish(load(two_ref, slot, neark, nearv, nearc, near_sem)[2:])

    near_stop = neark.shape[0]
    near_begin = near_stop - matching(nearc, lead_code)
    far_stop = wink.shape[0]
    far_begin = far_stop - matching(wcode, lead_code)
    linked = near_begin < near_stop
    window_part(
        scale, n, heads, far_begin, far_stop, lead_rows,
        q_ref, wk_ref, wink, winv, wkf, wvt, statet_ref, csum_ref,
        acc_ref, st2_ref, run_ref, racc_ref, sbuf_ref, smax_ref, bias_ref,
    )
    state_ref[...] = statet_ref[...].T
    csum_ref[...] = jnp.broadcast_to(
        jnp.sum(csum_ref[...], axis=1, keepdims=True), csum_ref.shape
    )

    link = linked.astype(F32)
    pad = lax.broadcasted_iota(jnp.int32, (n, 16), 1)
    v_aug = jnp.concatenate([v_ref[...], (pad < 2).astype(F32).astype(BF)], axis=1)
    statet_b = statet_ref[...].astype(BF)
    csum_b = csum_ref[:, :16].astype(BF)
    csum_b = jnp.where(pad[:width] < 2, csum_b.astype(F32), 0.0).astype(BF)
    state_aug = jnp.concatenate([state_ref[...].astype(BF), csum_b], axis=1)
    csum_row = jnp.sum(jnp.where(lax.broadcasted_iota(jnp.int32, csum_ref.shape, 1) == 0, csum_ref[...], 0.0).T, axis=0, keepdims=True)
    edge_row = lax.broadcasted_iota(jnp.int32, (16, width), 0)
    csum_hi = csum_row.astype(BF).astype(F32)
    csum_rows = jnp.where(edge_row == 0, csum_hi, jnp.where(edge_row == 1, csum_row - csum_hi, 0.0))
    statet_aug = jnp.concatenate([statet_b, csum_rows.astype(BF)], axis=0)
    kft_b = kf_ref[...].astype(BF)
    steps = [(qt, h) for qt in range(n // TQ) for h in range(heads)]
    held = {}

    def before(t):
        qt, h = steps[t]
        first = qt * TQ
        limit = first + TQ
        col = slice(h * n + first, h * n + limit)
        r = (start_ref[:, first:limit] == 0).astype(F32) * link
        qf = qf_ref[:, col]
        qf_b = qf.astype(BF)
        qf_r = (qf * r).astype(BF)
        carried = mm(statet_aug, qf_r)
        teacher = acc_ref[:, col] * (1.0 / st2_ref[1:2, col])
        inv = 1.0 / (den_ref[0:1, col] + carried[width : width + 1] + carried[width + 1 : width + 2])
        est = (num_ref[:, col] + carried[:width]) * inv
        stu_ref[first:limit, h * width : (h + 1) * width] = est.T.astype(BF)
        diff = est - teacher
        inv = inv * grad_scale
        gd = -jnp.sum(diff * est, axis=0, keepdims=True) * inv
        gd_hi = gd.astype(BF).astype(F32)
        row = lax.broadcasted_iota(jnp.int32, (16, TQ), 0)
        gd_rows = jnp.where(row == 0, gd_hi, jnp.where(row == 1, gd - gd_hi, 0.0))
        gn = diff * inv
        g = jnp.concatenate([gn.astype(BF), gd_rows.astype(BF)], axis=0)
        g_r = jnp.concatenate([(gn * r).astype(BF), (gd_rows * r).astype(BF)], axis=0)
        held[t] = (first, limit, h, qf_b, qf_r, g, g_r)

    def second_product(t):
        first, limit, h, qf_b, qf_r, g, g_r = held[t]
        start = start_ref[:, first:limit]
        i = lax.broadcasted_iota(jnp.int32, (1, TQ), 1) + first
        parts = []
        for at in range(0, limit, TQ):
            j = lax.broadcasted_iota(jnp.int32, (TQ, TQ), 0) + at
            ok = j >= start
            if at == first:
                ok = ok & (j <= i)
            parts.append(jnp.where(ok, mm(v_aug[at : at + TQ], g), 0.0).astype(BF))
        gp = jnp.concatenate(parts, axis=0)
        gkf2_ref[:limit] += mm(gp, qf_b, NT)
        adj_ref[...] += mm(qf_r, g, NT)
        held[t] = (first, limit, h, mm(jnp.concatenate([kft_b[:, :limit], state_aug], axis=1), jnp.concatenate([gp, g_r], axis=0)))

    def after(t):
        first, limit, h, gq = held.pop(t)
        col = slice(h * n + first, h * n + limit)
        ga = feature_back_t(qf_ref[:, col], gq).astype(BF)
        gwq_ref[h] += mm(ga, q_ref[first:limit, h * width : (h + 1) * width])

    count = len(steps)
    before(0)
    for t in range(count):
        if t + 1 < count:
            before(t + 1)
        second_product(t)
        if t:
            after(t - 1)
    after(count - 1)

    gkf = gkf2_ref[...].T
    gkf_ref[...] = gkf * back_scale
    gl = feature_back_t(kf_ref[...], gkf).astype(BF)
    gwk_ref[...] += mm(gl, k_ref[...])
    adj_b = adj_ref[:, :width].astype(BF)
    adjs_col = adj_ref[:, width : width + 1] + adj_ref[:, width + 1 : width + 2]

    def back_over(begin_key, stop_key, keys, values, feats):
        def back(kt, carry):
            row = pl.ds(pl.multiple_of(kt * TK, TK), TK)
            more = mm(adj_b, values[row], NT) + adjs_col
            j = lax.broadcasted_iota(jnp.int32, (1, TK), 1) + kt * TK
            gl = feature_back_t(feats[:, row], more)
            gl = jnp.where(j >= begin_key, gl, 0.0).astype(BF)
            gwk_ref[...] += mm(gl, keys[row])
            return carry

        lax.fori_loop(begin_key // TK, stop_key // TK, back, 0)

    for slot in range(2):
        finish(load(two_ref, slot, neark, nearv, nearc, near_sem)[:2])
    back_over(near_begin, near_stop, neark, nearv, near_kf)
    back_over(far_begin, far_stop, wink, winv, wkf)

    for h in range(heads):
        wq_ref[h * half : (h + 1) * half] = gwq_ref[h].astype(BF)
    adjs_ref[...] = jnp.broadcast_to(adjs_col, adjs_ref.shape)
    row = jnp.max(adjs_ref[...].T, axis=0, keepdims=True)
    row_hi = row.astype(BF).astype(F32)
    tail = jnp.where(edge_row == 0, row_hi, jnp.where(edge_row == 1, row - row_hi, 0.0)).astype(BF)
    gwk_b = gwk_ref[...].astype(BF)
    tensor = len(outs)
    rows = width // tensor
    mine = lax.axis_index("tensor")
    for k in range(tensor):
        piece = pl.ds(pl.multiple_of(lax.rem(mine + k, tensor) * rows, rows), rows)
        outs[k][0:rows] = gkf_ref[piece].astype(BF)
        part = adj_ref[piece, :width].astype(BF)
        blocks = [part[c * 16 : (c + 1) * 16] for c in range(rows // 16)] + [tail]
        blocks += [gwk_b[c * 16 : (c + 1) * 16] for c in range(half // 16)]
        outs[k][rows:] = jnp.zeros_like(outs[k][rows:])
        for c, block in enumerate(blocks):
            outs[k][rows:, c * width : (c + 1) * width] = block


def join_kernel(tensor, doc_ref, wq_ref, *refs):
    ins, (sum_ref, out_ref) = refs[:tensor], refs[tensor:]
    rows = sum_ref.shape[0]
    width = out_ref.shape[1]
    half = width // 2
    total = ins[0][...].astype(F32)
    for k in range(1, tensor):
        total = total + ins[k][...].astype(F32)
    sum_ref[...] = total[:rows]
    at = wq_ref.shape[0]
    out_ref[0:at] = wq_ref[...]
    pieces = [total[rows:, c * width : (c + 1) * width] for c in range(total.shape[1] // width)]
    parts = rows // 16
    out_ref[at : at + rows] = jnp.concatenate(pieces[:parts], axis=0).astype(BF)
    at += rows
    tail = pieces[parts]
    row = tail[0:1] + tail[1:2]
    row_hi = row.astype(BF).astype(F32)
    index = lax.broadcasted_iota(jnp.int32, (16, width), 0)
    code = (doc_ref[0] + 1).astype(F32)
    tail = jnp.where(index == 0, row_hi, jnp.where(index == 1, row - row_hi, code))
    out_ref[at : at + 16] = tail.astype(BF)
    at += 16
    gwk = jnp.concatenate(pieces[parts + 1 : parts + 1 + half // 16], axis=0)
    out_ref[at : at + half] = gwk.astype(BF)


def last_kernel(
    seq, back_scale,
    doc_ref, edge_ref, gath_ref, sum_ref, v_ref,
    kfg_ref, gwq_ref, gwk_ref,
    adj_ref, adjs_ref, col_ref,
):
    n, width = v_ref.shape
    heads, half = gwq_ref.shape[:2]
    rows = sum_ref.shape[0]
    me = lax.axis_index("seq")
    mine = lax.axis_index("tensor")
    last_code = (doc_ref[n - 1] + 1).astype(F32)
    edge = edge_ref[n - 1]

    def gathered(first, size):
        x = gath_ref[0, first : first + size].astype(F32)
        for d in range(1, seq):
            x = x + gath_ref[d, first : first + size].astype(F32)
        return x

    for h in range(heads):
        gwq_ref[h] = gathered(h * half, half)
    at = heads * half
    gwk_ref[...] = gathered(at + rows + 16, half)
    adj_ref[...] = jnp.zeros_like(adj_ref)
    adjs_ref[...] = jnp.zeros_like(adjs_ref)

    def later(s, carry):
        a = gath_ref[s, at : at + rows].astype(F32)
        t = gath_ref[s, at + rows : at + rows + 16].astype(F32)
        same = t[2:3] == last_code
        adj_ref[...] += jnp.where(same, a, 0.0)
        adjs_ref[...] += jnp.where(same, t[0:1] + t[1:2], 0.0)
        return carry

    lax.fori_loop(me + 1, jnp.minimum(me + REACH + 1, seq), later, 0)
    adj = adj_ref[...]
    a_hi = adj.astype(BF)
    a_lo = (adj - a_hi.astype(F32)).astype(BF)
    col_ref[...] = jnp.broadcast_to(adjs_ref[...], (width, width)).T
    col = col_ref[pl.ds(pl.multiple_of(mine * rows, rows), rows), 0:1]
    j = lax.broadcasted_iota(jnp.int32, (1, n), 1)
    more = mm(a_hi, v_ref[...], NT) + mm(a_lo, v_ref[...], NT) + col
    kfg_ref[...] = sum_ref[...] + jnp.where(j >= edge, more, 0.0) * back_scale


VM = pl.BlockSpec(memory_space=pltpu.VMEM)
SM = pl.BlockSpec(memory_space=pltpu.SMEM)
ANY = pl.BlockSpec(memory_space=pl.ANY)


def grant(mib):
    return pltpu.CompilerParams(vmem_limit_bytes=mib << 20)


def cost(flops, size):
    return pl.CostEstimate(flops=flops, bytes_accessed=size, transcendentals=0)


def shards(queries, keys, values, doc_ids, w_query, w_key):
    n, heads, width = queries.shape
    half = w_key.shape[1]
    seq = lax.axis_size("seq")
    tensor = lax.axis_size("tensor")
    scale = width ** (-0.5)
    everyone = range(seq)
    assert n // width <= 16 and n // width * 16 == width

    codes = (doc_ids.reshape(n // width, width) + 1).astype(BF)
    codes = jnp.pad(codes, ((0, 16 - n // width), (0, 0)))
    pack = jnp.concatenate([keys, values, codes], axis=0)

    def hop(x, distance):
        return lax.ppermute(x, "seq", [(i, i + distance) for i in everyone if i + distance < seq])

    two = hop(pack, 2)
    own = lax.ppermute(pack, "seq", [(i, i + 1) for i in everyone if i % 2 == 0])

    qs = queries.reshape(n, heads * width)
    starts = jnp.sum((doc_ids[None, :] < doc_ids[:, None]).astype(jnp.int32), axis=1)
    start_row = starts.reshape(1, n)
    wq_t = jnp.transpose(w_query, (0, 2, 1))
    wk_t = w_key.T
    sds = jax.ShapeDtypeStruct
    cols = heads * n
    rows = width // tensor
    near = REACH // 2
    chains = heads * min(n, CHAINS * TC // heads) // TC
    square = sds((width, width), F32)
    wide = sds((width, cols), F32)
    flat = sds((8, cols), F32)
    scan = [
        pltpu.VMEM((chains, 8, TC), F32),
        pltpu.VMEM((chains, width, TC), F32),
        pltpu.VMEM((chains, TK, TC), F32),
        pltpu.VMEM((chains, 8, TC), F32),
        pltpu.VMEM((TK, 128), F32),
    ]
    vt, acc, stat = pl.pallas_call(
        functools.partial(teacher_kernel, scale),
        out_shape=(sds((width, n), BF), wide, flat),
        in_specs=[VM] * 4,
        out_specs=[VM] * 3,
        compiler_params=grant(12),
        cost_estimate=cost(4 * n * n * width * heads, 4 << 20),
    )(qs, keys, values, start_row)
    four = hop(pack, 4)
    qf, kf, num, den = pl.pallas_call(
        student_kernel,
        out_shape=(wide, sds((width, n), F32), wide, flat),
        in_specs=[VM] * 6,
        out_specs=[VM] * 4,
        scratch_shapes=[pltpu.VMEM((n, width), BF)],
        compiler_params=grant(12),
        cost_estimate=cost(4 * n * n * width * heads, 4 << 20),
    )(qs, keys, vt, start_row, wq_t, wk_t)

    swap_two = lax.ppermute(two, "seq", [(i, i ^ 1) for i in everyone])
    acc, stat, near_kf, statet, csum = pl.pallas_call(
        functools.partial(window_kernel, scale),
        out_shape=(wide, flat, sds((width, near * n), F32), square, square),
        in_specs=[SM] + [VM] * 5 + [ANY] * 3,
        out_specs=[VM] * 5,
        scratch_shapes=[
            pltpu.VMEM((near * n, width), BF),
            pltpu.VMEM((near * n, width), BF),
            pltpu.VMEM((near, 16, width), BF),
            pltpu.VMEM((width, near * n), BF),
        ]
        + scan
        + [pltpu.SemaphoreType.DMA((near, 3))],
        compiler_params=grant(20),
        cost_estimate=cost(8 * n * n * width * heads, 4 << 20),
    )(doc_ids, qs, start_row, wk_t, acc, stat, own, two, swap_two)

    swap_four = lax.ppermute(four, "seq", [(i, i - 1) for i in everyone if i % 2 == 1])
    student, wq_part, *pieces = pl.pallas_call(
        functools.partial(main_kernel, scale, 2.0 / (n * seq), float(n * seq), tensor),
        out_shape=[sds((n, heads * width), BF), sds((heads * half, width), BF)]
        + [sds((rows + 16, n), BF)] * tensor,
        in_specs=[SM] + [VM] * 14 + [ANY] * 5,
        out_specs=[VM] * (2 + tensor),
        scratch_shapes=[
            pltpu.VMEM((near * n, width), BF),
            pltpu.VMEM((near * n, width), BF),
            pltpu.VMEM((near, 16, width), BF),
            pltpu.VMEM((2 * n, width), BF),
            pltpu.VMEM((2 * n, width), BF),
            pltpu.VMEM((2, 16, width), BF),
            pltpu.VMEM((width, 2 * n), F32),
            pltpu.VMEM((width, 2 * n), BF),
            pltpu.VMEM((heads, half, width), F32),
            pltpu.VMEM((half, width), F32),
            pltpu.VMEM((width, width + 16), F32),
            pltpu.VMEM((width, 128), F32),
            pltpu.VMEM((width, n), F32),
            pltpu.VMEM((n, width), F32),
            pltpu.VMEM((width, width), F32),
            pltpu.VMEM((width, width), F32),
            pltpu.VMEM((width, 128), F32),
            pltpu.VMEM((width, cols), F32),
            pltpu.VMEM((8, cols), F32),
        ]
        + scan
        + [pltpu.SemaphoreType.DMA((near, 3)), pltpu.SemaphoreType.DMA((2, 3))],
        compiler_params=grant(32),
        cost_estimate=cost(16 * n * n * width * heads, 8 << 20),
    )(
        doc_ids, qs, keys, values, start_row, wk_t,
        qf, kf, acc, num, stat, den, near_kf, statet, csum,
        two, four, own, swap_two, swap_four,
    )

    arrived = [pieces[0]]
    for k in range(1, tensor):
        arrived.append(
            lax.ppermute(pieces[k], "tensor", [(i, (i + k) % tensor) for i in range(tensor)])
        )
    packed = heads * half + rows + 16 + half
    part, out = pl.pallas_call(
        functools.partial(join_kernel, tensor),
        out_shape=(sds((rows, n), F32), sds((packed, width), BF)),
        in_specs=[SM] + [VM] * (tensor + 1),
        out_specs=[VM] * 2,
        compiler_params=grant(8),
        cost_estimate=cost(n * width, 1 << 20),
    )(doc_ids, wq_part, *arrived)
    gathered = lax.all_gather(out, "seq")
    key_grads, gwq, gwk = pl.pallas_call(
        functools.partial(last_kernel, seq, float(n * seq)),
        out_shape=(sds((rows, n), F32), sds((heads, half, width), F32), sds((half, width), F32)),
        in_specs=[SM, SM, VM, VM, VM],
        out_specs=[VM] * 3,
        scratch_shapes=[
            pltpu.VMEM((rows, width), F32),
            pltpu.VMEM((1, width), F32),
            pltpu.VMEM((width, width), F32),
        ],
        compiler_params=grant(12),
        cost_estimate=cost(4 * n * width * width, 2 << 20),
    )(doc_ids, starts, gathered, part, values)
    return student.reshape(n, heads, width), jnp.transpose(gwq, (0, 2, 1)), gwk.T, key_grads.T


def solution(mesh):
    placed = (
        P("seq", "tensor", None),
        P("seq", None),
        P("seq", None),
        P("seq"),
        P("tensor", None, None),
        P(),
    )

    return jax.shard_map(
        shards,
        mesh=mesh,
        in_specs=placed,
        out_specs=(P("seq", "tensor", None), P("tensor", None, None), P(), P("seq", "tensor")),
        check_vma=False,
    )
```

```python
import functools

import jax
import jax.numpy as jnp
from jax import lax
from jax.experimental import pallas as pl
from jax.experimental.pallas import tpu as pltpu
from jax.sharding import PartitionSpec as P


REACH = 4
NEG = -1e30
LOG2E = 1.4426950408889634
TQ = 256
TK = 1024
TC = 256
CH = 512
CHAINS = 8
BF = jnp.bfloat16
F32 = jnp.float32

NT = (((1,), (1,)), ((), ()))
NN = (((1,), (0,)), ((), ()))


def mm(a, b, dims=NN):
    return lax.dot_general(a, b, dims, preferred_element_type=F32)


def feature_t(logits):
    top = jnp.max(logits, axis=0, keepdims=True)
    low = jnp.min(logits, axis=0, keepdims=True)
    up = jnp.exp(logits - top)
    down = jnp.exp(low - logits)
    up = up * (1.0 / jnp.sum(up, axis=0, keepdims=True))
    down = down * (1.0 / jnp.sum(down, axis=0, keepdims=True))
    return jnp.concatenate([up, down], axis=0)


def feature_back_t(feat, grad):
    half = feat.shape[0] // 2
    p, m = feat[:half], feat[half:]
    a, b = grad[:half], grad[half:]
    return p * (a - jnp.sum(a * p, axis=0, keepdims=True)) - m * (
        b - jnp.sum(b * m, axis=0, keepdims=True)
    )


def allowed_t(limit, first, start):
    j = lax.broadcasted_iota(jnp.int32, (limit, TQ), 0)
    i = lax.broadcasted_iota(jnp.int32, (1, TQ), 1) + first
    return (j <= i) & (j >= start)


def transposed(x):
    return x.astype(F32).T


def teacher_kernel(scale, q_ref, k_ref, v_ref, start_ref, vt_ref, acc_ref, stat_ref):
    n, width = k_ref.shape
    heads = q_ref.shape[1] // width
    vt_ref[...] = transposed(v_ref[...]).astype(BF)

    def head(h, carry):
        lane = pl.multiple_of(h * width, width)
        for qt in range(n // TQ):
            first = qt * TQ
            limit = first + TQ
            col = pl.ds(pl.multiple_of(h * n + first, TQ), TQ)
            q = q_ref[first:limit, pl.ds(lane, width)]
            ok = allowed_t(limit, first, start_ref[:, first:limit])
            s = jnp.where(ok, mm(k_ref[:limit], q, NT), NEG)
            top = jnp.max(s, axis=0, keepdims=True)
            w = jnp.exp2((s - top) * (scale * LOG2E))
            stat_ref[0:1, col] = top
            stat_ref[1:2, col] = jnp.sum(w, axis=0, keepdims=True)
            acc_ref[:, col] = mm(vt_ref[:, :limit], w.astype(BF))
        return carry

    lax.fori_loop(0, heads, head, 0)


def student_kernel(
    q_ref, k_ref, vt_ref, start_ref, wq_ref, wk_ref, qf_ref, kf_ref, num_ref, den_ref, kfb_ref
):
    n, width = k_ref.shape
    heads = q_ref.shape[1] // width
    kf = feature_t(mm(wk_ref[...], k_ref[...], NT))
    kf_ref[...] = kf
    kfb_ref[...] = kf.T.astype(BF)

    def head(h, carry):
        lane = pl.multiple_of(h * width, width)
        for qt in range(n // TQ):
            first = qt * TQ
            limit = first + TQ
            col = pl.ds(pl.multiple_of(h * n + first, TQ), TQ)
            q = q_ref[first:limit, pl.ds(lane, width)]
            ok = allowed_t(limit, first, start_ref[:, first:limit])
            qf = feature_t(mm(wq_ref[h], q, NT))
            qf_ref[:, col] = qf
            pr = jnp.where(ok, mm(kfb_ref[:limit], qf.astype(BF)), 0.0)
            den_ref[0:1, col] = jnp.sum(pr, axis=0, keepdims=True)
            num_ref[:, col] = mm(vt_ref[:, :limit], pr.astype(BF))
        return carry

    lax.fori_loop(0, heads, head, 0)


def load(src, slot, keys, values, codes, sem):
    n = keys.shape[0] // codes.shape[0]
    return (
        pltpu.make_async_copy(src.at[0:n], keys.at[slot * n : (slot + 1) * n], sem.at[slot, 0]),
        pltpu.make_async_copy(src.at[n : 2 * n], values.at[slot * n : (slot + 1) * n], sem.at[slot, 1]),
        pltpu.make_async_copy(src.at[2 * n : 2 * n + 16], codes.at[slot], sem.at[slot, 2]),
    )


def begin(copies):
    for c in copies:
        c.start()


def finish(copies):
    for c in copies:
        c.wait()


def tile_rows(kt):
    if isinstance(kt, int):
        return pl.ds(kt * TK, TK)
    return pl.ds(pl.multiple_of(kt * TK, TK), TK)


def each_tile(begin_key, size, body):
    if size != 2 * TK:
        lax.fori_loop(begin_key // TK, size // TK, lambda kt, carry: body(kt) or carry, 0)
        return

    @pl.when(begin_key < TK)
    def _():
        body(0)
        body(1)

    @pl.when((begin_key >= TK) & (begin_key < size))
    def _():
        body(1)


def matching(codes, code):
    return jnp.sum((codes[...].astype(F32) == code).astype(jnp.int32))


def window_part(
    scale, n, heads, begin_key, stop_key, lead_rows,
    q_ref, wk_ref, wink, winv, wkf, wvt, statet_ref, csum_ref,
    acc_ref, st2_ref, run_ref, racc_ref, sbuf_ref, smax_ref, bias_ref,
):
    width = wink.shape[1]
    tile0 = begin_key // TK
    tiles = stop_key // TK
    cut = jnp.minimum(begin_key - tile0 * TK, 1)

    @pl.when(begin_key < stop_key)
    def _():
        def prepare(kt):
            row = tile_rows(kt)
            kf = feature_t(mm(wk_ref[...], wink[row], NT))
            wkf[:, row] = kf
            j = lax.broadcasted_iota(jnp.int32, (1, TK), 1) + kt * TK
            kfm = jnp.where(j >= begin_key, kf, 0.0).astype(BF)
            vt = transposed(winv[row]).astype(BF)
            wvt[:, row] = vt
            statet_ref[...] += mm(vt, kfm, NT)
            part = kfm.astype(F32)
            for c in range(TK // 128):
                csum_ref[...] += part[:, c * 128 : (c + 1) * 128]

        each_tile(begin_key, stop_key, prepare)
        key = lax.broadcasted_iota(jnp.int32, bias_ref.shape, 0) + tile0 * TK
        bias_ref[...] = jnp.where(key >= begin_key, 0.0, NEG)
        wq = min(n, CHAINS * TC // heads)
        chains = [(h, c) for h in range(heads) for c in range(wq // TC)]
        factor = scale * LOG2E

        def qtile(qt, carry):
            first = pl.multiple_of(qt * wq, wq)

            def column(h, c):
                return pl.ds(pl.multiple_of(h * n + first + c * TC, TC), TC)

            for x, (h, c) in enumerate(chains):
                col = column(h, c)
                run_ref[x, 0:1] = st2_ref[0:1, col]
                run_ref[x, 1:2] = st2_ref[1:2, col]
                racc_ref[x] = acc_ref[:, col]

            def scores(x, base, kt, part, masked):
                h, c = chains[x]
                q = q_ref[pl.ds(base + c * TC, TC), h * width : (h + 1) * width]
                row = pl.multiple_of(kt * TK + part * CH, CH)
                s = mm(wink[pl.ds(row, CH)], q, NT)
                if masked:
                    bias = bias_ref[part * CH : (part + 1) * CH]
                    s = s + jnp.concatenate([bias] * (TC // 128), axis=1)
                sbuf_ref[x, part * CH : (part + 1) * CH] = s
                return jnp.max(s.reshape(CH // 8, 8, TC), axis=0)

            def stage(cur, kt, nxt, base, kt_nxt, masked):
                old = run_ref[cur, 0:1]
                new = jnp.maximum(old, jnp.max(smax_ref[cur], axis=0, keepdims=True))
                tops, sums, parts = [], [], []
                for part in range(TK // CH):
                    tops.append(scores(nxt, base, kt_nxt, part, masked))
                    w = jnp.exp2((sbuf_ref[cur, part * CH : (part + 1) * CH] - new) * factor)
                    sums.append(jnp.sum(w.reshape(CH // 8, 8, TC), axis=0))
                    parts.append(w.astype(BF))
                smax_ref[nxt] = functools.reduce(jnp.maximum, tops)
                f = jnp.exp2((old - new) * factor)
                total_w = jnp.sum(functools.reduce(jnp.add, sums), axis=0, keepdims=True)
                run_ref[cur, 0:1] = new
                run_ref[cur, 1:2] = run_ref[cur, 1:2] * f + total_w
                row = pl.ds(pl.multiple_of(kt * TK, TK), TK)
                racc_ref[cur] = racc_ref[cur] * f + mm(
                    wvt[:, row], jnp.concatenate(parts, axis=0)
                )

            def sweep(kt, masked):
                for x in range(len(chains) - 1):
                    stage(x, kt, x + 1, first, kt, masked)
                turn = (kt + 1 == tiles) & (cut == 0)
                after_kt = jnp.where(turn, tile0, jnp.minimum(kt + 1, tiles - 1))
                after_first = jnp.where(turn, jnp.minimum(first + wq, n - wq), first)
                base = pl.multiple_of(after_first, wq)
                stage(len(chains) - 1, kt, 0, base, after_kt, False)

            def prime(masked):
                smax_ref[0] = functools.reduce(
                    jnp.maximum, [scores(0, first, tile0, part, masked) for part in range(TK // CH)]
                )

            @pl.when(cut > 0)
            def _():
                prime(True)
                sweep(tile0, True)

            @pl.when((cut == 0) & (qt == 0))
            def _():
                prime(False)


            def step(kt, carry):
                sweep(kt, False)
                return carry

            lax.fori_loop(tile0 + cut, tiles, step, 0)
            i = lax.broadcasted_iota(jnp.int32, (1, wq), 1) + first
            live = i < lead_rows
            for x, (h, c) in enumerate(chains):
                col = column(h, c)
                ok = live[:, c * TC : (c + 1) * TC]
                st2_ref[0:2, col] = jnp.where(ok, run_ref[x, 0:2], st2_ref[0:2, col])
                acc_ref[:, col] = jnp.where(ok, racc_ref[x], acc_ref[:, col])
            return carry

        lax.fori_loop(0, (lead_rows + wq - 1) // wq, qtile, 0)


def window_kernel(
    scale,
    doc_ref, q_ref, start_ref, wk_ref, acc_in, stat_in, own_ref, two_ref, swap_two_ref,
    acc_ref, st2_ref, wkf, statet_ref, csum_ref,
    wink, winv, wcode, wvt, run_ref, racc_ref, sbuf_ref, smax_ref, bias_ref, sem,
):
    width = wk_ref.shape[1]
    n = start_ref.shape[1]
    heads = q_ref.shape[1] // width
    odd = lax.rem(lax.axis_index("seq"), 2)
    begin(load(two_ref, 0, wink, winv, wcode, sem))

    @pl.when(odd == 0)
    def _():
        begin(load(swap_two_ref, 1, wink, winv, wcode, sem))

    @pl.when(odd == 1)
    def _():
        begin(load(own_ref, 1, wink, winv, wcode, sem))

    acc_ref[...] = acc_in[...]
    st2_ref[...] = stat_in[...]
    statet_ref[...] = jnp.zeros_like(statet_ref)
    csum_ref[...] = jnp.zeros_like(csum_ref)
    lead_code = (doc_ref[0] + 1).astype(F32)
    lead_rows = jnp.sum((start_ref[...] == 0).astype(jnp.int32))
    finish(load(two_ref, 0, wink, winv, wcode, sem))
    finish(load(two_ref, 1, wink, winv, wcode, sem))

    stop_key = wink.shape[0]
    window_part(
        scale, n, heads, stop_key - matching(wcode, lead_code), stop_key, lead_rows,
        q_ref, wk_ref, wink, winv, wkf, wvt, statet_ref, csum_ref,
        acc_ref, st2_ref, run_ref, racc_ref, sbuf_ref, smax_ref, bias_ref,
    )


def main_kernel(
    scale, grad_scale, back_scale, tensor_size,
    doc_ref, q_ref, k_ref, v_ref, start_ref, wk_ref,
    qf_ref, kf_ref, acc_in, num_ref, stat_in, den_ref, near_kf, statet_in, csum_in,
    two_ref, four_ref, own_ref, swap_two_ref, swap_four_ref,
    stu_ref, wq_ref, *rest,
):
    outs = rest[:tensor_size]
    (
        neark, nearv, nearc, wink, winv, wcode, wkf, wvt,
        gwq_ref, gwk_ref, adj_ref, adjs_ref, gkf_ref, gkf2_ref,
        state_ref, statet_ref, csum_ref, acc_ref, st2_ref, run_ref, racc_ref, sbuf_ref, smax_ref,
        bias_ref, near_sem, sem,
    ) = rest[tensor_size:]
    n, width = k_ref.shape
    heads = q_ref.shape[1] // width
    half = wk_ref.shape[0]
    odd = lax.rem(lax.axis_index("seq"), 2)
    begin(load(four_ref, 0, wink, winv, wcode, sem))
    begin(load(two_ref, 0, neark, nearv, nearc, near_sem))

    @pl.when(odd == 0)
    def _():
        begin(load(swap_four_ref, 1, wink, winv, wcode, sem))
        begin(load(swap_two_ref, 1, neark, nearv, nearc, near_sem))

    @pl.when(odd == 1)
    def _():
        begin(load(swap_two_ref, 1, wink, winv, wcode, sem))
        begin(load(own_ref, 1, neark, nearv, nearc, near_sem))

    gkf2_ref[...] = jnp.zeros_like(gkf2_ref)
    gwq_ref[...] = jnp.zeros_like(gwq_ref)
    gwk_ref[...] = jnp.zeros_like(gwk_ref)
    adj_ref[...] = jnp.zeros_like(adj_ref)
    statet_ref[...] = statet_in[...]
    csum_ref[...] = csum_in[...]
    acc_ref[...] = acc_in[...]
    st2_ref[...] = stat_in[...]
    lead_code = (doc_ref[0] + 1).astype(F32)
    lead_rows = jnp.sum((start_ref[...] == 0).astype(jnp.int32))
    for slot in range(2):
        finish(load(four_ref, slot, wink, winv, wcode, sem))
        finish(load(two_ref, slot, neark, nearv, nearc, near_sem)[2:])

    near_stop = neark.shape[0]
    near_begin = near_stop - matching(nearc, lead_code)
    far_stop = wink.shape[0]
    far_begin = far_stop - matching(wcode, lead_code)
    linked = near_begin < near_stop
    window_part(
        scale, n, heads, far_begin, far_stop, lead_rows,
        q_ref, wk_ref, wink, winv, wkf, wvt, statet_ref, csum_ref,
        acc_ref, st2_ref, run_ref, racc_ref, sbuf_ref, smax_ref, bias_ref,
    )
    state_ref[...] = statet_ref[...].T
    csum_ref[...] = jnp.broadcast_to(
        jnp.sum(csum_ref[...], axis=1, keepdims=True), csum_ref.shape
    )

    link = linked.astype(F32)
    pad = lax.broadcasted_iota(jnp.int32, (n, 16), 1)
    v_aug = jnp.concatenate([v_ref[...], (pad < 2).astype(F32).astype(BF)], axis=1)
    statet_b = statet_ref[...].astype(BF)
    csum_b = csum_ref[:, :16].astype(BF)
    csum_b = jnp.where(pad[:width] < 2, csum_b.astype(F32), 0.0).astype(BF)
    state_aug = jnp.concatenate([state_ref[...].astype(BF), csum_b], axis=1)
    csum_row = jnp.sum(jnp.where(lax.broadcasted_iota(jnp.int32, csum_ref.shape, 1) == 0, csum_ref[...], 0.0).T, axis=0, keepdims=True)
    edge_row = lax.broadcasted_iota(jnp.int32, (16, width), 0)
    csum_hi = csum_row.astype(BF).astype(F32)
    csum_rows = jnp.where(edge_row == 0, csum_hi, jnp.where(edge_row == 1, csum_row - csum_hi, 0.0))
    statet_aug = jnp.concatenate([statet_b, csum_rows.astype(BF)], axis=0)
    kft_b = kf_ref[...].astype(BF)
    steps = [(qt, h) for qt in range(n // TQ) for h in range(heads)]
    held = {}

    def before(t):
        qt, h = steps[t]
        first = qt * TQ
        limit = first + TQ
        col = slice(h * n + first, h * n + limit)
        r = (start_ref[:, first:limit] == 0).astype(F32) * link
        qf = qf_ref[:, col]
        qf_b = qf.astype(BF)
        qf_r = (qf * r).astype(BF)
        carried = mm(statet_aug, qf_r)
        teacher = acc_ref[:, col] * (1.0 / st2_ref[1:2, col])
        inv = 1.0 / (den_ref[0:1, col] + carried[width : width + 1] + carried[width + 1 : width + 2])
        est = (num_ref[:, col] + carried[:width]) * inv
        stu_ref[first:limit, h * width : (h + 1) * width] = est.T.astype(BF)
        diff = est - teacher
        inv = inv * grad_scale
        gd = -jnp.sum(diff * est, axis=0, keepdims=True) * inv
        gd_hi = gd.astype(BF).astype(F32)
        row = lax.broadcasted_iota(jnp.int32, (16, TQ), 0)
        gd_rows = jnp.where(row == 0, gd_hi, jnp.where(row == 1, gd - gd_hi, 0.0))
        gn = diff * inv
        g = jnp.concatenate([gn.astype(BF), gd_rows.astype(BF)], axis=0)
        g_r = jnp.concatenate([(gn * r).astype(BF), (gd_rows * r).astype(BF)], axis=0)
        held[t] = (first, limit, h, qf_b, qf_r, g, g_r)

    def second_product(t):
        first, limit, h, qf_b, qf_r, g, g_r = held[t]
        start = start_ref[:, first:limit]
        i = lax.broadcasted_iota(jnp.int32, (1, TQ), 1) + first
        parts = []
        for at in range(0, limit, TQ):
            j = lax.broadcasted_iota(jnp.int32, (TQ, TQ), 0) + at
            ok = j >= start
            if at == first:
                ok = ok & (j <= i)
            parts.append(jnp.where(ok, mm(v_aug[at : at + TQ], g), 0.0).astype(BF))
        gp = jnp.concatenate(parts, axis=0)
        gkf2_ref[:limit] += mm(gp, qf_b, NT)
        adj_ref[...] += mm(qf_r, g, NT)
        held[t] = (first, limit, h, mm(jnp.concatenate([kft_b[:, :limit], state_aug], axis=1), jnp.concatenate([gp, g_r], axis=0)))

    def after(t):
        first, limit, h, gq = held.pop(t)
        col = slice(h * n + first, h * n + limit)
        ga = feature_back_t(qf_ref[:, col], gq).astype(BF)
        gwq_ref[h] += mm(ga, q_ref[first:limit, h * width : (h + 1) * width])

    count = len(steps)
    before(0)
    for t in range(count):
        if t + 1 < count:
            before(t + 1)
        second_product(t)
        if t:
            after(t - 1)
    after(count - 1)

    gkf = gkf2_ref[...].T
    gkf_ref[...] = gkf * back_scale
    gl = feature_back_t(kf_ref[...], gkf).astype(BF)
    gwk_ref[...] += mm(gl, k_ref[...])
    adj_b = adj_ref[:, :width].astype(BF)
    adjs_col = adj_ref[:, width : width + 1] + adj_ref[:, width + 1 : width + 2]

    def back_over(begin_key, stop_key, keys, values, feats):
        def back(kt):
            row = tile_rows(kt)
            more = mm(adj_b, values[row], NT) + adjs_col
            j = lax.broadcasted_iota(jnp.int32, (1, TK), 1) + kt * TK
            gl = feature_back_t(feats[:, row], more)
            gl = jnp.where(j >= begin_key, gl, 0.0).astype(BF)
            gwk_ref[...] += mm(gl, keys[row])

        each_tile(begin_key, stop_key, back)

    for slot in range(2):
        finish(load(two_ref, slot, neark, nearv, nearc, near_sem)[:2])
    back_over(near_begin, near_stop, neark, nearv, near_kf)
    back_over(far_begin, far_stop, wink, winv, wkf)

    for h in range(heads):
        wq_ref[h * half : (h + 1) * half] = gwq_ref[h].astype(BF)
    adjs_ref[...] = jnp.broadcast_to(adjs_col, adjs_ref.shape)
    row = jnp.max(adjs_ref[...].T, axis=0, keepdims=True)
    row_hi = row.astype(BF).astype(F32)
    tail = jnp.where(edge_row == 0, row_hi, jnp.where(edge_row == 1, row - row_hi, 0.0)).astype(BF)
    gwk_b = gwk_ref[...].astype(BF)
    tensor = len(outs)
    rows = width // tensor
    mine = lax.axis_index("tensor")
    for k in range(tensor):
        piece = pl.ds(pl.multiple_of(lax.rem(mine + k, tensor) * rows, rows), rows)
        outs[k][0:rows] = gkf_ref[piece].astype(BF)
        part = adj_ref[piece, :width].astype(BF)
        blocks = [part[c * 16 : (c + 1) * 16] for c in range(rows // 16)] + [tail]
        blocks += [gwk_b[c * 16 : (c + 1) * 16] for c in range(half // 16)]
        outs[k][rows:] = jnp.zeros_like(outs[k][rows:])
        for c, block in enumerate(blocks):
            outs[k][rows:, c * width : (c + 1) * width] = block


def join_kernel(tensor, doc_ref, wq_ref, *refs):
    ins, (sum_ref, out_ref) = refs[:tensor], refs[tensor:]
    rows = sum_ref.shape[0]
    width = out_ref.shape[1]
    half = width // 2
    total = ins[0][...].astype(F32)
    for k in range(1, tensor):
        total = total + ins[k][...].astype(F32)
    sum_ref[...] = total[:rows]
    at = wq_ref.shape[0]
    out_ref[0:at] = wq_ref[...]
    pieces = [total[rows:, c * width : (c + 1) * width] for c in range(total.shape[1] // width)]
    parts = rows // 16
    out_ref[at : at + rows] = jnp.concatenate(pieces[:parts], axis=0).astype(BF)
    at += rows
    tail = pieces[parts]
    row = tail[0:1] + tail[1:2]
    row_hi = row.astype(BF).astype(F32)
    index = lax.broadcasted_iota(jnp.int32, (16, width), 0)
    code = (doc_ref[0] + 1).astype(F32)
    tail = jnp.where(index == 0, row_hi, jnp.where(index == 1, row - row_hi, code))
    out_ref[at : at + 16] = tail.astype(BF)
    at += 16
    gwk = jnp.concatenate(pieces[parts + 1 : parts + 1 + half // 16], axis=0)
    out_ref[at : at + half] = gwk.astype(BF)


def last_kernel(
    seq, back_scale,
    doc_ref, edge_ref, gath_ref, sum_ref, v_ref,
    kfg_ref, gwq_ref, gwk_ref,
    adj_ref, adjs_ref, col_ref,
):
    n, width = v_ref.shape
    heads, half = gwq_ref.shape[:2]
    rows = sum_ref.shape[0]
    me = lax.axis_index("seq")
    mine = lax.axis_index("tensor")
    last_code = (doc_ref[n - 1] + 1).astype(F32)
    edge = edge_ref[n - 1]

    def gathered(first, size):
        x = gath_ref[0, first : first + size].astype(F32)
        for d in range(1, seq):
            x = x + gath_ref[d, first : first + size].astype(F32)
        return x

    for h in range(heads):
        gwq_ref[h] = gathered(h * half, half)
    at = heads * half
    gwk_ref[...] = gathered(at + rows + 16, half)
    adj_ref[...] = jnp.zeros_like(adj_ref)
    adjs_ref[...] = jnp.zeros_like(adjs_ref)

    def later(s, carry):
        a = gath_ref[s, at : at + rows].astype(F32)
        t = gath_ref[s, at + rows : at + rows + 16].astype(F32)
        same = t[2:3] == last_code
        adj_ref[...] += jnp.where(same, a, 0.0)
        adjs_ref[...] += jnp.where(same, t[0:1] + t[1:2], 0.0)
        return carry

    lax.fori_loop(me + 1, jnp.minimum(me + REACH + 1, seq), later, 0)
    adj = adj_ref[...]
    a_hi = adj.astype(BF)
    a_lo = (adj - a_hi.astype(F32)).astype(BF)
    col_ref[...] = jnp.broadcast_to(adjs_ref[...], (width, width)).T
    col = col_ref[pl.ds(pl.multiple_of(mine * rows, rows), rows), 0:1]
    j = lax.broadcasted_iota(jnp.int32, (1, n), 1)
    more = mm(a_hi, v_ref[...], NT) + mm(a_lo, v_ref[...], NT) + col
    kfg_ref[...] = sum_ref[...] + jnp.where(j >= edge, more, 0.0) * back_scale


VM = pl.BlockSpec(memory_space=pltpu.VMEM)
SM = pl.BlockSpec(memory_space=pltpu.SMEM)
ANY = pl.BlockSpec(memory_space=pl.ANY)


def grant(mib):
    return pltpu.CompilerParams(vmem_limit_bytes=mib << 20)


def cost(flops, size):
    return pl.CostEstimate(flops=flops, bytes_accessed=size, transcendentals=0)


def shards(queries, keys, values, doc_ids, w_query, w_key):
    n, heads, width = queries.shape
    half = w_key.shape[1]
    seq = lax.axis_size("seq")
    tensor = lax.axis_size("tensor")
    scale = width ** (-0.5)
    everyone = range(seq)
    assert n // width <= 16 and n // width * 16 == width

    codes = (doc_ids.reshape(n // width, width) + 1).astype(BF)
    codes = jnp.pad(codes, ((0, 16 - n // width), (0, 0)))
    pack = jnp.concatenate([keys, values, codes], axis=0)

    def hop(x, distance):
        return lax.ppermute(x, "seq", [(i, i + distance) for i in everyone if i + distance < seq])

    two = hop(pack, 2)
    own = lax.ppermute(pack, "seq", [(i, i + 1) for i in everyone if i % 2 == 0])

    qs = queries.reshape(n, heads * width)
    starts = jnp.sum((doc_ids[None, :] < doc_ids[:, None]).astype(jnp.int32), axis=1)
    start_row = starts.reshape(1, n)
    wq_t = jnp.transpose(w_query, (0, 2, 1))
    wk_t = w_key.T
    sds = jax.ShapeDtypeStruct
    cols = heads * n
    rows = width // tensor
    near = REACH // 2
    chains = heads * min(n, CHAINS * TC // heads) // TC
    square = sds((width, width), F32)
    wide = sds((width, cols), F32)
    flat = sds((8, cols), F32)
    scan = [
        pltpu.VMEM((chains, 8, TC), F32),
        pltpu.VMEM((chains, width, TC), F32),
        pltpu.VMEM((chains, TK, TC), F32),
        pltpu.VMEM((chains, 8, TC), F32),
        pltpu.VMEM((TK, 128), F32),
    ]
    vt, acc, stat = pl.pallas_call(
        functools.partial(teacher_kernel, scale),
        out_shape=(sds((width, n), BF), wide, flat),
        in_specs=[VM] * 4,
        out_specs=[VM] * 3,
        compiler_params=grant(12),
        cost_estimate=cost(4 * n * n * width * heads, 4 << 20),
    )(qs, keys, values, start_row)
    four = hop(pack, 4)
    qf, kf, num, den = pl.pallas_call(
        student_kernel,
        out_shape=(wide, sds((width, n), F32), wide, flat),
        in_specs=[VM] * 6,
        out_specs=[VM] * 4,
        scratch_shapes=[pltpu.VMEM((n, width), BF)],
        compiler_params=grant(12),
        cost_estimate=cost(4 * n * n * width * heads, 4 << 20),
    )(qs, keys, vt, start_row, wq_t, wk_t)

    swap_two = lax.ppermute(two, "seq", [(i, i ^ 1) for i in everyone])
    acc, stat, near_kf, statet, csum = pl.pallas_call(
        functools.partial(window_kernel, scale),
        out_shape=(wide, flat, sds((width, near * n), F32), square, square),
        in_specs=[SM] + [VM] * 5 + [ANY] * 3,
        out_specs=[VM] * 5,
        scratch_shapes=[
            pltpu.VMEM((near * n, width), BF),
            pltpu.VMEM((near * n, width), BF),
            pltpu.VMEM((near, 16, width), BF),
            pltpu.VMEM((width, near * n), BF),
        ]
        + scan
        + [pltpu.SemaphoreType.DMA((near, 3))],
        compiler_params=grant(20),
        cost_estimate=cost(8 * n * n * width * heads, 4 << 20),
    )(doc_ids, qs, start_row, wk_t, acc, stat, own, two, swap_two)

    swap_four = lax.ppermute(four, "seq", [(i, i - 1) for i in everyone if i % 2 == 1])
    student, wq_part, *pieces = pl.pallas_call(
        functools.partial(main_kernel, scale, 2.0 / (n * seq), float(n * seq), tensor),
        out_shape=[sds((n, heads * width), BF), sds((heads * half, width), BF)]
        + [sds((rows + 16, n), BF)] * tensor,
        in_specs=[SM] + [VM] * 14 + [ANY] * 5,
        out_specs=[VM] * (2 + tensor),
        scratch_shapes=[
            pltpu.VMEM((near * n, width), BF),
            pltpu.VMEM((near * n, width), BF),
            pltpu.VMEM((near, 16, width), BF),
            pltpu.VMEM((2 * n, width), BF),
            pltpu.VMEM((2 * n, width), BF),
            pltpu.VMEM((2, 16, width), BF),
            pltpu.VMEM((width, 2 * n), F32),
            pltpu.VMEM((width, 2 * n), BF),
            pltpu.VMEM((heads, half, width), F32),
            pltpu.VMEM((half, width), F32),
            pltpu.VMEM((width, width + 16), F32),
            pltpu.VMEM((width, 128), F32),
            pltpu.VMEM((width, n), F32),
            pltpu.VMEM((n, width), F32),
            pltpu.VMEM((width, width), F32),
            pltpu.VMEM((width, width), F32),
            pltpu.VMEM((width, 128), F32),
            pltpu.VMEM((width, cols), F32),
            pltpu.VMEM((8, cols), F32),
        ]
        + scan
        + [pltpu.SemaphoreType.DMA((near, 3)), pltpu.SemaphoreType.DMA((2, 3))],
        compiler_params=grant(32),
        cost_estimate=cost(16 * n * n * width * heads, 8 << 20),
    )(
        doc_ids, qs, keys, values, start_row, wk_t,
        qf, kf, acc, num, stat, den, near_kf, statet, csum,
        two, four, own, swap_two, swap_four,
    )

    arrived = [pieces[0]]
    for k in range(1, tensor):
        arrived.append(
            lax.ppermute(pieces[k], "tensor", [(i, (i + k) % tensor) for i in range(tensor)])
        )
    packed = heads * half + rows + 16 + half
    part, out = pl.pallas_call(
        functools.partial(join_kernel, tensor),
        out_shape=(sds((rows, n), F32), sds((packed, width), BF)),
        in_specs=[SM] + [VM] * (tensor + 1),
        out_specs=[VM] * 2,
        compiler_params=grant(8),
        cost_estimate=cost(n * width, 1 << 20),
    )(doc_ids, wq_part, *arrived)
    gathered = lax.all_gather(out, "seq")
    key_grads, gwq, gwk = pl.pallas_call(
        functools.partial(last_kernel, seq, float(n * seq)),
        out_shape=(sds((rows, n), F32), sds((heads, half, width), F32), sds((half, width), F32)),
        in_specs=[SM, SM, VM, VM, VM],
        out_specs=[VM] * 3,
        scratch_shapes=[
            pltpu.VMEM((rows, width), F32),
            pltpu.VMEM((1, width), F32),
            pltpu.VMEM((width, width), F32),
        ],
        compiler_params=grant(12),
        cost_estimate=cost(4 * n * width * width, 2 << 20),
    )(doc_ids, starts, gathered, part, values)
    return student.reshape(n, heads, width), jnp.transpose(gwq, (0, 2, 1)), gwk.T, key_grads.T


def solution(mesh):
    placed = (
        P("seq", "tensor", None),
        P("seq", None),
        P("seq", None),
        P("seq"),
        P("tensor", None, None),
        P(),
    )

    return jax.shard_map(
        shards,
        mesh=mesh,
        in_specs=placed,
        out_specs=(P("seq", "tensor", None), P("tensor", None, None), P(), P("seq", "tensor")),
        check_vma=False,
    )
```
